32 devices in a mesh: dp: 8 (over z, x), expert: 4 (over y, core).
Axes of the slice: x: 2, y: 2, z: 4, core: 2. Of those that a mesh axis runs over, the one named last changes fastest.
Arguments:
- layer_input: bfloat16 [8, 2, 1024, 1536], P('dp', None, 'expert'), may hold values from -6 to 6
- cotangent: bfloat16 [8, 2, 1024, 1536], P('dp', None, 'expert'), may hold values from -6 to 6
- lengths: int32 [8, 2], P('dp'), may hold values from 512 to 1024, as said below
- routes: int32 [8, 2, 1024, 8], P('dp', None, 'expert'), may hold values from 0 to 39, all different within a row; in each aligned block of 256 rows (0 to 255, 256 to 511, ..., all dimensions but the last counted through in order) at most 64 rows name the same one
- capacity: int32 [40], replicated, may hold values from 48 to 64, as said below
- w_query: bfloat16 [1536, 1536], P(('dp', 'expert')), may hold values from -0.21875 to 0.21875
- key_weight: bfloat16 [1536, 512], P(('dp', 'expert')), may hold values from -0.21875 to 0.21875
- value_weight: bfloat16 [1536, 512], P(('dp', 'expert')), may hold values from -0.15625 to 0.15625
- w_output: bfloat16 [1536, 1536], P(('dp', 'expert')), may hold values from -0.625 to 0.625
- w_router: bfloat16 [1536, 40], P(('dp', 'expert')), may hold values from -0.078125 to 0.078125
- gain_attn: bfloat16 [1536], P(('dp', 'expert')), may hold values from 0.5 to 1.5
- gain_moe: bfloat16 [1536], P(('dp', 'expert')), may hold values from 0.5 to 1.5
- w_gate: bfloat16 [40, 1536, 512], P('expert', 'dp'), may hold values from -0.15625 to 0.15625
- w_up: bfloat16 [40, 1536, 512], P('expert', 'dp'), may hold values from -0.15625 to 0.15625
- w_down: bfloat16 [40, 512, 1536], P('expert', 'dp'), may hold values from -1 to 1
Outputs:
- layer_output: bfloat16 [8, 2, 1024, 1536], P('dp', None, 'expert')
- input_grad: float32 [8, 2, 1024, 1536], P('dp', None, 'expert')
- grad_query: float32 [1536, 1536], P(('dp', 'expert'))
- grad_key: float32 [1536, 512], P(('dp', 'expert'))
- grad_value: float32 [1536, 512], P(('dp', 'expert'))
- grad_output: float32 [1536, 1536], P(('dp', 'expert'))
- grad_router: float32 [1536, 40], P(('dp', 'expert'))
- grad_gain_attn: float32 [1536], P(('dp', 'expert'))
- grad_gain_moe: float32 [1536], P(('dp', 'expert'))
- grad_gate: float32 [40, 1536, 512], P('expert', 'dp')
- grad_up: float32 [40, 1536, 512], P('expert', 'dp')
- grad_down: float32 [40, 512, 1536], P('expert', 'dp')
The draws below stay inside these ranges and needn't reach their ends.
Inputs may be any that keep to these rules, and one draw needn't show every extreme that they name: `lengths`: in every draw some sequence has all 1024 positions valid. `capacity`: some expert accepts exactly 64 slots. `routes`: each position names 8 different experts. In each aligned block of 256 positions (the positions of one device in one micro-batch) no expert is named more than 64 times, a bound that some block reaches.
All inputs are finite; a program needn't handle non-finite values.
Results may differ from the reference program's by a relative error of at most 0.019.
Values may be sent and summed in bfloat16 or wider, within the bound.
No kernel may reach another device: no remote copies, remote signals or barrier semaphores. Data moves between devices by JAX's collectives and lax.ppermute only.
A program may use at most 216 MiB of HBM per device.

```python
import math
import jax
import jax.numpy as jnp
import numpy as np
from jax import lax

MODEL_DIMENSION = 1536
QUERY_HEAD_COUNT = 24
KEY_VALUE_HEADS = 8
HEAD_DIMENSION = 64
EXPERTS = 40
FFE = 512
TOPK = 8
MB = 2
SEQ = 1024
TOK_MB = 256
CAP = 64
N_DP = 8


def draw_lengths(key, part):
    key_draw = jax.random.fold_in(key, 11)
    key_pick = jax.random.fold_in(key, 12)
    drawn = jax.random.randint(key_draw, (N_DP * MB,), SEQ // 2, SEQ + 1)
    chosen_one = jax.random.randint(key_pick, (), 0, N_DP * MB)
    flat_lengths = jnp.where(jnp.arange(N_DP * MB) == chosen_one, SEQ, drawn)
    return flat_lengths.reshape(N_DP, MB).astype(jnp.int32)


def draw_capacity(key, part):
    key_draw = jax.random.fold_in(key, 21)
    key_pick = jax.random.fold_in(key, 22)
    drawn = jax.random.randint(key_draw, (EXPERTS,), 3 * CAP // 4, CAP + 1)
    chosen_one = jax.random.randint(key_pick, (), 0, EXPERTS)
    return jnp.where(jnp.arange(EXPERTS) == chosen_one, CAP, drawn).astype(jnp.int32)


def steps_of(rng, shape, cuts, smallest, high):
    def one(dim, blocks):
        draws = jax.random.uniform(jax.random.fold_in(jax.random.fold_in(rng, 6), dim), (blocks,), jnp.float32, smallest / len(cuts), high / len(cuts))
        return jnp.repeat(jnp.exp(draws), shape[dim] // blocks).reshape((-1,) + (1,) * (len(shape) - dim - 1))

    factor_of = one(*cuts[0])
    for cut in cuts[1:]:
        factor_of = factor_of * one(*cut)
    return factor_of


def assign_block(key, own, number, rows, count, top, most, skew):
    ranking = jax.random.permutation(key, count)
    crowded, common = load_shares(count, rows * top, most, skew, True), load_shares(count, rows * top, most, skew, False)
    places = jnp.arange(count)

    def named(sizes, turn):
        used = int((sizes > 0).sum())
        fixed = max(1, used // 4)
        moved = fixed + (places - fixed + turn * (used - fixed)) % max(1, count - fixed)
        return jnp.zeros((count,), jnp.int32).at[ranking[jnp.where(places < fixed, places, moved)]].set(jnp.asarray(sizes, jnp.int32))

    sizes = jnp.where(number % 4 == 0, named(crowded, number // 4), named(common, number - number // 4 - 1))
    mixed = jax.random.permutation(jax.random.fold_in(own, 3), count)
    donor, sink = mixed[0:count // 2 * 2:2], mixed[1:count // 2 * 2:2]
    room = jnp.minimum(sizes[donor] - 1, most - sizes[sink]) // 2
    room = jnp.where((donor == ranking[0]) | (sink == ranking[0]) | (sizes[sink] == 0), 0, jnp.maximum(room, 0))
    moved = jax.random.randint(jax.random.fold_in(own, 4), (count // 2,), 0, 1 << 20) % (room + 1)
    sizes = sizes.at[donor].add(-moved).at[sink].add(moved)
    items = jnp.searchsorted(jnp.cumsum(sizes), jnp.arange(rows * top), side="right").astype(jnp.int32)
    listing = items.reshape(top, rows).T
    listing = listing[jax.random.permutation(jax.random.fold_in(own, 1), rows)]
    turn = jax.random.randint(jax.random.fold_in(own, 2), (rows, 1), 0, top)
    return jnp.take_along_axis(listing, (jnp.arange(top)[None, :] + turn) % top, axis=1)


def load_shares(number_of, total, limit, slope, full):
    portions = [(1 << 20) // math.isqrt(rank ** slope) + 1 for rank in range(1, number_of + 1)]
    largest = limit if full else min(limit, max(-(-total // number_of), total * portions[0] // sum(portions)))
    least = 1 if total - largest >= number_of - 1 else 0
    holding, surplus = [largest] + [least] * (number_of - 1), total - largest - least * (number_of - 1)
    while surplus > 0:
        candidates = [i for i in range(1, number_of) if holding[i] < largest] or [i for i in range(1, number_of) if holding[i] < limit]
        whole, remaining = sum([portions[i] for i in candidates]), surplus
        for i in candidates:
            extra = min(limit - holding[i], max(1, remaining * portions[i] // whole), surplus)
            holding[i] = holding[i] + extra
            surplus = surplus - extra
    return np.array(holding)


def scatter_about(stream_key, dims, scale, bound, cuts=(), kind=jnp.bfloat16):
    factor_of = steps_of(stream_key, dims, cuts, -0.22, 0.18) if cuts else 1.0
    array = jax.random.normal(stream_key, dims, jnp.float32) * scale * factor_of
    return jnp.minimum(jnp.maximum(array, -bound), bound).astype(kind)


def setup_inputs(seed: int = 0) -> dict:
    arg_keys = jax.random.split(jax.random.key(seed), 16)
    layer_input = scatter_about(arg_keys[0], (N_DP, MB, SEQ, MODEL_DIMENSION), 1.0, 6.0, ((0, 8), (2, 4)))
    cotangent = scatter_about(arg_keys[1], (N_DP, MB, SEQ, MODEL_DIMENSION), 1.0, 6.0, ((0, 8), (2, 4)))
    lengths = draw_lengths(jax.random.fold_in(arg_keys[15], 71), 0)
    routes_keys = jax.random.split(jax.random.fold_in(arg_keys[3], 1), N_DP * MB * SEQ // TOK_MB)
    routes_turns = jax.random.permutation(jax.random.fold_in(arg_keys[3], 3), N_DP * MB * SEQ // TOK_MB)
    routes = jax.vmap(lambda own, number: assign_block(jax.random.fold_in(arg_keys[3], 2), own, number, TOK_MB, EXPERTS, TOPK, CAP, 1))(routes_keys, routes_turns).reshape((N_DP, MB, SEQ, TOPK))
    capacity = draw_capacity(jax.random.fold_in(arg_keys[15], 71), 0)
    w_query = scatter_about(arg_keys[5], (MODEL_DIMENSION, QUERY_HEAD_COUNT * HEAD_DIMENSION), (MODEL_DIMENSION // 2) ** -0.5, 0.21875, ((0, 32),))
    key_weight = scatter_about(arg_keys[6], (MODEL_DIMENSION, KEY_VALUE_HEADS * HEAD_DIMENSION), (MODEL_DIMENSION // 2) ** -0.5, 0.21875, ((0, 32),))
    value_weight = scatter_about(arg_keys[7], (MODEL_DIMENSION, KEY_VALUE_HEADS * HEAD_DIMENSION), MODEL_DIMENSION ** -0.5, 0.15625, ((0, 32),))
    w_output = scatter_about(arg_keys[8], (QUERY_HEAD_COUNT * HEAD_DIMENSION, MODEL_DIMENSION), (QUERY_HEAD_COUNT * HEAD_DIMENSION // 16) ** -0.5, 0.625, ((0, 32),))
    w_router = scatter_about(arg_keys[9], (MODEL_DIMENSION, EXPERTS), (4 * MODEL_DIMENSION) ** -0.5, 0.078125, ((0, 32),))
    gain_attn = jnp.clip(1.0 + 0.1 * jax.random.normal(arg_keys[10], (MODEL_DIMENSION,), jnp.float32), 0.5, 1.5).astype(jnp.bfloat16)
    gain_moe = jnp.clip(1.0 + 0.1 * jax.random.normal(arg_keys[11], (MODEL_DIMENSION,), jnp.float32), 0.5, 1.5).astype(jnp.bfloat16)
    w_gate = scatter_about(arg_keys[12], (EXPERTS, MODEL_DIMENSION, FFE), MODEL_DIMENSION ** -0.5, 0.15625, ((0, 4), (1, 8)))
    w_up = scatter_about(arg_keys[13], (EXPERTS, MODEL_DIMENSION, FFE), MODEL_DIMENSION ** -0.5, 0.15625, ((0, 4), (1, 8)))
    w_down = scatter_about(arg_keys[14], (EXPERTS, FFE, MODEL_DIMENSION), (FFE // 16) ** -0.5, 1.0, ((0, 4), (1, 8)))
    return {"layer_input": layer_input, "cotangent": cotangent, "lengths": lengths, "routes": routes, "capacity": capacity, "w_query": w_query, "key_weight": key_weight, "value_weight": value_weight, "w_output": w_output, "w_router": w_router, "gain_attn": gain_attn, "gain_moe": gain_moe, "w_gate": w_gate, "w_up": w_up, "w_down": w_down}


@jax.custom_vjp
def reduced_precision(v):
    return lax.optimization_barrier(v.astype(jnp.bfloat16)).astype(jnp.float32)

@jax.custom_vjp
def reduced_backward(v):
    return v

def low_keep(v):
    return (reduced_precision(v), None)

def low_pass(kept, grad):
    return (grad,)

def back_keep(v):
    return (v, None)

def back_low(kept, grad):
    return (reduced_precision(grad),)
reduced_precision.defvjp(low_keep, low_pass)
reduced_backward.defvjp(back_keep, back_low)
epsilon = 1e-06
rope_base = 10000.0
masked_score = -1e+30
highest = lax.Precision.HIGHEST

def matrix_multiply(left, right):
    return jnp.dot(left, right, precision=highest, preferred_element_type=jnp.float32)

def rope_tables(tally_count):
    places = jnp.arange(tally_count, dtype=jnp.int32).astype(jnp.float32)
    freqs = rope_base ** (-jnp.arange(0, HEAD_DIMENSION, 2, dtype=jnp.float32) / HEAD_DIMENSION)
    angles = places[:, None] * freqs[None, :]
    angles = jnp.concatenate([angles, angles], axis=1)
    return (jnp.cos(angles)[:, None, :], jnp.sin(angles)[:, None, :])

def rotate(value_matrix, cos_table, sin_table):
    half_size = value_matrix.shape[-1] // 2
    turned = jnp.concatenate([-value_matrix[..., half_size:], value_matrix[..., :half_size]], axis=-1)
    return value_matrix * cos_table + turned * sin_table

def forward_sequence(inputs, params, length, seq_routes, capacity):
    w_query, key_weight, value_weight, w_output, w_router, gain_attn, gain_moe, w_gate, w_up, w_down = params
    tally_count = inputs.shape[0]
    places = jnp.arange(tally_count, dtype=jnp.int32)
    query_group_count = QUERY_HEAD_COUNT // KEY_VALUE_HEADS
    score_scale = HEAD_DIMENSION ** (-0.5)
    scale_one = lax.rsqrt(lax.optimization_barrier(jnp.mean(inputs * inputs, axis=1, keepdims=True)) + epsilon)
    first_normalized = reduced_precision(inputs * scale_one * gain_attn)
    cos_table, sin_table = rope_tables(tally_count)
    query_rows = reduced_backward(matrix_multiply(first_normalized, w_query)).reshape(tally_count, QUERY_HEAD_COUNT, HEAD_DIMENSION)
    query_rows = reduced_precision(rotate(query_rows, cos_table, sin_table))
    key_rows = reduced_backward(matrix_multiply(first_normalized, key_weight)).reshape(tally_count, KEY_VALUE_HEADS, HEAD_DIMENSION)
    key_rows = reduced_precision(rotate(key_rows, cos_table, sin_table))
    value_matrix = reduced_backward(reduced_precision(matrix_multiply(first_normalized, value_weight))).reshape(tally_count, KEY_VALUE_HEADS, HEAD_DIMENSION)
    allowed = (places[None, :] <= places[:, None]) & (places[None, :] < length)
    split_query_heads = query_rows.reshape(tally_count, KEY_VALUE_HEADS, query_group_count, HEAD_DIMENSION).transpose(1, 2, 0, 3)
    key_heads = key_rows.transpose(1, 0, 2)
    value_heads = value_matrix.transpose(1, 0, 2)

    def head_block(pieces):
        query_one, key_one, value_one = pieces
        scores = jnp.einsum('gqd,kd->gqk', query_one, key_one, precision=highest) * score_scale
        scores = reduced_backward(scores)
        scores = jnp.where(allowed[None], scores, masked_score)
        probs = jax.nn.softmax(scores, axis=-1)
        return jnp.einsum('gqk,kd->gqd', reduced_precision(probs), value_one, precision=highest)
    blended_output = lax.map(jax.checkpoint(head_block), (split_query_heads, key_heads, value_heads))
    attended = reduced_backward(reduced_precision(blended_output.transpose(2, 0, 1, 3).reshape(tally_count, QUERY_HEAD_COUNT * HEAD_DIMENSION)))
    branch = reduced_backward(matrix_multiply(attended, w_output))
    middle = inputs + branch
    scale_two = lax.rsqrt(lax.optimization_barrier(jnp.mean(middle * middle, axis=1, keepdims=True)) + epsilon)
    normed_two = reduced_precision(middle * scale_two * gain_moe)
    logits = reduced_backward(matrix_multiply(normed_two, w_router))
    chosen = jnp.take_along_axis(logits, seq_routes, axis=1)
    gate_weights = jax.nn.softmax(chosen, axis=1)
    valid = places < length
    blocks = tally_count // TOK_MB
    block_routes = seq_routes.reshape(blocks, TOK_MB * TOPK)
    pair_valid = jnp.repeat(valid, TOPK).reshape(blocks, TOK_MB * TOPK)
    expert_ids = jnp.arange(EXPERTS, dtype=jnp.int32)
    matches = block_routes[:, :, None] == expert_ids[None, None, :]
    onehot = (matches & pair_valid[:, :, None]).astype(jnp.int32)
    running = jnp.cumsum(onehot, axis=1)
    slot_ranks = lax.optimization_barrier(jnp.sum(running * onehot, axis=2)) - 1
    limits = lax.optimization_barrier(jnp.sum(matches.astype(jnp.int32) * capacity[None, None, :], axis=2))
    kept = pair_valid & (slot_ranks < limits)
    slots = jnp.where(kept, block_routes * CAP + slot_ranks, EXPERTS * CAP).astype(jnp.int32)
    pair_rows = jnp.repeat(normed_two.reshape(blocks, TOK_MB, MODEL_DIMENSION), TOPK, axis=1)

    def fill_slots(slot_row, row_values):
        empty = jnp.zeros((EXPERTS * CAP + 1, MODEL_DIMENSION), jnp.float32)
        return empty.at[slot_row].add(row_values)[:EXPERTS * CAP]
    buffers = jax.vmap(fill_slots)(slots, pair_rows).reshape(blocks, EXPERTS, CAP, MODEL_DIMENSION)
    buffers = reduced_backward(buffers)
    gate_pre = reduced_backward(jnp.einsum('becd,edf->becf', buffers, w_gate, precision=highest))
    up_pre = reduced_backward(jnp.einsum('becd,edf->becf', buffers, w_up, precision=highest))
    hidden = reduced_precision(jax.nn.silu(gate_pre) * up_pre)
    expert_out = reduced_backward(reduced_precision(jnp.einsum('becf,efd->becd', hidden, w_down, precision=highest)))
    flat_out = expert_out.reshape(blocks, EXPERTS * CAP, MODEL_DIMENSION)
    padded = jnp.concatenate([flat_out, jnp.zeros((blocks, 1, MODEL_DIMENSION), jnp.float32)], axis=1)
    picked = jax.vmap(lambda source, positions: source[positions])(padded, slots)
    picked = picked.reshape(tally_count, TOPK, MODEL_DIMENSION)
    mixture = lax.optimization_barrier(jnp.sum(gate_weights[:, :, None] * picked, axis=1))
    return middle + mixture

def reference(layer_input, cotangent, lengths, routes, capacity, w_query, key_weight, value_weight, w_output, w_router, gain_attn, gain_moe, w_gate, w_up, w_down):
    params = tuple((weight.astype(jnp.float32) for weight in (w_query, key_weight, value_weight, w_output, w_router, gain_attn, gain_moe, w_gate, w_up, w_down)))
    totals = tuple((jnp.zeros_like(weight) for weight in params))
    inputs = layer_input.astype(jnp.float32).reshape(N_DP * MB, SEQ, MODEL_DIMENSION)
    upstream = cotangent.astype(jnp.float32).reshape(N_DP * MB, SEQ, MODEL_DIMENSION)
    all_lengths = lengths.reshape(N_DP * MB).astype(jnp.int32)
    all_routes = routes.reshape(N_DP * MB, SEQ, TOPK).astype(jnp.int32)

    def sequence_step(running_sums, item):
        seq_inputs, seq_upstream, length, seq_routes = item
        result, pullback = jax.vjp(lambda value_matrix, weights: forward_sequence(value_matrix, weights, length, seq_routes, capacity), seq_inputs, params)
        valid = (jnp.arange(SEQ, dtype=jnp.int32) < length).astype(jnp.float32)
        grad_inputs, grad_params = pullback(seq_upstream * valid[:, None])
        running_sums = tuple((total + piece for total, piece in zip(running_sums, grad_params)))
        return (running_sums, (result, grad_inputs))
    totals, (results, grad_inputs) = lax.scan(sequence_step, totals, (inputs, upstream, all_lengths, all_routes))
    layer_output = results.reshape(N_DP, MB, SEQ, MODEL_DIMENSION).astype(jnp.bfloat16)
    input_grad = grad_inputs.reshape(N_DP, MB, SEQ, MODEL_DIMENSION)
    return (layer_output, input_grad, totals[0], totals[1], totals[2], totals[3], totals[4], totals[5], totals[6], totals[7], totals[8], totals[9])
```

```python
import functools

import jax
import jax.numpy as jnp
from jax import lax
from jax.experimental import pallas as pl
from jax.experimental.pallas import tpu as pltpu
from jax.sharding import PartitionSpec as P

QUERY_HEAD_COUNT = 24
KEY_VALUE_HEADS = 8
HEAD_DIMENSION = 64
EXPERTS = 40
TOPK = 8

epsilon = 1e-06
rope_base = 10000.0
masked_score = -1e30

F32 = jnp.float32
BF16 = jnp.bfloat16
AXES = ("dp", "expert")
HALF_HEAD = HEAD_DIMENSION // 2
GROUP = QUERY_HEAD_COUNT // KEY_VALUE_HEADS
PAIRS = KEY_VALUE_HEADS // 2
PAIR_LANES = 2 * HEAD_DIMENSION
QUERY_LANES = GROUP * PAIR_LANES
LANES = 128
BLOCKS_PER_STEP = 4


def dot(left, right):
    return jnp.dot(left, right, preferred_element_type=F32)


def dot_rows(left, right):
    return lax.dot_general(left, right, (((0,), (0,)), ((), ())), preferred_element_type=F32)


def dot_cols(left, right):
    return lax.dot_general(left, right, (((1,), (1,)), ((), ())), preferred_element_type=F32)


def add_rounded(left, right):
    return (left.astype(F32) + right.astype(F32)).astype(left.dtype)


def params(limit_mib, steps=1):
    return pltpu.CompilerParams(
        dimension_semantics=("arbitrary",) * steps, vmem_limit_bytes=limit_mib << 20
    )


def lasting(micros):
    return pl.CostEstimate(flops=int(micros * 1.1e9), bytes_accessed=0, transcendentals=0)


def whole_spec():
    return pl.BlockSpec(memory_space=pltpu.VMEM)


def swap(array, place):
    axis, bit = place
    dp_count, owner_count = lax.axis_size("dp"), lax.axis_size("expert")
    flip = (1 << bit) * (owner_count if axis == "dp" else 1)
    return lax.ppermute(array, AXES, [(i, i ^ flip) for i in range(dp_count * owner_count)])


def gather_pieces(array, places):
    pieces = [array]
    for place in places:
        pieces = pieces + [swap(piece, place) for piece in pieces]
    return pieces


def after(value, *others):
    return lax.optimization_barrier((value, *others))


def gather_rows(array, places):
    pieces = jnp.stack(gather_pieces(array, places[:-1]))
    return pieces, swap(pieces, places[-1])


def sum_home(low, high, places):
    for place in reversed(places):
        total = high.shape[0]
        received = swap(high, place)
        if total == 1:
            return add_rounded(low, received)
        low, high = (
            add_rounded(low[: total // 2], received[: total // 2]),
            add_rounded(low[total // 2 :], received[total // 2 :]),
        )
    return low


class Trip:
    def __init__(self, stages, places, split):
        self.stages, self.places, self.split = stages[:-2], places, split
        self.rest = stages[-2]
        self.stage = len(places) - 1
        self.waiting = [swap(stages[-1], places[-1])]
        self.first = True
        self.mine = self.other = None

    def gather(self, received, stages):
        start = 0
        for stage in stages:
            size = self.stages[stage].shape[0]
            self.stages[stage] = add_rounded(
                self.stages[stage], received[start : start + size]
            )
            start += size

    def step(self, received):
        if self.first:
            self.first = False
            self.gather(received, [self.stage])
            self.waiting = [
                swap(self.rest, self.places[-1]),
                swap(self.stages[self.stage], self.places[self.stage - 1]),
            ]
            self.rest = None
        elif self.stage == len(self.places) - 1:
            self.gather(received, range(self.stage))
            self.stage -= 1
        elif self.stage > 0:
            self.gather(received, range(self.stage + 1))
            self.waiting.append(swap(self.stages[self.stage], self.places[self.stage - 1]))
            self.stage -= 1
        else:
            mine, received = self.stages[0][0].astype(F32), received[0].astype(F32)
            self.mine = mine if self.split == 2 else mine + received
            self.other = received


def arrive(value, *trips):
    value, *received = after(value, *[trip.waiting[0] for trip in trips])
    for trip, array in zip(trips, received):
        trip.waiting = trip.waiting[1:]
        trip.step(array)
    return value


def masks_of(places):
    found = []
    for piece in range(1 << len(places)):
        mask = {"dp": 0, "expert": 0}
        for stage, (axis, bit) in enumerate(places):
            if piece >> stage & 1:
                mask[axis] |= 1 << bit
        found.append(mask)
    return found


def half_swap(rows):
    lane = lax.broadcasted_iota(jnp.int32, rows.shape, 1)
    return jnp.where(
        lane % HEAD_DIMENSION < HALF_HEAD,
        pltpu.roll(rows, rows.shape[1] - HALF_HEAD, 1),
        pltpu.roll(rows, HALF_HEAD, 1),
    )


def project_kernel(x_ref, gain_ref, w_ref, cos_ref, sin_ref, h_ref, q_ref, kv_ref):
    x = x_ref[0].astype(F32)
    scale = lax.rsqrt(jnp.mean(x * x, axis=1, keepdims=True) + epsilon)
    h_ref[0] = (x * scale * gain_ref[...]).astype(BF16)
    cos, sin = cos_ref[...], sin_ref[...]
    width = q_ref.shape[2]
    key_width = kv_ref.shape[2] // 2

    def turn_into(out_ref, start, rows):
        for tile in range(0, rows.shape[1], LANES):
            part = rows[:, tile : tile + LANES]
            out_ref[0, :, start + tile : start + tile + LANES] = (
                part * cos + half_swap(part) * sin
            ).astype(BF16)

    for start in range(0, width, key_width):
        turn_into(q_ref, start, dot(h_ref[0], w_ref[:, start : start + key_width]))
    turn_into(kv_ref, 0, dot(h_ref[0], w_ref[:, width : width + key_width]))
    value = dot(h_ref[0], w_ref[:, width + key_width : width + 2 * key_width])
    kv_ref[0, :, key_width:] = value.astype(BF16)


def project(x, gain, dense, cos, sin):
    count, rows, width = x.shape
    key_width = KEY_VALUE_HEADS * HEAD_DIMENSION
    row_spec = pl.BlockSpec((1, rows, width), lambda i: (i, 0, 0))
    return pl.pallas_call(
        project_kernel,
        grid=(count,),
        in_specs=[
            row_spec,
            pl.BlockSpec((1, width), lambda i: (0, 0)),
            pl.BlockSpec(dense.shape, lambda i: (0, 0)),
            pl.BlockSpec((rows, LANES), lambda i: (0, 0)),
            pl.BlockSpec((rows, LANES), lambda i: (0, 0)),
        ],
        out_specs=[
            row_spec,
            row_spec,
            pl.BlockSpec((1, rows, 2 * key_width), lambda i: (i, 0, 0)),
        ],
        out_shape=[
            jax.ShapeDtypeStruct(x.shape, BF16),
            jax.ShapeDtypeStruct(x.shape, BF16),
            jax.ShapeDtypeStruct((count, rows, 2 * key_width), BF16),
        ],
        cost_estimate=lasting(8),
        compiler_params=params(48),
    )(x, gain, dense, cos, sin)


def middle_kernel(x_ref, o_ref, wo_ref, wr_ref, gain_ref, code_ref, y_ref, h_ref, g_ref):
    middle = x_ref[...].astype(F32) + dot(o_ref[...], wo_ref[...])
    y_ref[...] = middle
    scale = lax.rsqrt(jnp.mean(middle * middle, axis=1, keepdims=True) + epsilon)
    normed = (middle * scale * gain_ref[...]).astype(BF16)
    h_ref[...] = normed
    logits = dot(normed, wr_ref[...])
    chosen = code_ref[...] > -1.5
    peak = jnp.max(jnp.where(chosen, logits, masked_score), axis=1, keepdims=True)
    raised = jnp.where(chosen, jnp.exp(jnp.where(chosen, logits, peak) - peak), 0.0)
    g_ref[...] = raised / jnp.sum(raised, axis=1, keepdims=True)


def middle_rows(x, attended, dense, gain, code):
    rows, width = x.shape
    full = pl.BlockSpec((rows, width), lambda i: (0, 0))
    return pl.pallas_call(
        middle_kernel,
        grid=(1,),
        in_specs=[
            full,
            full,
            pl.BlockSpec((width, width), lambda i: (0, 0)),
            pl.BlockSpec((width, LANES), lambda i: (0, width // LANES)),
            pl.BlockSpec((1, width), lambda i: (0, 0)),
            pl.BlockSpec((rows, LANES), lambda i: (0, 0)),
        ],
        out_specs=[full, full, pl.BlockSpec((rows, LANES), lambda i: (0, 0))],
        out_shape=[
            jax.ShapeDtypeStruct((rows, width), F32),
            jax.ShapeDtypeStruct((rows, width), BF16),
            jax.ShapeDtypeStruct((rows, LANES), F32),
        ],
        cost_estimate=lasting(4.5),
        compiler_params=params(48),
    )(x, attended, dense, dense, gain, code)


def middle_back_kernel(
    acc_ref, y_ref, dy_ref, g_ref, dg_ref, gain_ref, wr_ref, wo_ref,
    dz_ref, dy1_ref, dr_ref, do_ref, dgain_ref,
):
    gates, gate_grads = g_ref[...], dg_ref[...].astype(F32)
    mean = jnp.sum(gates * gate_grads, axis=1, keepdims=True)
    dz = (gates * (gate_grads - mean)).astype(BF16)
    dz_ref[...] = dz
    dh = acc_ref[...].astype(F32) + dot_cols(dz, wr_ref[...])
    middle = y_ref[...]
    scale = lax.rsqrt(jnp.mean(middle * middle, axis=1, keepdims=True) + epsilon)
    dgain_ref[...] = jnp.sum(dh * middle * scale, axis=0, keepdims=True)
    scaled = dh * gain_ref[...]
    along = jnp.mean(scaled * middle, axis=1, keepdims=True)
    dy1 = dy_ref[...].astype(F32) + scale * scaled - middle * (scale * scale * scale * along)
    dy1_ref[...] = dy1
    rounded = dy1.astype(BF16)
    dr_ref[...] = rounded
    do_ref[...] = dot_cols(rounded, wo_ref[...]).astype(BF16)


def middle_back(acc, middle, dy, gates, gain, dense):
    rows, width = middle.shape
    full = pl.BlockSpec((rows, width), lambda i: (0, 0))
    lane = pl.BlockSpec((rows, LANES), lambda i: (0, 0))
    line = pl.BlockSpec((1, width), lambda i: (0, 0))
    return pl.pallas_call(
        middle_back_kernel,
        grid=(1,),
        in_specs=[
            full, full, full, lane,
            pl.BlockSpec((rows, LANES), lambda i: (0, width // LANES)),
            line,
            pl.BlockSpec((width, LANES), lambda i: (0, width // LANES)),
            pl.BlockSpec((width, width), lambda i: (0, 0)),
        ],
        out_specs=[lane, full, full, full, line],
        out_shape=[
            jax.ShapeDtypeStruct((rows, LANES), BF16),
            jax.ShapeDtypeStruct((rows, width), F32),
            jax.ShapeDtypeStruct((rows, width), BF16),
            jax.ShapeDtypeStruct((rows, width), BF16),
            jax.ShapeDtypeStruct((1, width), F32),
        ],
        cost_estimate=lasting(6.6),
        compiler_params=params(56),
    )(acc, middle, dy, gates, acc, gain, dense, dense)


def project_back_kernel(
    dq_ref, pairs_ref, x_ref, dy1_ref, gain_ref, w_ref, cos_ref, sin_ref,
    dx_ref, dkv_ref, dgain_ref,
):
    cos, sin = cos_ref[...], sin_ref[...]
    width = x_ref.shape[1]
    key_width = dkv_ref.shape[1] // 2
    for pair in range(PAIRS):
        lanes = slice(pair * LANES, (pair + 1) * LANES)
        start = 2 * pair * LANES
        part = pairs_ref[:, start : start + LANES].astype(F32)
        dkv_ref[:, lanes] = (part * cos - half_swap(part) * sin).astype(BF16)
        lanes = slice(key_width + pair * LANES, key_width + (pair + 1) * LANES)
        dkv_ref[:, lanes] = pairs_ref[:, start + LANES : start + 2 * LANES]
    dh = dot_cols(dq_ref[...], w_ref[:, :width])
    dh = dh + dot_cols(dkv_ref[...], w_ref[:, width : width + 2 * key_width])
    x = x_ref[...].astype(F32)
    scale = lax.rsqrt(jnp.mean(x * x, axis=1, keepdims=True) + epsilon)
    dgain_ref[...] = jnp.sum(dh * x * scale, axis=0, keepdims=True)
    scaled = dh * gain_ref[...]
    along = jnp.mean(scaled * x, axis=1, keepdims=True)
    dx_ref[...] = dy1_ref[...] + scale * scaled - x * (scale * scale * scale * along)


def project_back(dq, pairs, x, dy1, gain, dense, cos, sin):
    rows, width = x.shape
    key_width = pairs.shape[1] // 2
    full = pl.BlockSpec((rows, width), lambda i: (0, 0))
    lane = pl.BlockSpec((rows, LANES), lambda i: (0, 0))
    line = pl.BlockSpec((1, width), lambda i: (0, 0))
    both = pl.BlockSpec((rows, 2 * key_width), lambda i: (0, 0))
    return pl.pallas_call(
        project_back_kernel,
        grid=(1,),
        in_specs=[
            full, both, full, full, line, pl.BlockSpec(dense.shape, lambda i: (0, 0)), lane, lane,
        ],
        out_specs=[full, both, line],
        out_shape=[
            jax.ShapeDtypeStruct((rows, width), F32),
            jax.ShapeDtypeStruct((rows, 2 * key_width), BF16),
            jax.ShapeDtypeStruct((1, width), F32),
        ],
        cost_estimate=lasting(8.2),
        compiler_params=params(56),
    )(dq, pairs, x, dy1, gain, dense, cos, sin)


def weight_grad_kernel(count, *refs):
    left_refs, right_refs, out_ref = refs[:count], refs[count : 2 * count], refs[-1]
    rows, columns = out_ref.shape
    if len(refs) > 2 * count + 1:
        gain = jnp.broadcast_to(refs[2 * count][...], (8, rows)).T
    lane = lax.broadcasted_iota(jnp.int32, (rows, LANES), 1)
    start = 0
    for left_ref, right_ref in zip(left_refs, right_refs):
        left = left_ref[...].T
        width = right_ref.shape[1]
        step = min(width, 4 * LANES)
        for tile in range(0, width, step):
            part = dot(left, right_ref[:, tile : tile + step])
            if start + tile + step == columns and len(refs) > 2 * count + 1:
                edge = part[:, step - LANES :]
                edge = jnp.where(lane == EXPERTS, gain[:, 0:1], edge)
                out_ref[:, columns - LANES :] = edge.astype(BF16)
                part = part[:, : step - LANES]
            if part.shape[1]:
                out_ref[:, start + tile : start + tile + part.shape[1]] = part.astype(BF16)
        start += width
    if start < columns:
        out_ref[:, start:] = jnp.where(lane == EXPERTS, gain[:, 0:1], 0.0).astype(BF16)


def weight_grads(lefts, rights, gain, columns):
    rows = lefts[0].shape[1]
    operands = [*lefts, *rights] + ([] if gain is None else [gain])
    return pl.pallas_call(
        functools.partial(weight_grad_kernel, len(lefts)),
        in_specs=[whole_spec() for _ in operands],
        out_specs=whole_spec(),
        out_shape=jax.ShapeDtypeStruct((rows, columns), BF16),
        cost_estimate=lasting(9),
        compiler_params=pltpu.CompilerParams(vmem_limit_bytes=56 << 20),
    )(*operands)


def fill_bias(places_ref, bias_ref, rows):
    query = places_ref[0] + lax.broadcasted_iota(jnp.int32, (rows, rows), 1)
    inside = lax.broadcasted_iota(jnp.int32, (rows, rows), 0)
    for block in range(bias_ref.shape[0] // rows):
        key = places_ref[2 + block] + inside
        allowed = (key <= query) & (key < places_ref[1])
        bias_ref[block * rows : (block + 1) * rows, :] = jnp.where(allowed, 0.0, masked_score)


def attend_kernel(places_ref, q_ref, k_ref, v_ref, o_ref, lse_ref, bias_ref):
    rows = q_ref.shape[0]

    @pl.when(pl.program_id(0) == 0)
    def _():
        fill_bias(places_ref, bias_ref, rows)

    outs = []
    for side in range(2):
        lanes = slice(side * HEAD_DIMENSION, (side + 1) * HEAD_DIMENSION)
        key = k_ref[:, lanes]
        value_t = v_ref[:, lanes].T
        for member in range(GROUP):
            head = side * GROUP + member
            query = q_ref[:, head * HEAD_DIMENSION : (head + 1) * HEAD_DIMENSION]
            scores = dot_cols(key, query * HEAD_DIMENSION**-0.5) + bias_ref[...]
            peak = jnp.max(scores, axis=0, keepdims=True)
            raised = jnp.exp(scores - peak)
            total = jnp.sum(raised, axis=0, keepdims=True)
            outs.append(dot(value_t, raised.astype(BF16)) / total)
            lse_ref[0, head : head + 1, :] = peak + jnp.log(total)
    o_ref[...] = jnp.concatenate(outs, axis=0).T.astype(BF16)


def attend(places, q, kv):
    rows, width = q.shape
    keys = kv.shape[0]
    return pl.pallas_call(
        attend_kernel,
        grid_spec=pltpu.PrefetchScalarGridSpec(
            num_scalar_prefetch=1,
            grid=(PAIRS,),
            in_specs=[
                pl.BlockSpec((rows, QUERY_LANES), lambda i, s: (0, i)),
                pl.BlockSpec((keys, PAIR_LANES), lambda i, s: (0, i)),
                pl.BlockSpec((keys, PAIR_LANES), lambda i, s: (0, PAIRS + i)),
            ],
            out_specs=[
                pl.BlockSpec((rows, QUERY_LANES), lambda i, s: (0, i)),
                pl.BlockSpec((1, 8, rows), lambda i, s: (i, 0, 0)),
            ],
            scratch_shapes=[pltpu.VMEM((keys, rows), F32)],
        ),
        out_shape=[
            jax.ShapeDtypeStruct((rows, width), BF16),
            jax.ShapeDtypeStruct((PAIRS, 8, rows), F32),
        ],
        cost_estimate=lasting(19),
        compiler_params=params(48),
    )(places, q, kv, kv)


def attend_back_kernel(
    places_ref, q_ref, k_ref, v_ref, do_ref, o_ref, lse_ref, cos_ref, sin_ref,
    dq_ref, dkv_ref, bias_ref,
):
    rows = q_ref.shape[0]

    @pl.when(pl.program_id(0) == 0)
    def _():
        fill_bias(places_ref, bias_ref, rows)

    score_scale = HEAD_DIMENSION**-0.5
    cos, sin = cos_ref[...], sin_ref[...]
    ones = jnp.ones((8, HEAD_DIMENSION), F32)
    query_grads = []
    for side in range(2):
        lanes = slice(side * HEAD_DIMENSION, (side + 1) * HEAD_DIMENSION)
        key, value = k_ref[:, lanes], v_ref[:, lanes]
        key_t = key.T
        key_grad = None
        value_grad = None
        for member in range(GROUP):
            head = side * GROUP + member
            columns = slice(head * HEAD_DIMENSION, (head + 1) * HEAD_DIMENSION)
            query = q_ref[:, columns] * score_scale
            grad = do_ref[:, columns]
            overlap = grad.astype(F32) * o_ref[:, columns].astype(F32)
            along = lax.dot_general(
                ones, overlap, (((1,), (1,)), ((), ())),
                precision=lax.Precision.HIGHEST, preferred_element_type=F32,
            )[0:1]
            scores = dot_cols(key, query) + bias_ref[...]
            probs = jnp.exp(scores - lse_ref[0, head : head + 1, :])
            score_grad = (probs * (dot_cols(value, grad) - along)).astype(BF16)
            value_part = dot(probs.astype(BF16), grad)
            key_part = dot(score_grad, query)
            value_grad = value_part if value_grad is None else value_grad + value_part
            key_grad = key_part if key_grad is None else key_grad + key_part
            turned = dot(key_t, score_grad) * score_scale
            upper, lower = turned[:HALF_HEAD], turned[HALF_HEAD:]
            query_grads += [upper * cos + lower * sin, lower * cos - upper * sin]
        dkv_ref[:, lanes] = key_grad.astype(BF16)
        shifted = slice(LANES + side * HEAD_DIMENSION, LANES + (side + 1) * HEAD_DIMENSION)
        dkv_ref[:, shifted] = value_grad.astype(BF16)
    dq_ref[...] = jnp.concatenate(query_grads, axis=0).T.astype(BF16)


def attend_back(places, q, kv, grad, attended, lse, cos_t, sin_t):
    rows, width = q.shape
    keys = kv.shape[0]
    key_width = kv.shape[1] // 2
    wide = pl.BlockSpec((rows, QUERY_LANES), lambda i, s: (0, i))
    tall = pl.BlockSpec((keys, PAIR_LANES), lambda i, s: (0, i))
    table = pl.BlockSpec((HALF_HEAD, rows), lambda i, s: (0, 0))
    return pl.pallas_call(
        attend_back_kernel,
        grid_spec=pltpu.PrefetchScalarGridSpec(
            num_scalar_prefetch=1,
            grid=(PAIRS,),
            in_specs=[
                wide,
                tall,
                pl.BlockSpec((keys, PAIR_LANES), lambda i, s: (0, PAIRS + i)),
                wide,
                wide,
                pl.BlockSpec((1, 8, rows), lambda i, s: (i, 0, 0)),
                table,
                table,
            ],
            out_specs=[wide, pl.BlockSpec((keys, 2 * PAIR_LANES), lambda i, s: (0, i))],
            scratch_shapes=[pltpu.VMEM((keys, rows), F32)],
        ),
        out_shape=[
            jax.ShapeDtypeStruct((rows, width), BF16),
            jax.ShapeDtypeStruct((keys, 2 * key_width), BF16),
        ],
        cost_estimate=lasting(23.5),
        compiler_params=params(56),
    )(places, q, kv, kv, grad, attended, lse, cos_t, sin_t)


def expert_kernel(masks, stage_sizes, expert, aliased, me_ref, *refs):
    count = len(masks)
    pieces, refs = refs[:count], refs[count:]
    h_ref, dy_ref, rank_ref, gate_ref = refs[:4]
    refs = refs[4 + (2 if aliased else 0) :]
    eg_ref, db_ref = refs[:2]
    out_refs, refs = refs[2 : 2 + len(stage_sizes)], refs[2 + len(stage_sizes) :]
    w_in, w_down, g_in, g_down, rows_all, de_all, hidden_all, dau_all, in_sem, out_sem = refs
    step = pl.program_id(0)
    blocks, tokens, width = h_ref.shape
    slots = eg_ref.shape[2]
    chunk = blocks * slots
    inner = w_down.shape[0]
    deep = width // count
    shallow = inner // count
    wide = width // inner
    me = me_ref[0]

    def windows(piece_ref, shard, into, down):
        top = pl.ds(pl.multiple_of(shard * deep, 16), deep)
        low = pl.ds(pl.multiple_of(shard * shallow, 16), shallow)
        pairs = [
            (piece_ref.at[pl.ds(0, deep)], into.at[top, pl.ds(0, inner)]),
            (piece_ref.at[pl.ds(deep, deep)], into.at[top, pl.ds(inner, inner)]),
        ]
        for part in range(wide):
            pairs.append(
                (
                    piece_ref.at[pl.ds(2 * deep + part * shallow, shallow)],
                    down.at[low, pl.ds(part * inner, inner)],
                )
            )
        return pairs

    def loads():
        made = []
        for piece, mask in enumerate(masks):
            for source, target in windows(pieces[piece].at[expert], me ^ mask, w_in, w_down):
                made.append(pltpu.make_async_copy(source, target, in_sem.at[len(made)]))
        return made

    def stores():
        made = []
        for piece, mask in enumerate(masks):
            start = 0
            for out_ref, size in zip(out_refs, stage_sizes):
                if start <= piece < start + size:
                    target = out_ref.at[piece - start]
                start += size
            for there, here in windows(target, me ^ mask, g_in, g_down):
                made.append(pltpu.make_async_copy(here, there, out_sem.at[len(made)]))
        return made

    @pl.when(step == 0)
    def _():
        for copy in loads():
            copy.start()

    slot = lax.broadcasted_iota(jnp.int32, (slots, tokens), 0)
    grads = []
    weights = []
    for block in range(blocks):
        start = pl.multiple_of((step * blocks + block) * tokens, LANES)
        hit = slot == rank_ref[expert : expert + 1, pl.ds(start, tokens)]
        select = jnp.where(hit, 1.0, 0.0).astype(BF16)
        place = pl.ds(pl.multiple_of(step * chunk + block * slots, 16), slots)
        rows_all[place, :] = dot(select, h_ref[block]).astype(BF16)
        grads.append(dot(select, dy_ref[block]))
        gate = gate_ref[expert : expert + 1, pl.ds(start, tokens)]
        weights.append(jnp.sum(jnp.where(hit, gate, 0.0), axis=1, keepdims=True))

    @pl.when(step == 0)
    def _():
        for copy in loads():
            copy.wait()

    here = pl.ds(pl.multiple_of(step * chunk, 16), chunk)
    grad_rows = jnp.concatenate(grads, axis=0)
    weight = jnp.concatenate(weights, axis=0)
    pre = dot(rows_all[here, :], w_in[...])
    gate_pre, up_pre = pre[:, :inner], pre[:, inner:]
    sigmoid = 1.0 / (1.0 + jnp.exp(-gate_pre))
    silu = gate_pre * sigmoid
    hidden = (silu * up_pre).astype(BF16)
    hidden_all[here, :] = hidden
    out = dot(hidden, w_down[...]).astype(BF16).astype(F32)
    row_grad = jnp.sum(grad_rows * out, axis=1, keepdims=True)
    out = (weight * out).astype(BF16)
    lane = lax.broadcasted_iota(jnp.int32, (slots, LANES), 1)
    for block in range(blocks):
        part = slice(block * slots, (block + 1) * slots)
        eg_ref[block, 0] = out[part]
        db_ref[block, 0, :, width:] = jnp.where(lane == me_ref[1] + expert, row_grad[part], 0.0).astype(
            BF16
        )
    de = (weight * grad_rows).astype(BF16)
    de_all[here, :] = de
    grad_hidden = dot_cols(de, w_down[...])
    grad_up = (grad_hidden * silu).astype(BF16)
    grad_gate = (
        grad_hidden * up_pre * sigmoid * (1.0 + gate_pre * (1.0 - sigmoid))
    ).astype(BF16)
    dau_all[here, :inner] = grad_gate
    dau_all[here, inner:] = grad_up
    back = dot_cols(dau_all[here, :], w_in[...]).astype(BF16)
    for block in range(blocks):
        db_ref[block, 0, :, :width] = back[block * slots : (block + 1) * slots]

    @pl.when(step == pl.num_programs(0) - 1)
    def _():
        for part in range(wide):
            lanes = slice(part * inner, (part + 1) * inner)
            g_in[lanes, :] = dot_rows(rows_all[:, lanes], dau_all[...]).astype(BF16)
        g_down[...] = dot_rows(hidden_all[...], de_all[...]).astype(BF16)
        made = stores()
        for copy in made:
            copy.start()
        for copy in made:
            copy.wait()


def run_expert(
    expert, me, pieces, masks, h_all, dy_all, ranks, gates, slots, local, earlier
):
    block_count, tokens, width = h_all.shape
    piece_rows, inner = pieces[0].shape[1:]
    count = len(pieces)
    stage_sizes = [1]
    while 2 * sum(stage_sizes) < count:
        stage_sizes.append(sum(stage_sizes))
    stage_sizes += [count // 4, count // 4]
    steps = block_count // BLOCKS_PER_STEP
    rows = block_count * slots
    block_spec = pl.BlockSpec((BLOCKS_PER_STEP, tokens, width), lambda i, s: (i, 0, 0))
    any_spec = pl.BlockSpec(memory_space=pl.ANY)
    table = pl.BlockSpec(ranks.shape, lambda i, s: (0, 0))
    widths = (width, width + LANES)
    copies = count * (2 + width // inner)
    aliases = {}
    extra = []
    if earlier is not None:
        extra = list(earlier)
        aliases = {1 + count + 4: 0, 1 + count + 5: 1}
    return pl.pallas_call(
        functools.partial(expert_kernel, masks, stage_sizes, expert, earlier is not None),
        grid_spec=pltpu.PrefetchScalarGridSpec(
            num_scalar_prefetch=1,
            grid=(steps,),
            in_specs=[any_spec] * count
            + [block_spec, block_spec, table, table]
            + [any_spec] * len(extra),
            out_specs=[
                pl.BlockSpec((BLOCKS_PER_STEP, 1, slots, w), lambda i, s: (i, expert, 0, 0))
                for w in widths
            ]
            + [any_spec] * len(stage_sizes),
            scratch_shapes=[
                pltpu.VMEM((width, 2 * inner), BF16),
                pltpu.VMEM((inner, width), BF16),
                pltpu.VMEM((width, 2 * inner), BF16),
                pltpu.VMEM((inner, width), BF16),
                pltpu.VMEM((rows, width), BF16),
                pltpu.VMEM((rows, width), BF16),
                pltpu.VMEM((rows, inner), BF16),
                pltpu.VMEM((rows, 2 * inner), BF16),
                pltpu.SemaphoreType.DMA((copies,)),
                pltpu.SemaphoreType.DMA((copies,)),
            ],
        ),
        out_shape=[jax.ShapeDtypeStruct((block_count, local, slots, w), BF16) for w in widths]
        + [jax.ShapeDtypeStruct((size, piece_rows, inner), BF16) for size in stage_sizes],
        input_output_aliases=aliases,
        cost_estimate=lasting(31),
        compiler_params=params(60),
    )(me, *pieces, h_all, dy_all, ranks, gates, *extra)


def combine_kernel(src_ref, place_ref, out_ref):
    _, local, slots, width = src_ref.shape
    tokens = out_ref.shape[1]
    lane = lax.broadcasted_iota(jnp.int32, (tokens, local * slots), 1)
    hit = lane == place_ref[0, :, 0:1]
    for expert in range(1, local):
        hit = hit | (lane == place_ref[0, :, expert : expert + 1])
    source = src_ref[0].reshape(local * slots, width)
    out_ref[0] = dot(jnp.where(hit, 1.0, 0.0).astype(BF16), source).astype(BF16)


def combine(source, places, first, size):
    _, local, slots, width = source.shape
    tokens = places.shape[1]
    return pl.pallas_call(
        combine_kernel,
        grid=(size,),
        in_specs=[
            pl.BlockSpec((1, local, slots, width), lambda i: (first + i, 0, 0, 0)),
            pl.BlockSpec((1, tokens, places.shape[2]), lambda i: (first + i, 0, 0)),
        ],
        out_specs=pl.BlockSpec((1, tokens, width), lambda i: (i, 0, 0)),
        out_shape=jax.ShapeDtypeStruct((size, tokens, width), BF16),
        cost_estimate=lasting(4.4),
        compiler_params=params(32),
    )(source, places)


def pack_experts(gate, up, down):
    count, shallow, width = down.shape
    inner = gate.shape[2]
    turned = down.reshape(count, shallow, width // inner, inner).transpose(0, 2, 1, 3)
    return jnp.concatenate(
        [gate, up, turned.reshape(count, shallow * width // inner, inner)], axis=1
    )


def slot_codes(picks, valid, capacity):
    rows = picks.shape[0]
    ids = jnp.arange(EXPERTS, dtype=jnp.int32)
    named = jnp.any(picks[:, :, None] == ids[None, None, :], axis=1)
    counted = (named & valid[:, None]).astype(BF16)
    before = (
        lax.broadcasted_iota(jnp.int32, (rows, rows), 1)
        < lax.broadcasted_iota(jnp.int32, (rows, rows), 0)
    ).astype(BF16)
    ranks = dot(before, counted)
    kept = (counted > 0) & (ranks < capacity[None, :].astype(F32))
    return jnp.where(kept, ranks, jnp.where(named, -1.0, -2.0))


def shards(
    layer_input,
    cotangent,
    lengths,
    routes,
    capacity,
    w_query,
    key_weight,
    value_weight,
    w_output,
    w_router,
    gain_attn,
    gain_moe,
    w_gate,
    w_up,
    w_down,
):
    micro_count, tokens, width = layer_input.shape[1:]
    dp_count, owner_count = lax.axis_size("dp"), lax.axis_size("expert")
    dp_index, owner_index = lax.axis_index("dp"), lax.axis_index("expert")
    slots = tokens // 4
    owned = w_gate.shape[0]
    key_width = key_weight.shape[1]
    dp_bits = dp_count.bit_length() - 1
    owner_bits = owner_count.bit_length() - 1
    split = 2 if owned % 2 == 0 and dp_bits > 1 else 1
    local = owned // split
    pair_bit = 1 if dp_bits > 1 else 0
    dp_places = [("dp", pair_bit)] + [
        ("dp", bit) for bit in reversed(range(dp_bits)) if bit != pair_bit
    ]
    row_places = [("expert", bit) for bit in range(1, owner_bits)]
    key_places = row_places + [("expert", 0)]
    if split == 2:
        token_places = [
            row_places + [("dp", pair_bit), ("expert", 0)],
            [("dp", pair_bit)] + row_places + [("expert", 0)],
        ]
    else:
        token_places = [key_places, key_places]
    half = (dp_index >> pair_bit) & 1 if split == 2 else 0
    first_expert = owner_index * owned + half * local

    rows_owned = w_query.shape[0]

    def dense_gather(parts):
        taken = sum(part.shape[1] for part in parts)
        pad = jnp.zeros((rows_owned, -taken % LANES), BF16)
        packed = jnp.concatenate(parts + [pad], axis=1)
        return lax.all_gather(packed, AXES, axis=0, tiled=True)

    dense_one = dense_gather([w_query, key_weight, value_weight, gain_attn[:, None]])

    def packed_half(which):
        return pack_experts(
            *[
                lax.dynamic_slice_in_dim(weight, which * local, local, 0)
                for weight in (w_gate, w_up, w_down)
            ]
        )

    mine_packed = packed_half(half)
    other_packed = packed_half(1 - half) if split == 2 else mine_packed
    weight_masks = [mask["dp"] for mask in masks_of(dp_places)]
    start_row = owner_index * tokens
    places = start_row + jnp.arange(tokens, dtype=jnp.int32)
    freqs = rope_base ** (-jnp.arange(0, HEAD_DIMENSION, 2, dtype=F32) / HEAD_DIMENSION)
    angles = places.astype(F32)[:, None] * freqs[None, :]
    cos_half, sin_half = jnp.cos(angles), jnp.sin(angles)
    cos = jnp.tile(cos_half, (1, LANES // HALF_HEAD))
    sin = jnp.tile(jnp.concatenate([-sin_half, sin_half], axis=1), (1, LANES // HEAD_DIMENSION))
    cos_t, sin_t = cos_half.T, sin_half.T
    key_starts = jnp.stack(
        [(owner_index ^ mask["expert"]) * tokens for mask in masks_of(key_places)]
    )
    codes, attend_places, dys, dy_rows = [], [], [], []
    for index in range(micro_count):
        length = lengths[0, index]
        valid = places < length
        code = slot_codes(routes[0, index], valid, capacity)
        code = jnp.concatenate([code, jnp.full((tokens, LANES - EXPERTS), -2.0, F32)], axis=1)
        codes.append(code)
        attend_places.append(
            jnp.concatenate([jnp.stack([start_row, length]), key_starts]).astype(jnp.int32)
        )
        dy = jnp.where(valid[:, None], cotangent[0, index], 0)
        dys.append(dy)
        dy_rows.append(jnp.concatenate([dy, code.astype(BF16)], axis=1))

    rows_here = jnp.stack(dy_rows)[None]
    direct = [
        swap(other_packed if stage == 0 else mine_packed, place)
        for stage, place in enumerate(dp_places)
    ]
    dy_received = swap(rows_here, token_places[0][0])
    dense_one, dy_received, *direct = after(dense_one, dy_received, *direct)
    rows_here = jnp.concatenate([rows_here, dy_received], axis=0)

    weight_pieces = [mine_packed, direct[0]]
    for stage, place in enumerate(dp_places[1:], 1):
        received = [direct[stage]]
        for piece in weight_pieces[1:]:
            if len(received) > 1:
                piece, received[-1] = after(piece, received[-1])
            received.append(swap(piece, place))
        weight_pieces = weight_pieces + received
    levels = [index.bit_count() for index in range(len(weight_pieces))]

    def weights_here(value, indices):
        value, *pieces = after(value, *[weight_pieces[index] for index in indices])
        for index, piece in zip(indices, pieces):
            weight_pieces[index] = piece
        return value

    output_rows, dense_one = after(w_output, dense_one)
    dense_two = dense_gather([output_rows, w_router, gain_moe[:, None]])
    for place in token_places[0][1:-1]:
        rows_here = jnp.concatenate([rows_here, swap(rows_here, place)], axis=0)

    gain_one = dense_one[:, width + 2 * key_width].astype(F32)[None]
    gain_two = dense_two[:, width + EXPERTS].astype(F32)[None]
    x = layer_input[0]
    normed, queries, keys_values = project(x, gain_one, dense_one, cos, sin)
    key_rows, attended, log_totals, middles, normed_two, gates = [], [], [], [], [], []
    row_halves = []
    for index in range(micro_count):
        halves = gather_rows(keys_values[index], key_places)
        key_rows.append(jnp.concatenate(halves, axis=0).reshape(-1, 2 * key_width))
    for index in range(micro_count):
        if index == 1:
            attend_places[index], rows_here = after(attend_places[index], rows_here)
            rows_there = swap(rows_here, token_places[0][-1])
        rows, lse = attend(attend_places[index], queries[index], key_rows[index])
        attended.append(rows)
        log_totals.append(lse)
        if index == 1:
            gain_two = weights_here(
                gain_two,
                [
                    i for i, level in enumerate(levels)
                    if level == 2 and i > len(levels) // 2
                ][:1],
            )
        middle, normed_rows, gate = middle_rows(x[index], rows, dense_two, gain_two, codes[index])
        middles.append(middle)
        normed_two.append(normed_rows)
        gates.append(gate)
        row_halves += gather_rows(normed_rows, token_places[index])
    row_all = jnp.concatenate(row_halves, axis=0)
    block_count = row_all.shape[0]
    per_micro = block_count // micro_count

    dy_blocks = []
    for index in range(micro_count):
        order = [token_places[0].index(place) for place in token_places[index]]
        for piece in range(per_micro):
            source = sum((piece >> stage & 1) << order[stage] for stage in range(len(order)))
            side = rows_here if source < per_micro // 2 else rows_there
            dy_blocks.append(side[source % (per_micro // 2), index])
    dy_all = jnp.stack(dy_blocks)
    code_all = dy_all[:, :, width : width + EXPERTS].astype(F32).transpose(2, 0, 1)
    code_all = jnp.roll(code_all.reshape(EXPERTS, block_count * tokens), -first_expert, axis=0)
    rank_table = code_all[:8].astype(jnp.int32)

    router_t = jnp.roll(dense_two[:, width : width + EXPERTS].T, -first_expert, axis=0)
    router_t = weights_here(router_t, [i for i, level in enumerate(levels) if level == 2])
    logits = dot_cols(router_t, row_all.reshape(block_count * tokens, width))
    chosen = code_all > -1.5
    peak = jnp.max(jnp.where(chosen, logits, masked_score), axis=0, keepdims=True)
    raised = jnp.where(chosen, jnp.exp(jnp.where(chosen, logits, peak) - peak), 0.0)
    gate_table = (raised / jnp.sum(raised, axis=0, keepdims=True))[:8]
    me = jnp.stack([dp_index, first_expert]).astype(jnp.int32)
    held = None
    trips = []
    for expert in range(local):
        if 2 <= expert <= 4:
            me = arrive(me, *[trips[0], trips[0], trips[1]][expert - 2 : expert - 1])
            if expert == 4:
                me = arrive(me, trips[0])
        outs = run_expert(
            expert, me, weight_pieces, weight_masks, row_all, dy_all, rank_table,
            gate_table, slots, local, held,
        )
        held = outs[:2]
        trips.append(Trip(list(outs[2:]), dp_places, split))
    eg_all, db_all = held

    slot_place = rank_table[:local]
    slot_place = jnp.where(
        slot_place >= 0, slot_place + slots * jnp.arange(local, dtype=jnp.int32)[:, None], -1
    )
    slot_place = jnp.concatenate(
        [slot_place, jnp.full((8 - local, block_count * tokens), -1, jnp.int32)], axis=0
    )
    slot_place = slot_place.reshape(8, block_count, tokens).transpose(1, 2, 0)

    def first_trade(source, places):
        found = []
        for index in range(micro_count):
            first, size = index * per_micro, per_micro // 2
            high = combine(source, places, first + size, size)
            received = swap(high, token_places[index][-1])
            low = combine(source, places, first, size)
            half_size = size // 2
            found.append(
                [
                    add_rounded(low[:half_size], received[:half_size]),
                    add_rounded(low[half_size:], received[half_size:]),
                ]
            )
        return found

    slot_place = arrive(slot_place, trips[1])
    sums = first_trade(db_all, slot_place)
    sums[1][1] = arrive(sums[1][1], trips[2], trips[1], trips[0])
    received = [
        swap(sums[index][1], token_places[index][-2]) for index in range(micro_count)
    ]
    mix_place, *lows = after(slot_place, *[pair[0] for pair in sums])
    mixed = first_trade(eg_all, mix_place)
    flat, shape = jax.tree.flatten((received, mixed))
    received, mixed = jax.tree.unflatten(shape, lax.optimization_barrier(tuple(flat)))
    row_grads = []
    lows[0] = arrive(lows[0], trips[2])
    for index in range(micro_count):
        total = add_rounded(lows[index], received[index])
        row_grads.append(sum_home(total[:1], total[1:], token_places[index][:1])[0])
    back_gain = arrive(gain_two, trips[3], trips[2], trips[1])

    router_grads, middle_grads, branch_grads, head_grads, gain_two_grads = [], [], [], [], []
    for index in range(micro_count):
        dz, dy1, branch, head_grad, gain_grad = middle_back(
            row_grads[index], middles[index], dys[index], gates[index], back_gain, dense_two
        )
        router_grads.append(dz)
        middle_grads.append(dy1)
        branch_grads.append(branch)
        head_grads.append(head_grad)
        gain_two_grads.append(gain_grad)

    def tall(parts):
        return jnp.concatenate(parts, axis=0)

    def to_owner(grads):
        return lax.psum_scatter(grads, AXES, scatter_dimension=0, tiled=True).astype(F32)

    gain_two_grads[0] = arrive(gain_two_grads[0], trips[3])
    early = weight_grads(
        [tall(attended), tall(normed_two)],
        [tall(branch_grads), tall(router_grads)],
        sum(gain_two_grads),
        width + LANES,
    )
    output_grads = to_owner(early)
    head_grads[0], early = after(head_grads[0], early)

    query_grads, pair_grads = [], []
    for index in range(micro_count):
        if index == micro_count - 1:
            attend_places[index], query_grads[0] = after(attend_places[index], query_grads[0])
            attend_places[index] = arrive(attend_places[index], trips[4], trips[3], trips[2])
        dq, pairs = attend_back(
            attend_places[index], queries[index], key_rows[index], head_grads[index],
            attended[index], log_totals[index], cos_t, sin_t,
        )
        pairs = pairs.reshape(owner_count, tokens, pairs.shape[1])
        middle_point = owner_count // 2
        pair_grads.append(sum_home(pairs[:middle_point], pairs[middle_point:], key_places)[0])
        query_grads.append(dq)
    normed_all = normed.reshape(micro_count * tokens, width)

    query_grads[-1], *highs = after(query_grads[-1], *[pair[1] for pair in mixed])
    last_gain = arrive(gain_one, trips[4])
    mix_received = [
        swap(highs[index], token_places[index][-2]) for index in range(micro_count)
    ]
    key_grads, input_grads, gain_one_grads = [], [], []
    for index in range(micro_count):
        dx, dkv, gain_grad = project_back(
            query_grads[index], pair_grads[index], x[index], middle_grads[index], last_gain,
            dense_one, cos, sin,
        )
        input_grads.append(dx)
        key_grads.append(dkv)
        gain_one_grads.append(gain_grad)
    gain_one_grad = arrive(sum(gain_one_grads), trips[4], trips[3])
    gain_one_grad, output_grads, *mix_received = after(gain_one_grad, output_grads, *mix_received)
    late = weight_grads(
        [normed_all, normed_all],
        [tall(query_grads), tall(key_grads)],
        gain_one_grad,
        width + 2 * key_width + LANES,
    )
    late_grads = to_owner(late)
    mix_received[0], late = after(mix_received[0], late)
    mixtures = []
    for index in range(micro_count):
        total = add_rounded(mixed[index][0], mix_received[index])
        mixtures.append(sum_home(total[:1], total[1:], token_places[index][:1])[0])
    layer_output = jnp.stack(
        [
            (middles[index] + mixtures[index].astype(F32)).astype(BF16)
            for index in range(micro_count)
        ]
    )[None]
    for trip in trips:
        while trip.mine is None:
            trip.step(trip.waiting.pop(0))

    mine = jnp.stack([trip.mine for trip in trips])
    if split == 2:
        other = jnp.stack([trip.other for trip in trips])
        lower = half == 0
        mine = jnp.concatenate(
            [jnp.where(lower, mine, other), jnp.where(lower, other, mine)], axis=0
        )
    deep = w_gate.shape[1]
    inner = w_gate.shape[2]
    grad_gate = mine[:, :deep]
    grad_up = mine[:, deep : 2 * deep]
    grad_down = (
        mine[:, 2 * deep :]
        .reshape(owned, width // inner, w_down.shape[1], inner)
        .transpose(0, 2, 1, 3)
        .reshape(w_down.shape)
    )
    return (
        layer_output,
        jnp.stack(input_grads)[None],
        late_grads[:, :width],
        late_grads[:, width : width + key_width],
        late_grads[:, width + key_width : width + 2 * key_width],
        output_grads[:, :width],
        output_grads[:, width : width + EXPERTS],
        late_grads[:, width + 2 * key_width + EXPERTS],
        output_grads[:, width + EXPERTS],
        grad_gate,
        grad_up,
        grad_down,
    )


def solution(mesh):
    return jax.shard_map(
        shards,
        mesh=mesh,
        in_specs=(
            P("dp", None, "expert", None),
            P("dp", None, "expert", None),
            P("dp", None),
            P("dp", None, "expert", None),
            P(),
            P(("dp", "expert"), None),
            P(("dp", "expert"), None),
            P(("dp", "expert"), None),
            P(("dp", "expert"), None),
            P(("dp", "expert"), None),
            P(("dp", "expert")),
            P(("dp", "expert")),
            P("expert", "dp", None),
            P("expert", "dp", None),
            P("expert", "dp", None),
        ),
        out_specs=(
            P("dp", None, "expert", None),
            P("dp", None, "expert", None),
            P(("dp", "expert"), None),
            P(("dp", "expert"), None),
            P(("dp", "expert"), None),
            P(("dp", "expert"), None),
            P(("dp", "expert"), None),
            P(("dp", "expert")),
            P(("dp", "expert")),
            P("expert", "dp", None),
            P("expert", "dp", None),
            P("expert", "dp", None),
        ),
        check_vma=False,
    )
```

```python
import functools

import jax
import jax.numpy as jnp
from jax import lax
from jax.experimental import pallas as pl
from jax.experimental.pallas import tpu as pltpu
from jax.sharding import PartitionSpec as P

QUERY_HEAD_COUNT = 24
KEY_VALUE_HEADS = 8
HEAD_DIMENSION = 64
EXPERTS = 40
TOPK = 8

epsilon = 1e-06
rope_base = 10000.0
masked_score = -1e30

F32 = jnp.float32
BF16 = jnp.bfloat16
AXES = ("dp", "expert")
HALF_HEAD = HEAD_DIMENSION // 2
GROUP = QUERY_HEAD_COUNT // KEY_VALUE_HEADS
PAIRS = KEY_VALUE_HEADS // 2
PAIR_LANES = 2 * HEAD_DIMENSION
QUERY_LANES = GROUP * PAIR_LANES
LANES = 128
BLOCKS_PER_STEP = 4


def dot(left, right):
    return jnp.dot(left, right, preferred_element_type=F32)


def dot_rows(left, right):
    return lax.dot_general(left, right, (((0,), (0,)), ((), ())), preferred_element_type=F32)


def dot_cols(left, right):
    return lax.dot_general(left, right, (((1,), (1,)), ((), ())), preferred_element_type=F32)


def add_rounded(left, right):
    return (left.astype(F32) + right.astype(F32)).astype(left.dtype)


def params(limit_mib, steps=1):
    return pltpu.CompilerParams(
        dimension_semantics=("arbitrary",) * steps, vmem_limit_bytes=limit_mib << 20
    )


def lasting(micros):
    return pl.CostEstimate(flops=int(micros * 3e7), bytes_accessed=0, transcendentals=0)


def whole_spec():
    return pl.BlockSpec(memory_space=pltpu.VMEM)


def swap(array, place):
    axis, bit = place
    dp_count, owner_count = lax.axis_size("dp"), lax.axis_size("expert")
    flip = (1 << bit) * (owner_count if axis == "dp" else 1)
    return lax.ppermute(array, AXES, [(i, i ^ flip) for i in range(dp_count * owner_count)])


def gather_pieces(array, places):
    pieces = [array]
    for place in places:
        pieces = pieces + [swap(piece, place) for piece in pieces]
    return pieces


def after(value, *others):
    return lax.optimization_barrier((value, *others))


def gather_rows(array, places):
    pieces = jnp.stack(gather_pieces(array, places[:-1]))
    return pieces, swap(pieces, places[-1])


def sum_home(low, high, places):
    for place in reversed(places):
        total = high.shape[0]
        received = swap(high, place)
        if total == 1:
            return add_rounded(low, received)
        low, high = (
            add_rounded(low[: total // 2], received[: total // 2]),
            add_rounded(low[total // 2 :], received[total // 2 :]),
        )
    return low


def without_bit(index, bit):
    return ((index >> (bit + 1)) << bit) | (index & ((1 << bit) - 1))


class Homeward:
    def __init__(self, grads, places):
        bits = lax.axis_size("dp").bit_length() + lax.axis_size("expert").bit_length() - 2
        self.held = grads.reshape((2,) * bits + (grads.shape[0] >> bits, grads.shape[1]))
        self.ranks = list(reversed(range(bits)))
        self.places = list(places)
        self.start()

    def start(self):
        axis, bit = self.places[0]
        owner_bits = lax.axis_size("expert").bit_length() - 1
        depth = self.ranks.index(bit + (owner_bits if axis == "dp" else 0))
        self.ranks.pop(depth)
        upper = (lax.axis_index(axis) >> bit) & 1
        away = lax.dynamic_index_in_dim(self.held, 1 - upper, depth, False)
        self.held = lax.dynamic_index_in_dim(self.held, upper, depth, False)
        self.received = swap(away, self.places.pop(0))

    def join(self):
        self.held = add_rounded(self.held, self.received)
        if self.places:
            self.start()
        else:
            self.received = None

    def pin(self, value):
        value, self.received = after(value, self.received)
        self.join()
        return value

    def rows(self):
        while self.received is not None:
            self.join()
        return self.held.astype(F32)


def masks_of(places):
    found = []
    for piece in range(1 << len(places)):
        mask = {"dp": 0, "expert": 0}
        for stage, (axis, bit) in enumerate(places):
            if piece >> stage & 1:
                mask[axis] |= 1 << bit
        found.append(mask)
    return found


def half_swap(rows):
    lane = lax.broadcasted_iota(jnp.int32, rows.shape, 1)
    return jnp.where(
        lane % HEAD_DIMENSION < HALF_HEAD,
        pltpu.roll(rows, rows.shape[1] - HALF_HEAD, 1),
        pltpu.roll(rows, HALF_HEAD, 1),
    )


def project_kernel(x_ref, gain_ref, w_ref, cos_ref, sin_ref, h_ref, q_ref, kv_ref):
    x = x_ref[0].astype(F32)
    scale = lax.rsqrt(jnp.mean(x * x, axis=1, keepdims=True) + epsilon)
    h_ref[0] = (x * scale * gain_ref[...]).astype(BF16)
    cos, sin = cos_ref[...], sin_ref[...]
    width = q_ref.shape[2]
    key_width = kv_ref.shape[2] // 2

    def turn_into(out_ref, start, rows):
        for tile in range(0, rows.shape[1], LANES):
            part = rows[:, tile : tile + LANES]
            out_ref[0, :, start + tile : start + tile + LANES] = (
                part * cos + half_swap(part) * sin
            ).astype(BF16)

    first = width + LANES
    for start in range(0, width, key_width):
        turn_into(q_ref, start, dot(h_ref[0], w_ref[:, first + start : first + start + key_width]))
    first = first + width
    turn_into(kv_ref, 0, dot(h_ref[0], w_ref[:, first : first + key_width]))
    value = dot(h_ref[0], w_ref[:, first + key_width : first + 2 * key_width])
    kv_ref[0, :, key_width:] = value.astype(BF16)


def project(x, gain, dense, cos, sin):
    count, rows, width = x.shape
    key_width = KEY_VALUE_HEADS * HEAD_DIMENSION
    row_spec = pl.BlockSpec((1, rows, width), lambda i: (i, 0, 0))
    return pl.pallas_call(
        project_kernel,
        grid=(count,),
        in_specs=[
            row_spec,
            pl.BlockSpec((1, width), lambda i: (0, 0)),
            pl.BlockSpec(dense.shape, lambda i: (0, 0), pipeline_mode=pl.Buffered(1)),
            pl.BlockSpec((rows, LANES), lambda i: (0, 0)),
            pl.BlockSpec((rows, LANES), lambda i: (0, 0)),
        ],
        out_specs=[
            row_spec,
            row_spec,
            pl.BlockSpec((1, rows, 2 * key_width), lambda i: (i, 0, 0)),
        ],
        out_shape=[
            jax.ShapeDtypeStruct(x.shape, BF16),
            jax.ShapeDtypeStruct(x.shape, BF16),
            jax.ShapeDtypeStruct((count, rows, 2 * key_width), BF16),
        ],
        cost_estimate=lasting(8),
        compiler_params=params(48),
    )(x, gain, dense, cos, sin)


def middle_kernel(x_ref, o_ref, wo_ref, wr_ref, gain_ref, code_ref, y_ref, h_ref, g_ref):
    middle = x_ref[...].astype(F32) + dot(o_ref[...], wo_ref[...])
    y_ref[...] = middle
    scale = lax.rsqrt(jnp.mean(middle * middle, axis=1, keepdims=True) + epsilon)
    normed = (middle * scale * gain_ref[...]).astype(BF16)
    h_ref[...] = normed
    logits = dot(normed, wr_ref[...])
    chosen = code_ref[...] > -1.5
    peak = jnp.max(jnp.where(chosen, logits, masked_score), axis=1, keepdims=True)
    raised = jnp.where(chosen, jnp.exp(jnp.where(chosen, logits, peak) - peak), 0.0)
    g_ref[...] = raised / jnp.sum(raised, axis=1, keepdims=True)


def middle_rows(x, attended, dense, gain, code):
    rows, width = x.shape
    full = pl.BlockSpec((rows, width), lambda i: (0, 0))
    return pl.pallas_call(
        middle_kernel,
        grid=(1,),
        in_specs=[
            full,
            full,
            pl.BlockSpec((width, width), lambda i: (0, 0)),
            pl.BlockSpec((width, LANES), lambda i: (0, width // LANES)),
            pl.BlockSpec((1, width), lambda i: (0, 0)),
            pl.BlockSpec((rows, LANES), lambda i: (0, 0)),
        ],
        out_specs=[full, full, pl.BlockSpec((rows, LANES), lambda i: (0, 0))],
        out_shape=[
            jax.ShapeDtypeStruct((rows, width), F32),
            jax.ShapeDtypeStruct((rows, width), BF16),
            jax.ShapeDtypeStruct((rows, LANES), F32),
        ],
        cost_estimate=lasting(4.5),
        compiler_params=params(48),
    )(x, attended, dense, dense, gain, code)


def middle_back_kernel(
    acc_ref, y_ref, dy_ref, g_ref, dg_ref, gain_ref, wr_ref, wo_ref,
    dz_ref, dy1_ref, dr_ref, do_ref, dgain_ref,
):
    gates, gate_grads = g_ref[...], dg_ref[...].astype(F32)
    mean = jnp.sum(gates * gate_grads, axis=1, keepdims=True)
    dz = (gates * (gate_grads - mean)).astype(BF16)
    dz_ref[...] = dz
    dh = acc_ref[...].astype(F32) + dot_cols(dz, wr_ref[...])
    middle = y_ref[...]
    scale = lax.rsqrt(jnp.mean(middle * middle, axis=1, keepdims=True) + epsilon)
    dgain_ref[...] = jnp.sum(dh * middle * scale, axis=0, keepdims=True)
    scaled = dh * gain_ref[...]
    along = jnp.mean(scaled * middle, axis=1, keepdims=True)
    dy1 = dy_ref[...].astype(F32) + scale * scaled - middle * (scale * scale * scale * along)
    dy1_ref[...] = dy1
    rounded = dy1.astype(BF16)
    dr_ref[...] = rounded
    do_ref[...] = dot_cols(rounded, wo_ref[...]).astype(BF16)


def middle_back(acc, middle, dy, gates, gain, dense):
    rows, width = middle.shape
    full = pl.BlockSpec((rows, width), lambda i: (0, 0))
    lane = pl.BlockSpec((rows, LANES), lambda i: (0, 0))
    line = pl.BlockSpec((1, width), lambda i: (0, 0))
    return pl.pallas_call(
        middle_back_kernel,
        grid=(1,),
        in_specs=[
            full, full, full, lane,
            pl.BlockSpec((rows, LANES), lambda i: (0, width // LANES)),
            line,
            pl.BlockSpec((width, LANES), lambda i: (0, width // LANES)),
            pl.BlockSpec((width, width), lambda i: (0, 0)),
        ],
        out_specs=[lane, full, full, full, line],
        out_shape=[
            jax.ShapeDtypeStruct((rows, LANES), BF16),
            jax.ShapeDtypeStruct((rows, width), F32),
            jax.ShapeDtypeStruct((rows, width), BF16),
            jax.ShapeDtypeStruct((rows, width), BF16),
            jax.ShapeDtypeStruct((1, width), F32),
        ],
        cost_estimate=lasting(6.6),
        compiler_params=params(56),
    )(acc, middle, dy, gates, acc, gain, dense, dense)


def project_back_kernel(
    dq_ref, pairs_ref, x_ref, dy1_ref, gain_ref, w_ref, cos_ref, sin_ref,
    dx_ref, dkv_ref, dgain_ref,
):
    cos, sin = cos_ref[...], sin_ref[...]
    width = x_ref.shape[1]
    key_width = dkv_ref.shape[1] // 2
    for pair in range(PAIRS):
        lanes = slice(pair * LANES, (pair + 1) * LANES)
        start = 2 * pair * LANES
        part = pairs_ref[:, start : start + LANES].astype(F32)
        dkv_ref[:, lanes] = (part * cos - half_swap(part) * sin).astype(BF16)
        lanes = slice(key_width + pair * LANES, key_width + (pair + 1) * LANES)
        dkv_ref[:, lanes] = pairs_ref[:, start + LANES : start + 2 * LANES]
    first = width + LANES
    dh = dot_cols(dq_ref[...], w_ref[:, first : first + width])
    first = first + width
    dh = dh + dot_cols(dkv_ref[...], w_ref[:, first : first + 2 * key_width])
    x = x_ref[...].astype(F32)
    scale = lax.rsqrt(jnp.mean(x * x, axis=1, keepdims=True) + epsilon)
    dgain_ref[...] = jnp.sum(dh * x * scale, axis=0, keepdims=True)
    scaled = dh * gain_ref[...]
    along = jnp.mean(scaled * x, axis=1, keepdims=True)
    dx_ref[...] = dy1_ref[...] + scale * scaled - x * (scale * scale * scale * along)


def project_back(dq, pairs, x, dy1, gain, dense, cos, sin):
    rows, width = x.shape
    key_width = pairs.shape[1] // 2
    full = pl.BlockSpec((rows, width), lambda i: (0, 0))
    lane = pl.BlockSpec((rows, LANES), lambda i: (0, 0))
    line = pl.BlockSpec((1, width), lambda i: (0, 0))
    both = pl.BlockSpec((rows, 2 * key_width), lambda i: (0, 0))
    return pl.pallas_call(
        project_back_kernel,
        grid=(1,),
        in_specs=[
            full, both, full, full, line,
            pl.BlockSpec(dense.shape, lambda i: (0, 0), pipeline_mode=pl.Buffered(1)),
            lane, lane,
        ],
        out_specs=[full, both, line],
        out_shape=[
            jax.ShapeDtypeStruct((rows, width), F32),
            jax.ShapeDtypeStruct((rows, 2 * key_width), BF16),
            jax.ShapeDtypeStruct((1, width), F32),
        ],
        cost_estimate=lasting(8.2),
        compiler_params=params(56),
    )(dq, pairs, x, dy1, gain, dense, cos, sin)


def weight_grad_kernel(count, *refs):
    left_refs, right_refs, out_ref = refs[:count], refs[count : 2 * count], refs[-1]
    rows, columns = out_ref.shape
    if len(refs) > 2 * count + 1:
        gain = jnp.broadcast_to(refs[2 * count][...], (8, rows)).T
    lane = lax.broadcasted_iota(jnp.int32, (rows, LANES), 1)
    start = 0
    for left_ref, right_ref in zip(left_refs, right_refs):
        left = left_ref[...].T
        width = right_ref.shape[1]
        step = min(width, 4 * LANES)
        for tile in range(0, width, step):
            part = dot(left, right_ref[:, tile : tile + step])
            if start + tile + step == columns and len(refs) > 2 * count + 1:
                edge = part[:, step - LANES :]
                edge = jnp.where(lane == EXPERTS, gain[:, 0:1], edge)
                out_ref[:, columns - LANES :] = edge.astype(BF16)
                part = part[:, : step - LANES]
            if part.shape[1]:
                out_ref[:, start + tile : start + tile + part.shape[1]] = part.astype(BF16)
        start += width
    if start < columns:
        out_ref[:, start:] = jnp.where(lane == EXPERTS, gain[:, 0:1], 0.0).astype(BF16)


def weight_grads(lefts, rights, gain, columns):
    rows = lefts[0].shape[1]
    operands = [*lefts, *rights] + ([] if gain is None else [gain])
    return pl.pallas_call(
        functools.partial(weight_grad_kernel, len(lefts)),
        in_specs=[whole_spec() for _ in operands],
        out_specs=whole_spec(),
        out_shape=jax.ShapeDtypeStruct((rows, columns), BF16),
        cost_estimate=lasting(9),
        compiler_params=pltpu.CompilerParams(vmem_limit_bytes=56 << 20),
    )(*operands)


def fill_bias(places_ref, bias_ref, rows):
    query = places_ref[0] + lax.broadcasted_iota(jnp.int32, (rows, rows), 1)
    inside = lax.broadcasted_iota(jnp.int32, (rows, rows), 0)
    for block in range(bias_ref.shape[0] // rows):
        key = places_ref[2 + block] + inside
        allowed = (key <= query) & (key < places_ref[1])
        bias_ref[block * rows : (block + 1) * rows, :] = jnp.where(allowed, 0.0, masked_score)


def attend_kernel(places_ref, q_ref, k_ref, v_ref, o_ref, lse_ref, bias_ref):
    rows = q_ref.shape[0]

    @pl.when(pl.program_id(0) == 0)
    def _():
        fill_bias(places_ref, bias_ref, rows)

    outs = []
    for side in range(2):
        lanes = slice(side * HEAD_DIMENSION, (side + 1) * HEAD_DIMENSION)
        key = k_ref[:, lanes]
        value_t = v_ref[:, lanes].T
        for member in range(GROUP):
            head = side * GROUP + member
            query = q_ref[:, head * HEAD_DIMENSION : (head + 1) * HEAD_DIMENSION]
            scores = dot_cols(key, query * HEAD_DIMENSION**-0.5) + bias_ref[...]
            peak = jnp.max(scores, axis=0, keepdims=True)
            raised = jnp.exp(scores - peak)
            total = jnp.sum(raised, axis=0, keepdims=True)
            outs.append(dot(value_t, raised.astype(BF16)) / total)
            lse_ref[0, head : head + 1, :] = peak + jnp.log(total)
    o_ref[...] = jnp.concatenate(outs, axis=0).T.astype(BF16)


def attend(places, q, kv):
    rows, width = q.shape
    keys = kv.shape[0]
    return pl.pallas_call(
        attend_kernel,
        grid_spec=pltpu.PrefetchScalarGridSpec(
            num_scalar_prefetch=1,
            grid=(PAIRS,),
            in_specs=[
                pl.BlockSpec((rows, QUERY_LANES), lambda i, s: (0, i)),
                pl.BlockSpec((keys, PAIR_LANES), lambda i, s: (0, i)),
                pl.BlockSpec((keys, PAIR_LANES), lambda i, s: (0, PAIRS + i)),
            ],
            out_specs=[
                pl.BlockSpec((rows, QUERY_LANES), lambda i, s: (0, i)),
                pl.BlockSpec((1, 8, rows), lambda i, s: (i, 0, 0)),
            ],
            scratch_shapes=[pltpu.VMEM((keys, rows), F32)],
        ),
        out_shape=[
            jax.ShapeDtypeStruct((rows, width), BF16),
            jax.ShapeDtypeStruct((PAIRS, 8, rows), F32),
        ],
        cost_estimate=lasting(19),
        compiler_params=params(48),
    )(places, q, kv, kv)


def attend_back_kernel(
    places_ref, q_ref, k_ref, v_ref, do_ref, o_ref, lse_ref, cos_ref, sin_ref,
    dq_ref, dkv_ref, bias_ref,
):
    rows = q_ref.shape[0]

    @pl.when(pl.program_id(0) == 0)
    def _():
        fill_bias(places_ref, bias_ref, rows)

    score_scale = HEAD_DIMENSION**-0.5
    cos, sin = cos_ref[...], sin_ref[...]
    ones = jnp.ones((8, HEAD_DIMENSION), F32)
    query_grads = []
    for side in range(2):
        lanes = slice(side * HEAD_DIMENSION, (side + 1) * HEAD_DIMENSION)
        key, value = k_ref[:, lanes], v_ref[:, lanes]
        key_t = key.T
        key_grad = None
        value_grad = None
        for member in range(GROUP):
            head = side * GROUP + member
            columns = slice(head * HEAD_DIMENSION, (head + 1) * HEAD_DIMENSION)
            query = q_ref[:, columns] * score_scale
            grad = do_ref[:, columns]
            overlap = grad.astype(F32) * o_ref[:, columns].astype(F32)
            along = lax.dot_general(
                ones, overlap, (((1,), (1,)), ((), ())),
                precision=lax.Precision.HIGHEST, preferred_element_type=F32,
            )[0:1]
            scores = dot_cols(key, query) + bias_ref[...]
            probs = jnp.exp(scores - lse_ref[0, head : head + 1, :])
            score_grad = (probs * (dot_cols(value, grad) - along)).astype(BF16)
            value_part = dot(probs.astype(BF16), grad)
            key_part = dot(score_grad, query)
            value_grad = value_part if value_grad is None else value_grad + value_part
            key_grad = key_part if key_grad is None else key_grad + key_part
            turned = dot(key_t, score_grad) * score_scale
            upper, lower = turned[:HALF_HEAD], turned[HALF_HEAD:]
            query_grads += [upper * cos + lower * sin, lower * cos - upper * sin]
        dkv_ref[:, lanes] = key_grad.astype(BF16)
        shifted = slice(LANES + side * HEAD_DIMENSION, LANES + (side + 1) * HEAD_DIMENSION)
        dkv_ref[:, shifted] = value_grad.astype(BF16)
    dq_ref[...] = jnp.concatenate(query_grads, axis=0).T.astype(BF16)


def attend_back(places, q, kv, grad, attended, lse, cos_t, sin_t):
    rows, width = q.shape
    keys = kv.shape[0]
    key_width = kv.shape[1] // 2
    wide = pl.BlockSpec((rows, QUERY_LANES), lambda i, s: (0, i))
    tall = pl.BlockSpec((keys, PAIR_LANES), lambda i, s: (0, i))
    table = pl.BlockSpec((HALF_HEAD, rows), lambda i, s: (0, 0))
    return pl.pallas_call(
        attend_back_kernel,
        grid_spec=pltpu.PrefetchScalarGridSpec(
            num_scalar_prefetch=1,
            grid=(PAIRS,),
            in_specs=[
                wide,
                tall,
                pl.BlockSpec((keys, PAIR_LANES), lambda i, s: (0, PAIRS + i)),
                wide,
                wide,
                pl.BlockSpec((1, 8, rows), lambda i, s: (i, 0, 0)),
                table,
                table,
            ],
            out_specs=[wide, pl.BlockSpec((keys, 2 * PAIR_LANES), lambda i, s: (0, i))],
            scratch_shapes=[pltpu.VMEM((keys, rows), F32)],
        ),
        out_shape=[
            jax.ShapeDtypeStruct((rows, width), BF16),
            jax.ShapeDtypeStruct((keys, 2 * key_width), BF16),
        ],
        cost_estimate=lasting(23.5),
        compiler_params=params(56),
    )(places, q, kv, kv, grad, attended, lse, cos_t, sin_t)


def expert_kernel(masks, sources, pair_bit, first, aliased, me_ref, *refs):
    count = len(masks)
    arrays = 1 + max(array for per_expert in sources for array, _ in per_expert)
    pieces, refs = refs[:arrays], refs[arrays:]
    h_ref, dy_ref, rank_ref, gate_ref = refs[:4]
    refs = refs[4 + (2 if aliased else 0) :]
    eg_ref, db_ref = refs[:2]
    out_ref, refs = refs[2], refs[3:]
    w_in, w_down, g_in, g_down, rows_all, de_all, hidden_all, dau_all, in_sem, out_sem = refs
    member, step = pl.program_id(0), pl.program_id(1)
    expert = first + member
    side = lax.rem(member, 2)
    blocks, tokens, width = h_ref.shape
    slots = eg_ref.shape[2]
    chunk = blocks * slots
    inner = w_down.shape[1]
    deep = width // count
    shallow = inner // count
    wide = width // inner
    me = me_ref[0]

    def windows(piece_ref, shard, into, down):
        top = pl.ds(pl.multiple_of(shard * deep, 16), deep)
        low = pl.ds(pl.multiple_of(shard * shallow, 16), shallow)
        pairs = [
            (piece_ref.at[pl.ds(0, deep)], into.at[top, pl.ds(0, inner)]),
            (piece_ref.at[pl.ds(deep, deep)], into.at[top, pl.ds(inner, inner)]),
        ]
        for part in range(wide):
            pairs.append(
                (
                    piece_ref.at[pl.ds(2 * deep + part * shallow, shallow)],
                    down.at[low, pl.ds(part * inner, inner)],
                )
            )
        return pairs

    def loads(which):
        made = []
        into, down, sems = w_in.at[which % 2], w_down.at[which % 2], in_sem.at[which % 2]
        for (array, index), mask in zip(sources[which], masks):
            for source, target in windows(pieces[array].at[index], me ^ mask, into, down):
                made.append(pltpu.make_async_copy(source, target, sems.at[len(made)]))
        return made

    def stores(which):
        made = []
        for piece, mask in enumerate(masks):
            target = out_ref.at[without_bit(me ^ mask, pair_bit), piece & 1, which]
            for there, here in windows(target, me ^ mask, g_in, g_down):
                made.append(pltpu.make_async_copy(here, there, out_sem.at[len(made)]))
        return made

    for which in range(len(sources)):
        early = (member == 0) & (step == 0) if which == 0 else (member == which - 1) & (step == 1)

        @pl.when(early)
        def _(which=which):
            for copy in loads(which):
                copy.start()

    slot = lax.broadcasted_iota(jnp.int32, (slots, tokens), 0)
    grads = []
    weights = []
    for block in range(blocks):
        start = pl.multiple_of((step * blocks + block) * tokens, LANES)
        hit = slot == rank_ref[expert, :, pl.ds(start, tokens)]
        select = jnp.where(hit, 1.0, 0.0).astype(BF16)
        place = pl.ds(pl.multiple_of(step * chunk + block * slots, 16), slots)
        rows_all[place, :] = dot(select, h_ref[block]).astype(BF16)
        grads.append(dot(select, dy_ref[block]))
        gate = gate_ref[expert, :, pl.ds(start, tokens)]
        weights.append(jnp.sum(jnp.where(hit, gate, 0.0), axis=1, keepdims=True))

    for which in range(len(sources)):

        @pl.when((member == which) & (step == 0))
        def _(which=which):
            for copy in loads(which):
                copy.wait()

    here = pl.ds(pl.multiple_of(step * chunk, 16), chunk)
    grad_rows = jnp.concatenate(grads, axis=0)
    weight = jnp.concatenate(weights, axis=0)
    pre = dot(rows_all[here, :], w_in[side])
    gate_pre, up_pre = pre[:, :inner], pre[:, inner:]
    sigmoid = 1.0 / (1.0 + jnp.exp(-gate_pre))
    silu = gate_pre * sigmoid
    hidden = (silu * up_pre).astype(BF16)
    hidden_all[here, :] = hidden
    out = dot(hidden, w_down[side]).astype(BF16).astype(F32)
    row_grad = jnp.sum(grad_rows * out, axis=1, keepdims=True)
    out = (weight * out).astype(BF16)
    lane = lax.broadcasted_iota(jnp.int32, (slots, LANES), 1)
    for block in range(blocks):
        part = slice(block * slots, (block + 1) * slots)
        eg_ref[block, 0] = out[part]
        db_ref[block, 0, :, width:] = jnp.where(lane == me_ref[1] + expert, row_grad[part], 0.0).astype(
            BF16
        )
    de = (weight * grad_rows).astype(BF16)
    de_all[here, :] = de
    grad_hidden = dot_cols(de, w_down[side])
    grad_up = (grad_hidden * silu).astype(BF16)
    grad_gate = (
        grad_hidden * up_pre * sigmoid * (1.0 + gate_pre * (1.0 - sigmoid))
    ).astype(BF16)
    dau_all[here, :inner] = grad_gate
    dau_all[here, inner:] = grad_up
    back = dot_cols(dau_all[here, :], w_in[side]).astype(BF16)
    for block in range(blocks):
        db_ref[block, 0, :, :width] = back[block * slots : (block + 1) * slots]

    last = step == pl.num_programs(1) - 1
    for which in range(1, len(sources)):

        @pl.when(last & (member == which))
        def _(which=which):
            for copy in stores(which - 1):
                copy.wait()

    @pl.when(last)
    def _():
        for part in range(wide):
            lanes = slice(part * inner, (part + 1) * inner)
            g_in[lanes, :] = dot_rows(rows_all[:, lanes], dau_all[...]).astype(BF16)
        g_down[...] = dot_rows(hidden_all[...], de_all[...]).astype(BF16)

    for which in range(len(sources)):

        @pl.when(last & (member == which))
        def _(which=which):
            for copy in stores(which):
                copy.start()
            if which == len(sources) - 1:
                for copy in stores(which):
                    copy.wait()


def run_experts(first, me, pieces, masks, pair_bit, h_all, dy_all, ranks, gates, slots, local, earlier):
    block_count, tokens, width = h_all.shape
    members = len(pieces)
    arrays = []
    sources = []
    for per_expert in pieces:
        found = []
        for array, index in per_expert:
            known = [place for place, other in enumerate(arrays) if other is array]
            if not known:
                known = [len(arrays)]
                arrays.append(array)
            found.append((known[0], index))
        sources.append(found)
    piece_rows, inner = arrays[0].shape[1:]
    count = len(masks)
    steps = block_count // BLOCKS_PER_STEP
    rows = block_count * slots
    block_spec = pl.BlockSpec((BLOCKS_PER_STEP, tokens, width), lambda g, i, s: (i, 0, 0))
    any_spec = pl.BlockSpec(memory_space=pl.ANY)
    table = pl.BlockSpec((ranks.shape[0], 1, ranks.shape[1]), lambda g, i, s: (0, 0, 0))
    widths = (width, width + LANES)
    copies = count * (2 + width // inner)
    extra = [] if earlier is None else list(earlier)
    start = 1 + len(arrays) + 4
    aliases = {start + place: place for place in range(len(extra))}
    return pl.pallas_call(
        functools.partial(expert_kernel, masks, sources, pair_bit, first, earlier is not None),
        grid_spec=pltpu.PrefetchScalarGridSpec(
            num_scalar_prefetch=1,
            grid=(members, steps),
            in_specs=[any_spec] * len(arrays)
            + [block_spec, block_spec, table, table]
            + [any_spec] * len(extra),
            out_specs=[
                pl.BlockSpec(
                    (BLOCKS_PER_STEP, 1, slots, w), lambda g, i, s: (i, first + g, 0, 0)
                )
                for w in widths
            ]
            + [any_spec],
            scratch_shapes=[
                pltpu.VMEM((2, width, 2 * inner), BF16),
                pltpu.VMEM((2, inner, width), BF16),
                pltpu.VMEM((width, 2 * inner), BF16),
                pltpu.VMEM((inner, width), BF16),
                pltpu.VMEM((rows, width), BF16),
                pltpu.VMEM((rows, width), BF16),
                pltpu.VMEM((rows, inner), BF16),
                pltpu.VMEM((rows, 2 * inner), BF16),
                pltpu.SemaphoreType.DMA((2, copies)),
                pltpu.SemaphoreType.DMA((copies,)),
            ],
        ),
        out_shape=[jax.ShapeDtypeStruct((block_count, local, slots, w), BF16) for w in widths]
        + [jax.ShapeDtypeStruct((count // 2, 2, members, piece_rows, inner), BF16)],
        input_output_aliases=aliases,
        cost_estimate=lasting(31 * members),
        compiler_params=params(60, 2),
    )(me, *arrays, h_all, dy_all, ranks[:, None], gates[:, None], *extra)


def combine_kernel(src_ref, place_ref, out_ref):
    _, local, slots, width = src_ref.shape
    tokens = out_ref.shape[1]
    lane = lax.broadcasted_iota(jnp.int32, (tokens, local * slots), 1)
    hit = lane == place_ref[0, :, 0:1]
    for expert in range(1, local):
        hit = hit | (lane == place_ref[0, :, expert : expert + 1])
    source = src_ref[0].reshape(local * slots, width)
    out_ref[0] = dot(jnp.where(hit, 1.0, 0.0).astype(BF16), source).astype(BF16)


def combine(source, places, first, size):
    _, local, slots, width = source.shape
    tokens = places.shape[1]
    return pl.pallas_call(
        combine_kernel,
        grid=(size,),
        in_specs=[
            pl.BlockSpec((1, local, slots, width), lambda i: (first + i, 0, 0, 0)),
            pl.BlockSpec((1, tokens, places.shape[2]), lambda i: (first + i, 0, 0)),
        ],
        out_specs=pl.BlockSpec((1, tokens, width), lambda i: (i, 0, 0)),
        out_shape=jax.ShapeDtypeStruct((size, tokens, width), BF16),
        cost_estimate=lasting(4.4),
        compiler_params=params(60),
    )(source, places)


def pack_experts(gate, up, down):
    count, shallow, width = down.shape
    inner = gate.shape[2]
    turned = down.reshape(count, shallow, width // inner, inner).transpose(0, 2, 1, 3)
    return jnp.concatenate(
        [gate, up, turned.reshape(count, shallow * width // inner, inner)], axis=1
    )


def slot_codes(picks, valid, capacity):
    rows = picks.shape[0]
    ids = jnp.arange(EXPERTS, dtype=jnp.int32)
    named = jnp.any(picks[:, :, None] == ids[None, None, :], axis=1)
    counted = (named & valid[:, None]).astype(BF16)
    before = (
        lax.broadcasted_iota(jnp.int32, (rows, rows), 1)
        < lax.broadcasted_iota(jnp.int32, (rows, rows), 0)
    ).astype(BF16)
    ranks = dot(before, counted)
    kept = (counted > 0) & (ranks < capacity[None, :].astype(F32))
    return jnp.where(kept, ranks, jnp.where(named, -1.0, -2.0))


def shards(
    layer_input,
    cotangent,
    lengths,
    routes,
    capacity,
    w_query,
    key_weight,
    value_weight,
    w_output,
    w_router,
    gain_attn,
    gain_moe,
    w_gate,
    w_up,
    w_down,
):
    micro_count, tokens, width = layer_input.shape[1:]
    dp_count, owner_count = lax.axis_size("dp"), lax.axis_size("expert")
    dp_index, owner_index = lax.axis_index("dp"), lax.axis_index("expert")
    slots = tokens // 4
    owned = w_gate.shape[0]
    key_width = key_weight.shape[1]
    dp_bits = dp_count.bit_length() - 1
    owner_bits = owner_count.bit_length() - 1
    split = 2 if owned % 2 == 0 and dp_bits > 1 else 1
    local = owned // split
    pair_bit = 1 if dp_bits > 1 else 0
    dp_places = [("dp", pair_bit)] + [
        ("dp", bit) for bit in reversed(range(dp_bits)) if bit != pair_bit
    ]
    row_places = [("expert", bit) for bit in range(1, owner_bits)]
    key_places = row_places + [("expert", 0)]
    if split == 2:
        token_places = [
            row_places + [("dp", pair_bit), ("expert", 0)],
            [("dp", pair_bit)] + row_places + [("expert", 0)],
        ]
    else:
        token_places = [key_places, key_places]
    half = (dp_index >> pair_bit) & 1 if split == 2 else 0
    first_expert = owner_index * owned + half * local

    rows_owned = w_query.shape[0]

    def padded(parts):
        taken = sum(part.shape[1] for part in parts)
        return parts + [jnp.zeros((rows_owned, -taken % LANES), BF16)]

    packed = padded([w_output, w_router, gain_moe[:, None]])
    packed += padded([w_query, key_weight, value_weight, gain_attn[:, None]])
    dense = lax.all_gather(jnp.concatenate(packed, axis=1), AXES, axis=0, tiled=True)

    def packed_half(which):
        return pack_experts(
            *[
                lax.dynamic_slice_in_dim(weight, which * local, local, 0)
                for weight in (w_gate, w_up, w_down)
            ]
        )

    mine_packed = packed_half(half)
    other_packed = packed_half(1 - half) if split == 2 else mine_packed
    weight_masks = [mask["dp"] for mask in masks_of(dp_places)]
    start_row = owner_index * tokens
    places = start_row + jnp.arange(tokens, dtype=jnp.int32)
    freqs = rope_base ** (-jnp.arange(0, HEAD_DIMENSION, 2, dtype=F32) / HEAD_DIMENSION)
    angles = places.astype(F32)[:, None] * freqs[None, :]
    cos_half, sin_half = jnp.cos(angles), jnp.sin(angles)
    cos = jnp.tile(cos_half, (1, LANES // HALF_HEAD))
    sin = jnp.tile(jnp.concatenate([-sin_half, sin_half], axis=1), (1, LANES // HEAD_DIMENSION))
    cos_t, sin_t = cos_half.T, sin_half.T
    key_starts = jnp.stack(
        [(owner_index ^ mask["expert"]) * tokens for mask in masks_of(key_places)]
    )
    codes, attend_places, dys, dy_rows = [], [], [], []
    for index in range(micro_count):
        length = lengths[0, index]
        valid = places < length
        code = slot_codes(routes[0, index], valid, capacity)
        code = jnp.concatenate([code, jnp.full((tokens, LANES - EXPERTS), -2.0, F32)], axis=1)
        codes.append(code)
        attend_places.append(
            jnp.concatenate([jnp.stack([start_row, length]), key_starts]).astype(jnp.int32)
        )
        dy = jnp.where(valid[:, None], cotangent[0, index], 0)
        dys.append(dy)
        dy_rows.append(jnp.concatenate([dy, code.astype(BF16)], axis=1))

    cut = (local + 1) // 2
    rows_here = jnp.stack(dy_rows)[None]
    first_piece = swap(other_packed, dp_places[0])
    last_piece = swap(mine_packed, dp_places[-1])
    dy_received = swap(rows_here, token_places[0][0])
    own_rows, dense, rows_here, first_piece, last_piece, dy_received = after(
        mine_packed, dense, rows_here, first_piece, last_piece, dy_received
    )
    between = swap(own_rows, dp_places[1])
    rows_here = jnp.concatenate([rows_here, dy_received], axis=0)
    dy_received = swap(rows_here, token_places[0][1])
    if len(token_places[0]) > 3:
        rows_here = jnp.concatenate([rows_here, dy_received], axis=0)
        dy_received = swap(rows_here, token_places[0][2])
    forward = swap(first_piece, dp_places[-1])

    gain_one = dense[:, dense.shape[1] - LANES].astype(F32)[None]
    gain_two = dense[:, width + EXPERTS].astype(F32)[None]
    x = layer_input[0]
    normed, queries, keys_values = project(x, gain_one, dense, cos, sin)
    key_rows, attended, log_totals, middles, normed_two, gates = [], [], [], [], [], []
    row_halves = []
    for index in range(micro_count):
        halves = gather_rows(keys_values[index], key_places)
        key_rows.append(jnp.concatenate(halves, axis=0).reshape(-1, 2 * key_width))

    rows, lse = attend(attend_places[0], queries[0], key_rows[0])
    attended.append(rows)
    log_totals.append(lse)
    rows, lse = attend(attend_places[1], queries[1], key_rows[1])
    attended.append(rows)
    log_totals.append(lse)
    stage_rows = []
    for index in range(micro_count):
        middle, normed_rows, gate = middle_rows(
            x[index], attended[index], dense, gain_two, codes[index]
        )
        middles.append(middle)
        normed_two.append(normed_rows)
        gates.append(gate)
        stage_rows.append([swap(normed_rows, place) for place in token_places[index][:-1]])
    flat = [row for rows in stage_rows for row in rows]
    between, forward, first_piece, dy_received, *flat = after(
        between, forward, first_piece, dy_received, *flat
    )
    rows_here = jnp.concatenate([rows_here, dy_received], axis=0)
    stage_rows = [flat[: len(flat) // 2], flat[len(flat) // 2 :]]
    firsts = [first_piece[:cut], first_piece[cut:]]
    onward = [swap(firsts[0], dp_places[1])]
    along = swap(between, dp_places[-1])
    rows_there = swap(rows_here, token_places[0][-1])

    dy_blocks = []
    per_micro = 2 * rows_here.shape[0]
    block_count = micro_count * per_micro
    for index in range(micro_count):
        order = [token_places[0].index(place) for place in token_places[index]]
        for piece in range(per_micro):
            source = sum((piece >> stage & 1) << order[stage] for stage in range(len(order)))
            side = rows_here if source < per_micro // 2 else rows_there
            dy_blocks.append(side[source % (per_micro // 2), index])
    dy_all = jnp.stack(dy_blocks)
    code_all = dy_all[:, :, width : width + EXPERTS].astype(F32).transpose(2, 0, 1)
    code_all = jnp.roll(code_all.reshape(EXPERTS, block_count * tokens), -first_expert, axis=0)
    rank_table = code_all[:8].astype(jnp.int32)

    for index in range(micro_count):
        pieces = [normed_two[index], *stage_rows[index]]
        pieces.append(swap(pieces[1], token_places[index][1]))
        pieces = jnp.stack(pieces)
        if index == 1:
            pieces, along, onward[0], firsts[1], dy_all, rank_table = after(
                pieces, along, onward[0], firsts[1], dy_all, rank_table
            )
            onward.append(swap(firsts[1], dp_places[1]))
            across = [swap(part, dp_places[-1]) for part in onward]
        row_halves += [pieces, swap(pieces, token_places[index][-1])]
    row_all = jnp.concatenate(row_halves, axis=0)

    def expert_pieces(expert):
        return [
            (parts[0], expert)
            if len(parts) == 1
            else (parts[expert >= cut], expert - cut * (expert >= cut))
            for parts in weight_parts
        ]

    router_t = jnp.roll(dense[:, width : width + EXPERTS].T, -first_expert, axis=0)
    logits = dot_cols(router_t, row_all.reshape(block_count * tokens, width))
    chosen = code_all > -1.5
    peak = jnp.max(jnp.where(chosen, logits, masked_score), axis=0, keepdims=True)
    raised = jnp.where(chosen, jnp.exp(jnp.where(chosen, logits, peak) - peak), 0.0)
    gate_table = (raised / jnp.sum(raised, axis=0, keepdims=True))[:8]
    me = jnp.stack([dp_index, first_expert]).astype(jnp.int32)
    held = None
    groups = [
        [index for index in range(dp_count) if index >> pair_bit & 1 == side] for side in range(2)
    ]
    summed = []
    me, *across = after(me, *across)
    weight_parts = [[mine_packed], [first_piece], [between], onward, [last_piece], [forward], [along], across]
    if len(dp_places) > 3:
        more = [[mine_packed], [first_piece], [between], onward]
        for place in dp_places[2:-1]:
            more = more + [[swap(part, place) for part in parts] for parts in more]
        weight_parts = more + [[swap(part, dp_places[-1]) for part in parts] for parts in more]

    for first, end in ((0, cut), (cut, local)):
        *held, grads = run_experts(
            first, me, [expert_pieces(expert) for expert in range(first, end)], weight_masks,
            pair_bit, row_all, dy_all, rank_table, gate_table, slots, local, held,
        )
        summed.append(
            lax.psum_scatter(
                grads, "dp", scatter_dimension=0, axis_index_groups=groups, tiled=True
            )[0]
        )
    eg_all, db_all = held

    slot_place = rank_table[:local]
    slot_place = jnp.where(
        slot_place >= 0, slot_place + slots * jnp.arange(local, dtype=jnp.int32)[:, None], -1
    )
    slot_place = jnp.concatenate(
        [slot_place, jnp.full((8 - local, block_count * tokens), -1, jnp.int32)], axis=0
    )
    slot_place = slot_place.reshape(8, block_count, tokens).transpose(1, 2, 0)

    def first_trade(source, places):
        found = []
        for index in range(micro_count):
            first, size = index * per_micro, per_micro // 2
            high = combine(source, places, first + size, size)
            received = swap(high, token_places[index][-1])
            low = combine(source, places, first, size)
            half_size = size // 2
            found.append(
                [
                    add_rounded(low[:half_size], received[:half_size]),
                    add_rounded(low[half_size:], received[half_size:]),
                ]
            )
        return found

    sums = first_trade(db_all, slot_place)
    received = [
        swap(sums[index][1], token_places[index][-2]) for index in range(micro_count)
    ]
    mix_place, *lows = after(slot_place, *[pair[0] for pair in sums])
    mixed = first_trade(eg_all, mix_place)
    flat, shape = jax.tree.flatten((received, mixed))
    received, mixed = jax.tree.unflatten(shape, lax.optimization_barrier(tuple(flat)))
    row_grads = []
    for index in range(micro_count):
        total = add_rounded(lows[index], received[index])
        row_grads.append(sum_home(total[:1], total[1:], token_places[index][:1])[0])

    router_grads, middle_grads, branch_grads, head_grads, gain_two_grads = [], [], [], [], []
    for index in range(micro_count):
        dz, dy1, branch, head_grad, gain_grad = middle_back(
            row_grads[index], middles[index], dys[index], gates[index], gain_two, dense
        )
        router_grads.append(dz)
        middle_grads.append(dy1)
        branch_grads.append(branch)
        head_grads.append(head_grad)
        gain_two_grads.append(gain_grad)

    def tall(parts):
        return jnp.concatenate(parts, axis=0)

    early = weight_grads(
        [tall(attended), tall(normed_two)],
        [tall(branch_grads), tall(router_grads)],
        sum(gain_two_grads),
        width + LANES,
    )
    along_z = [("dp", bit) for bit in reversed(range(1, dp_bits))]
    along_x = [("dp", 0)] if dp_bits else []
    home_two = Homeward(early, [("expert", 0)] + along_x + row_places + along_z)
    head_grads[0], early = after(head_grads[0], early)

    query_grads, pair_grads = [], []
    for index in range(micro_count):
        if index == micro_count - 1:
            attend_places[index], query_grads[0] = after(attend_places[index], query_grads[0])
            attend_places[index] = home_two.pin(attend_places[index])
        dq, pairs = attend_back(
            attend_places[index], queries[index], key_rows[index], head_grads[index],
            attended[index], log_totals[index], cos_t, sin_t,
        )
        pairs = pairs.reshape(owner_count, tokens, pairs.shape[1])
        middle_point = owner_count // 2
        pair_grads.append(sum_home(pairs[:middle_point], pairs[middle_point:], key_places)[0])
        query_grads.append(dq)
    normed_all = normed.reshape(micro_count * tokens, width)

    pair_grads[0], summed[0] = after(pair_grads[0], summed[0])
    other = [swap(summed[0][1], dp_places[0])]
    key_grads, input_grads, gain_one_grads = [], [], []
    for index in range(micro_count):
        dx, dkv, gain_grad = project_back(
            query_grads[index], pair_grads[index], x[index], middle_grads[index], gain_one,
            dense, cos, sin,
        )
        input_grads.append(dx)
        key_grads.append(dkv)
        gain_one_grads.append(gain_grad)
    gain_one_grad = home_two.pin(sum(gain_one_grads))
    late = weight_grads(
        [normed_all, normed_all],
        [tall(query_grads), tall(key_grads)],
        gain_one_grad,
        width + 2 * key_width + LANES,
    )
    home_one = Homeward(late, [("expert", 0)] + row_places + along_x + along_z)
    other.append(swap(summed[1][1], dp_places[0]))
    home_one.received, home_two.received = after(home_one.received, home_two.received)
    home_one.join()
    home_two.join()
    home_one.received, home_two.received = after(home_one.received, home_two.received)
    home_one.join()
    home_two.join()
    highs = after(home_one.held, *[pair[1] for pair in mixed])[1:]
    mix_received = [
        swap(highs[index], token_places[index][-2]) for index in range(micro_count)
    ]
    home_one.received, *other = after(home_one.received, *other)
    home_one.join()
    home_one.received, *mix_received = after(home_one.received, *mix_received)
    home_one.join()
    mixtures = []
    for index in range(micro_count):
        total = add_rounded(mixed[index][0], mix_received[index])
        mixtures.append(sum_home(total[:1], total[1:], token_places[index][:1])[0])
    layer_output = jnp.stack(
        [
            (middles[index] + mixtures[index].astype(F32)).astype(BF16)
            for index in range(micro_count)
        ]
    )[None]

    mine = jnp.concatenate([part[0] for part in summed], axis=0).astype(F32)
    other = jnp.concatenate(other, axis=0).astype(F32)
    if split == 2:
        lower = half == 0
        mine = jnp.concatenate(
            [jnp.where(lower, mine, other), jnp.where(lower, other, mine)], axis=0
        )
    else:
        mine = mine + other
    deep = w_gate.shape[1]
    inner = w_gate.shape[2]
    grad_gate = mine[:, :deep]
    grad_up = mine[:, deep : 2 * deep]
    grad_down = (
        mine[:, 2 * deep :]
        .reshape(owned, width // inner, w_down.shape[1], inner)
        .transpose(0, 2, 1, 3)
        .reshape(w_down.shape)
    )
    late_grads = home_one.rows()
    output_grads = home_two.rows()
    return (
        layer_output,
        jnp.stack(input_grads)[None],
        late_grads[:, :width],
        late_grads[:, width : width + key_width],
        late_grads[:, width + key_width : width + 2 * key_width],
        output_grads[:, :width],
        output_grads[:, width : width + EXPERTS],
        late_grads[:, width + 2 * key_width + EXPERTS],
        output_grads[:, width + EXPERTS],
        grad_gate,
        grad_up,
        grad_down,
    )


def solution(mesh):
    return jax.shard_map(
        shards,
        mesh=mesh,
        in_specs=(
            P("dp", None, "expert", None),
            P("dp", None, "expert", None),
            P("dp", None),
            P("dp", None, "expert", None),
            P(),
            P(("dp", "expert"), None),
            P(("dp", "expert"), None),
            P(("dp", "expert"), None),
            P(("dp", "expert"), None),
            P(("dp", "expert"), None),
            P(("dp", "expert")),
            P(("dp", "expert")),
            P("expert", "dp", None),
            P("expert", "dp", None),
            P("expert", "dp", None),
        ),
        out_specs=(
            P("dp", None, "expert", None),
            P("dp", None, "expert", None),
            P(("dp", "expert"), None),
            P(("dp", "expert"), None),
            P(("dp", "expert"), None),
            P(("dp", "expert"), None),
            P(("dp", "expert"), None),
            P(("dp", "expert")),
            P(("dp", "expert")),
            P("expert", "dp", None),
            P("expert", "dp", None),
            P("expert", "dp", None),
        ),
        check_vma=False,
    )
```

```python
import functools

import jax
import jax.numpy as jnp
from jax import lax
from jax.experimental import pallas as pl
from jax.experimental.pallas import tpu as pltpu
from jax.sharding import PartitionSpec as P

QUERY_HEAD_COUNT = 24
KEY_VALUE_HEADS = 8
HEAD_DIMENSION = 64
EXPERTS = 40
TOPK = 8

epsilon = 1e-06
rope_base = 10000.0
masked_score = -1e30

F32 = jnp.float32
BF16 = jnp.bfloat16
AXES = ("dp", "expert")
HALF_HEAD = HEAD_DIMENSION // 2
GROUP = QUERY_HEAD_COUNT // KEY_VALUE_HEADS
PAIRS = KEY_VALUE_HEADS // 2
PAIR_LANES = 2 * HEAD_DIMENSION
QUERY_LANES = GROUP * PAIR_LANES
LANES = 128
BLOCKS_PER_STEP = 4


def dot(left, right):
    return jnp.dot(left, right, preferred_element_type=F32)


def dot_rows(left, right):
    return lax.dot_general(left, right, (((0,), (0,)), ((), ())), preferred_element_type=F32)


def dot_cols(left, right):
    return lax.dot_general(left, right, (((1,), (1,)), ((), ())), preferred_element_type=F32)


def add_rounded(left, right):
    return (left.astype(F32) + right.astype(F32)).astype(left.dtype)


def params(limit_mib, steps=1):
    return pltpu.CompilerParams(
        dimension_semantics=("arbitrary",) * steps, vmem_limit_bytes=limit_mib << 20
    )


def lasting(micros):
    return pl.CostEstimate(flops=int(micros * 3e7), bytes_accessed=0, transcendentals=0)


def whole_spec():
    return pl.BlockSpec(memory_space=pltpu.VMEM)


def swap(array, place):
    axis, bit = place
    dp_count, owner_count = lax.axis_size("dp"), lax.axis_size("expert")
    flip = (1 << bit) * (owner_count if axis == "dp" else 1)
    return lax.ppermute(array, AXES, [(i, i ^ flip) for i in range(dp_count * owner_count)])


def gather_pieces(array, places):
    pieces = [array]
    for place in places:
        pieces = pieces + [swap(piece, place) for piece in pieces]
    return pieces


def after(value, *others):
    return lax.optimization_barrier((value, *others))


def gather_rows(array, places):
    pieces = jnp.stack(gather_pieces(array, places[:-1]))
    return pieces, swap(pieces, places[-1])


def sum_home(low, high, places):
    for place in reversed(places):
        total = high.shape[0]
        received = swap(high, place)
        if total == 1:
            return add_rounded(low, received)
        low, high = (
            add_rounded(low[: total // 2], received[: total // 2]),
            add_rounded(low[total // 2 :], received[total // 2 :]),
        )
    return low


def without_bit(index, bit):
    return ((index >> (bit + 1)) << bit) | (index & ((1 << bit) - 1))


class Homeward:
    def __init__(self, grads, places):
        bits = lax.axis_size("dp").bit_length() + lax.axis_size("expert").bit_length() - 2
        self.held = grads.reshape((2,) * bits + (grads.shape[0] >> bits, grads.shape[1]))
        self.ranks = list(reversed(range(bits)))
        self.places = list(places)
        self.start()

    def start(self):
        axis, bit = self.places[0]
        owner_bits = lax.axis_size("expert").bit_length() - 1
        depth = self.ranks.index(bit + (owner_bits if axis == "dp" else 0))
        self.ranks.pop(depth)
        upper = (lax.axis_index(axis) >> bit) & 1
        away = lax.dynamic_index_in_dim(self.held, 1 - upper, depth, False)
        self.held = lax.dynamic_index_in_dim(self.held, upper, depth, False)
        self.received = swap(away, self.places.pop(0))

    def join(self):
        self.held = add_rounded(self.held, self.received)
        if self.places:
            self.start()
        else:
            self.received = None

    def pin(self, value):
        value, self.received = after(value, self.received)
        self.join()
        return value

    def rows(self):
        while self.received is not None:
            self.join()
        return self.held.astype(F32)


def masks_of(places):
    found = []
    for piece in range(1 << len(places)):
        mask = {"dp": 0, "expert": 0}
        for stage, (axis, bit) in enumerate(places):
            if piece >> stage & 1:
                mask[axis] |= 1 << bit
        found.append(mask)
    return found


def half_swap(rows):
    lane = lax.broadcasted_iota(jnp.int32, rows.shape, 1)
    return jnp.where(
        lane % HEAD_DIMENSION < HALF_HEAD,
        pltpu.roll(rows, rows.shape[1] - HALF_HEAD, 1),
        pltpu.roll(rows, HALF_HEAD, 1),
    )


def project_kernel(x_ref, gain_ref, w_ref, cos_ref, sin_ref, h_ref, q_ref, kv_ref):
    x = x_ref[0].astype(F32)
    scale = lax.rsqrt(jnp.mean(x * x, axis=1, keepdims=True) + epsilon)
    h_ref[0] = (x * scale * gain_ref[...]).astype(BF16)
    cos, sin = cos_ref[...], sin_ref[...]
    width = q_ref.shape[2]
    key_width = kv_ref.shape[2] // 2

    def turn_into(out_ref, start, rows):
        for tile in range(0, rows.shape[1], LANES):
            part = rows[:, tile : tile + LANES]
            out_ref[0, :, start + tile : start + tile + LANES] = (
                part * cos + half_swap(part) * sin
            ).astype(BF16)

    first = width + LANES
    for start in range(0, width, key_width):
        turn_into(q_ref, start, dot(h_ref[0], w_ref[:, first + start : first + start + key_width]))
    first = first + width
    turn_into(kv_ref, 0, dot(h_ref[0], w_ref[:, first : first + key_width]))
    value = dot(h_ref[0], w_ref[:, first + key_width : first + 2 * key_width])
    kv_ref[0, :, key_width:] = value.astype(BF16)


def project(x, gain, dense, cos, sin):
    count, rows, width = x.shape
    key_width = KEY_VALUE_HEADS * HEAD_DIMENSION
    row_spec = pl.BlockSpec((1, rows, width), lambda i: (i, 0, 0))
    return pl.pallas_call(
        project_kernel,
        grid=(count,),
        in_specs=[
            row_spec,
            pl.BlockSpec((1, width), lambda i: (0, 0)),
            pl.BlockSpec(dense.shape, lambda i: (0, 0), pipeline_mode=pl.Buffered(1)),
            pl.BlockSpec((rows, LANES), lambda i: (0, 0)),
            pl.BlockSpec((rows, LANES), lambda i: (0, 0)),
        ],
        out_specs=[
            row_spec,
            row_spec,
            pl.BlockSpec((1, rows, 2 * key_width), lambda i: (i, 0, 0)),
        ],
        out_shape=[
            jax.ShapeDtypeStruct(x.shape, BF16),
            jax.ShapeDtypeStruct(x.shape, BF16),
            jax.ShapeDtypeStruct((count, rows, 2 * key_width), BF16),
        ],
        cost_estimate=lasting(8),
        compiler_params=params(48),
    )(x, gain, dense, cos, sin)


def middle_kernel(x_ref, o_ref, wo_ref, wr_ref, gain_ref, code_ref, y_ref, h_ref, g_ref):
    middle = x_ref[...].astype(F32) + dot(o_ref[...], wo_ref[...])
    y_ref[...] = middle
    scale = lax.rsqrt(jnp.mean(middle * middle, axis=1, keepdims=True) + epsilon)
    normed = (middle * scale * gain_ref[...]).astype(BF16)
    h_ref[...] = normed
    logits = dot(normed, wr_ref[...])
    chosen = code_ref[...] > -1.5
    peak = jnp.max(jnp.where(chosen, logits, masked_score), axis=1, keepdims=True)
    raised = jnp.where(chosen, jnp.exp(jnp.where(chosen, logits, peak) - peak), 0.0)
    g_ref[...] = raised / jnp.sum(raised, axis=1, keepdims=True)


def middle_rows(x, attended, dense, gain, code):
    rows, width = x.shape
    full = pl.BlockSpec((rows, width), lambda i: (0, 0))
    return pl.pallas_call(
        middle_kernel,
        grid=(1,),
        in_specs=[
            full,
            full,
            pl.BlockSpec((width, width), lambda i: (0, 0)),
            pl.BlockSpec((width, LANES), lambda i: (0, width // LANES)),
            pl.BlockSpec((1, width), lambda i: (0, 0)),
            pl.BlockSpec((rows, LANES), lambda i: (0, 0)),
        ],
        out_specs=[full, full, pl.BlockSpec((rows, LANES), lambda i: (0, 0))],
        out_shape=[
            jax.ShapeDtypeStruct((rows, width), F32),
            jax.ShapeDtypeStruct((rows, width), BF16),
            jax.ShapeDtypeStruct((rows, LANES), F32),
        ],
        cost_estimate=lasting(4.5),
        compiler_params=params(48),
    )(x, attended, dense, dense, gain, code)


def middle_back_kernel(
    acc_ref, y_ref, dy_ref, g_ref, dg_ref, gain_ref, wr_ref, wo_ref,
    dz_ref, dy1_ref, dr_ref, do_ref, dgain_ref,
):
    gates, gate_grads = g_ref[...], dg_ref[...].astype(F32)
    mean = jnp.sum(gates * gate_grads, axis=1, keepdims=True)
    dz = (gates * (gate_grads - mean)).astype(BF16)
    dz_ref[...] = dz
    dh = acc_ref[...].astype(F32) + dot_cols(dz, wr_ref[...])
    middle = y_ref[...]
    scale = lax.rsqrt(jnp.mean(middle * middle, axis=1, keepdims=True) + epsilon)
    dgain_ref[...] = jnp.sum(dh * middle * scale, axis=0, keepdims=True)
    scaled = dh * gain_ref[...]
    along = jnp.mean(scaled * middle, axis=1, keepdims=True)
    dy1 = dy_ref[...].astype(F32) + scale * scaled - middle * (scale * scale * scale * along)
    dy1_ref[...] = dy1
    rounded = dy1.astype(BF16)
    dr_ref[...] = rounded
    do_ref[...] = dot_cols(rounded, wo_ref[...]).astype(BF16)


def middle_back(acc, middle, dy, gates, gain, dense):
    rows, width = middle.shape
    full = pl.BlockSpec((rows, width), lambda i: (0, 0))
    lane = pl.BlockSpec((rows, LANES), lambda i: (0, 0))
    line = pl.BlockSpec((1, width), lambda i: (0, 0))
    return pl.pallas_call(
        middle_back_kernel,
        grid=(1,),
        in_specs=[
            full, full, full, lane,
            pl.BlockSpec((rows, LANES), lambda i: (0, width // LANES)),
            line,
            pl.BlockSpec((width, LANES), lambda i: (0, width // LANES)),
            pl.BlockSpec((width, width), lambda i: (0, 0)),
        ],
        out_specs=[lane, full, full, full, line],
        out_shape=[
            jax.ShapeDtypeStruct((rows, LANES), BF16),
            jax.ShapeDtypeStruct((rows, width), F32),
            jax.ShapeDtypeStruct((rows, width), BF16),
            jax.ShapeDtypeStruct((rows, width), BF16),
            jax.ShapeDtypeStruct((1, width), F32),
        ],
        cost_estimate=lasting(6.6),
        compiler_params=params(56),
    )(acc, middle, dy, gates, acc, gain, dense, dense)


def project_back_kernel(
    dq_ref, pairs_ref, x_ref, dy1_ref, gain_ref, w_ref, cos_ref, sin_ref,
    dx_ref, dkv_ref, dgain_ref,
):
    cos, sin = cos_ref[...], sin_ref[...]
    width = x_ref.shape[1]
    key_width = dkv_ref.shape[1] // 2
    for pair in range(PAIRS):
        lanes = slice(pair * LANES, (pair + 1) * LANES)
        start = 2 * pair * LANES
        part = pairs_ref[:, start : start + LANES].astype(F32)
        dkv_ref[:, lanes] = (part * cos - half_swap(part) * sin).astype(BF16)
        lanes = slice(key_width + pair * LANES, key_width + (pair + 1) * LANES)
        dkv_ref[:, lanes] = pairs_ref[:, start + LANES : start + 2 * LANES]
    first = width + LANES
    dh = dot_cols(dq_ref[...], w_ref[:, first : first + width])
    first = first + width
    dh = dh + dot_cols(dkv_ref[...], w_ref[:, first : first + 2 * key_width])
    x = x_ref[...].astype(F32)
    scale = lax.rsqrt(jnp.mean(x * x, axis=1, keepdims=True) + epsilon)
    dgain_ref[...] = jnp.sum(dh * x * scale, axis=0, keepdims=True)
    scaled = dh * gain_ref[...]
    along = jnp.mean(scaled * x, axis=1, keepdims=True)
    dx_ref[...] = dy1_ref[...] + scale * scaled - x * (scale * scale * scale * along)


def project_back(dq, pairs, x, dy1, gain, dense, cos, sin):
    rows, width = x.shape
    key_width = pairs.shape[1] // 2
    full = pl.BlockSpec((rows, width), lambda i: (0, 0))
    lane = pl.BlockSpec((rows, LANES), lambda i: (0, 0))
    line = pl.BlockSpec((1, width), lambda i: (0, 0))
    both = pl.BlockSpec((rows, 2 * key_width), lambda i: (0, 0))
    return pl.pallas_call(
        project_back_kernel,
        grid=(1,),
        in_specs=[
            full, both, full, full, line,
            pl.BlockSpec(dense.shape, lambda i: (0, 0), pipeline_mode=pl.Buffered(1)),
            lane, lane,
        ],
        out_specs=[full, both, line],
        out_shape=[
            jax.ShapeDtypeStruct((rows, width), F32),
            jax.ShapeDtypeStruct((rows, 2 * key_width), BF16),
            jax.ShapeDtypeStruct((1, width), F32),
        ],
        cost_estimate=lasting(8.2),
        compiler_params=params(56),
    )(dq, pairs, x, dy1, gain, dense, cos, sin)


def weight_grad_kernel(count, *refs):
    left_refs, right_refs, out_ref = refs[:count], refs[count : 2 * count], refs[-1]
    rows, columns = out_ref.shape
    if len(refs) > 2 * count + 1:
        gain = jnp.broadcast_to(refs[2 * count][...], (8, rows)).T
    lane = lax.broadcasted_iota(jnp.int32, (rows, LANES), 1)
    start = 0
    for left_ref, right_ref in zip(left_refs, right_refs):
        left = left_ref[...].T
        width = right_ref.shape[1]
        step = min(width, 4 * LANES)
        for tile in range(0, width, step):
            part = dot(left, right_ref[:, tile : tile + step])
            if start + tile + step == columns and len(refs) > 2 * count + 1:
                edge = part[:, step - LANES :]
                edge = jnp.where(lane == EXPERTS, gain[:, 0:1], edge)
                out_ref[:, columns - LANES :] = edge.astype(BF16)
                part = part[:, : step - LANES]
            if part.shape[1]:
                out_ref[:, start + tile : start + tile + part.shape[1]] = part.astype(BF16)
        start += width
    if start < columns:
        out_ref[:, start:] = jnp.where(lane == EXPERTS, gain[:, 0:1], 0.0).astype(BF16)


def weight_grads(lefts, rights, gain, columns):
    rows = lefts[0].shape[1]
    operands = [*lefts, *rights] + ([] if gain is None else [gain])
    return pl.pallas_call(
        functools.partial(weight_grad_kernel, len(lefts)),
        in_specs=[whole_spec() for _ in operands],
        out_specs=whole_spec(),
        out_shape=jax.ShapeDtypeStruct((rows, columns), BF16),
        cost_estimate=lasting(9),
        compiler_params=pltpu.CompilerParams(vmem_limit_bytes=56 << 20),
    )(*operands)


def fill_bias(places_ref, bias_ref, rows):
    query = places_ref[0] + lax.broadcasted_iota(jnp.int32, (rows, rows), 1)
    inside = lax.broadcasted_iota(jnp.int32, (rows, rows), 0)
    for block in range(bias_ref.shape[0] // rows):
        key = places_ref[2 + block] + inside
        allowed = (key <= query) & (key < places_ref[1])
        bias_ref[block * rows : (block + 1) * rows, :] = jnp.where(allowed, 0.0, masked_score)


def attend_kernel(places_ref, q_ref, k_ref, v_ref, o_ref, lse_ref, bias_ref):
    rows = q_ref.shape[0]

    @pl.when(pl.program_id(0) == 0)
    def _():
        fill_bias(places_ref, bias_ref, rows)

    outs = []
    for side in range(2):
        lanes = slice(side * HEAD_DIMENSION, (side + 1) * HEAD_DIMENSION)
        key = k_ref[:, lanes]
        value_t = v_ref[:, lanes].T
        for member in range(GROUP):
            head = side * GROUP + member
            query = q_ref[:, head * HEAD_DIMENSION : (head + 1) * HEAD_DIMENSION]
            scores = dot_cols(key, query * HEAD_DIMENSION**-0.5) + bias_ref[...]
            peak = jnp.max(scores, axis=0, keepdims=True)
            raised = jnp.exp(scores - peak)
            total = jnp.sum(raised, axis=0, keepdims=True)
            outs.append(dot(value_t, raised.astype(BF16)) / total)
            lse_ref[0, head : head + 1, :] = peak + jnp.log(total)
    o_ref[...] = jnp.concatenate(outs, axis=0).T.astype(BF16)


def attend(places, q, kv):
    rows, width = q.shape
    keys = kv.shape[0]
    return pl.pallas_call(
        attend_kernel,
        grid_spec=pltpu.PrefetchScalarGridSpec(
            num_scalar_prefetch=1,
            grid=(PAIRS,),
            in_specs=[
                pl.BlockSpec((rows, QUERY_LANES), lambda i, s: (0, i)),
                pl.BlockSpec((keys, PAIR_LANES), lambda i, s: (0, i)),
                pl.BlockSpec((keys, PAIR_LANES), lambda i, s: (0, PAIRS + i)),
            ],
            out_specs=[
                pl.BlockSpec((rows, QUERY_LANES), lambda i, s: (0, i)),
                pl.BlockSpec((1, 8, rows), lambda i, s: (i, 0, 0)),
            ],
            scratch_shapes=[pltpu.VMEM((keys, rows), F32)],
        ),
        out_shape=[
            jax.ShapeDtypeStruct((rows, width), BF16),
            jax.ShapeDtypeStruct((PAIRS, 8, rows), F32),
        ],
        cost_estimate=lasting(19),
        compiler_params=params(48),
    )(places, q, kv, kv)


def attend_back_kernel(
    places_ref, q_ref, k_ref, v_ref, do_ref, o_ref, lse_ref, cos_ref, sin_ref,
    dq_ref, dkv_ref, bias_ref,
):
    rows = q_ref.shape[0]

    @pl.when(pl.program_id(0) == 0)
    def _():
        fill_bias(places_ref, bias_ref, rows)

    score_scale = HEAD_DIMENSION**-0.5
    cos, sin = cos_ref[...], sin_ref[...]
    ones = jnp.ones((8, HEAD_DIMENSION), F32)
    query_grads = []
    for side in range(2):
        lanes = slice(side * HEAD_DIMENSION, (side + 1) * HEAD_DIMENSION)
        key, value = k_ref[:, lanes], v_ref[:, lanes]
        key_t = key.T
        key_grad = None
        value_grad = None
        for member in range(GROUP):
            head = side * GROUP + member
            columns = slice(head * HEAD_DIMENSION, (head + 1) * HEAD_DIMENSION)
            query = q_ref[:, columns] * score_scale
            grad = do_ref[:, columns]
            overlap = grad.astype(F32) * o_ref[:, columns].astype(F32)
            along = lax.dot_general(
                ones, overlap, (((1,), (1,)), ((), ())),
                precision=lax.Precision.HIGHEST, preferred_element_type=F32,
            )[0:1]
            scores = dot_cols(key, query) + bias_ref[...]
            probs = jnp.exp(scores - lse_ref[0, head : head + 1, :])
            score_grad = (probs * (dot_cols(value, grad) - along)).astype(BF16)
            value_part = dot(probs.astype(BF16), grad)
            key_part = dot(score_grad, query)
            value_grad = value_part if value_grad is None else value_grad + value_part
            key_grad = key_part if key_grad is None else key_grad + key_part
            turned = dot(key_t, score_grad) * score_scale
            upper, lower = turned[:HALF_HEAD], turned[HALF_HEAD:]
            query_grads += [upper * cos + lower * sin, lower * cos - upper * sin]
        dkv_ref[:, lanes] = key_grad.astype(BF16)
        shifted = slice(LANES + side * HEAD_DIMENSION, LANES + (side + 1) * HEAD_DIMENSION)
        dkv_ref[:, shifted] = value_grad.astype(BF16)
    dq_ref[...] = jnp.concatenate(query_grads, axis=0).T.astype(BF16)


def attend_back(places, q, kv, grad, attended, lse, cos_t, sin_t):
    rows, width = q.shape
    keys = kv.shape[0]
    key_width = kv.shape[1] // 2
    wide = pl.BlockSpec((rows, QUERY_LANES), lambda i, s: (0, i))
    tall = pl.BlockSpec((keys, PAIR_LANES), lambda i, s: (0, i))
    table = pl.BlockSpec((HALF_HEAD, rows), lambda i, s: (0, 0))
    return pl.pallas_call(
        attend_back_kernel,
        grid_spec=pltpu.PrefetchScalarGridSpec(
            num_scalar_prefetch=1,
            grid=(PAIRS,),
            in_specs=[
                wide,
                tall,
                pl.BlockSpec((keys, PAIR_LANES), lambda i, s: (0, PAIRS + i)),
                wide,
                wide,
                pl.BlockSpec((1, 8, rows), lambda i, s: (i, 0, 0)),
                table,
                table,
            ],
            out_specs=[wide, pl.BlockSpec((keys, 2 * PAIR_LANES), lambda i, s: (0, i))],
            scratch_shapes=[pltpu.VMEM((keys, rows), F32)],
        ),
        out_shape=[
            jax.ShapeDtypeStruct((rows, width), BF16),
            jax.ShapeDtypeStruct((keys, 2 * key_width), BF16),
        ],
        cost_estimate=lasting(23.5),
        compiler_params=params(56),
    )(places, q, kv, kv, grad, attended, lse, cos_t, sin_t)


def expert_kernel(masks, sources, pair_bit, first, aliased, me_ref, *refs):
    count = len(masks)
    arrays = 1 + max(array for per_expert in sources for array, _ in per_expert)
    pieces, refs = refs[:arrays], refs[arrays:]
    h_ref, dy_ref, rank_ref, gate_ref = refs[:4]
    refs = refs[4 + (2 if aliased else 0) :]
    eg_ref, db_ref = refs[:2]
    out_ref, refs = refs[2], refs[3:]
    w_in, w_down, g_in, g_down, rows_all, de_all, hidden_all, dau_all, in_sem, out_sem = refs
    member, step = pl.program_id(0), pl.program_id(1)
    expert = first + member
    side = lax.rem(member, 2)
    blocks, tokens, width = h_ref.shape
    slots = eg_ref.shape[2]
    chunk = blocks * slots
    inner = w_down.shape[1]
    deep = width // count
    shallow = inner // count
    wide = width // inner
    me = me_ref[0]

    def windows(piece_ref, shard, into, down):
        top = pl.ds(pl.multiple_of(shard * deep, 16), deep)
        low = pl.ds(pl.multiple_of(shard * shallow, 16), shallow)
        pairs = [
            (piece_ref.at[pl.ds(0, deep)], into.at[top, pl.ds(0, inner)]),
            (piece_ref.at[pl.ds(deep, deep)], into.at[top, pl.ds(inner, inner)]),
        ]
        for part in range(wide):
            pairs.append(
                (
                    piece_ref.at[pl.ds(2 * deep + part * shallow, shallow)],
                    down.at[low, pl.ds(part * inner, inner)],
                )
            )
        return pairs

    def loads(which):
        made = []
        into, down, sems = w_in.at[which % 2], w_down.at[which % 2], in_sem.at[which % 2]
        for (array, index), mask in zip(sources[which], masks):
            for source, target in windows(pieces[array].at[index], me ^ mask, into, down):
                made.append(pltpu.make_async_copy(source, target, sems.at[len(made)]))
        return made

    def stores(which):
        made = []
        for piece, mask in enumerate(masks):
            target = out_ref.at[without_bit(me ^ mask, pair_bit), piece & 1, which]
            for there, here in windows(target, me ^ mask, g_in, g_down):
                made.append(pltpu.make_async_copy(here, there, out_sem.at[len(made)]))
        return made

    for which in range(len(sources)):
        early = (member == 0) & (step == 0) if which == 0 else (member == which - 1) & (step == 1)

        @pl.when(early)
        def _(which=which):
            for copy in loads(which):
                copy.start()

    slot = lax.broadcasted_iota(jnp.int32, (slots, tokens), 0)
    grads = []
    weights = []
    for block in range(blocks):
        start = pl.multiple_of((step * blocks + block) * tokens, LANES)
        hit = slot == rank_ref[expert, :, pl.ds(start, tokens)]
        select = jnp.where(hit, 1.0, 0.0).astype(BF16)
        place = pl.ds(pl.multiple_of(step * chunk + block * slots, 16), slots)
        rows_all[place, :] = dot(select, h_ref[block]).astype(BF16)
        grads.append(dot(select, dy_ref[block]))
        gate = gate_ref[expert, :, pl.ds(start, tokens)]
        weights.append(jnp.sum(jnp.where(hit, gate, 0.0), axis=1, keepdims=True))

    for which in range(len(sources)):

        @pl.when((member == which) & (step == 0))
        def _(which=which):
            for copy in loads(which):
                copy.wait()

    here = pl.ds(pl.multiple_of(step * chunk, 16), chunk)
    grad_rows = jnp.concatenate(grads, axis=0)
    weight = jnp.concatenate(weights, axis=0)
    pre = dot(rows_all[here, :], w_in[side])
    gate_pre, up_pre = pre[:, :inner], pre[:, inner:]
    sigmoid = 1.0 / (1.0 + jnp.exp(-gate_pre))
    silu = gate_pre * sigmoid
    hidden = (silu * up_pre).astype(BF16)
    hidden_all[here, :] = hidden
    out = dot(hidden, w_down[side]).astype(BF16).astype(F32)
    row_grad = jnp.sum(grad_rows * out, axis=1, keepdims=True)
    out = (weight * out).astype(BF16)
    lane = lax.broadcasted_iota(jnp.int32, (slots, LANES), 1)
    for block in range(blocks):
        part = slice(block * slots, (block + 1) * slots)
        eg_ref[block, 0] = out[part]
        db_ref[block, 0, :, width:] = jnp.where(lane == me_ref[1] + expert, row_grad[part], 0.0).astype(
            BF16
        )
    de = (weight * grad_rows).astype(BF16)
    de_all[here, :] = de
    grad_hidden = dot_cols(de, w_down[side])
    grad_up = (grad_hidden * silu).astype(BF16)
    grad_gate = (
        grad_hidden * up_pre * sigmoid * (1.0 + gate_pre * (1.0 - sigmoid))
    ).astype(BF16)
    dau_all[here, :inner] = grad_gate
    dau_all[here, inner:] = grad_up
    back = dot_cols(dau_all[here, :], w_in[side]).astype(BF16)
    for block in range(blocks):
        db_ref[block, 0, :, :width] = back[block * slots : (block + 1) * slots]

    last = step == pl.num_programs(1) - 1
    for which in range(1, len(sources)):

        @pl.when(last & (member == which))
        def _(which=which):
            for copy in stores(which - 1):
                copy.wait()

    @pl.when(last)
    def _():
        for part in range(wide):
            lanes = slice(part * inner, (part + 1) * inner)
            g_in[lanes, :] = dot_rows(rows_all[:, lanes], dau_all[...]).astype(BF16)
        g_down[...] = dot_rows(hidden_all[...], de_all[...]).astype(BF16)

    for which in range(len(sources)):

        @pl.when(last & (member == which))
        def _(which=which):
            for copy in stores(which):
                copy.start()
            if which == len(sources) - 1:
                for copy in stores(which):
                    copy.wait()


def run_experts(first, me, pieces, masks, pair_bit, h_all, dy_all, ranks, gates, slots, local, earlier):
    block_count, tokens, width = h_all.shape
    members = len(pieces)
    arrays = []
    sources = []
    for per_expert in pieces:
        found = []
        for array, index in per_expert:
            known = [place for place, other in enumerate(arrays) if other is array]
            if not known:
                known = [len(arrays)]
                arrays.append(array)
            found.append((known[0], index))
        sources.append(found)
    piece_rows, inner = arrays[0].shape[1:]
    count = len(masks)
    steps = block_count // BLOCKS_PER_STEP
    rows = block_count * slots
    block_spec = pl.BlockSpec((BLOCKS_PER_STEP, tokens, width), lambda g, i, s: (i, 0, 0))
    any_spec = pl.BlockSpec(memory_space=pl.ANY)
    table = pl.BlockSpec((ranks.shape[0], 1, ranks.shape[1]), lambda g, i, s: (0, 0, 0))
    widths = (width, width + LANES)
    copies = count * (2 + width // inner)
    extra = [] if earlier is None else list(earlier)
    start = 1 + len(arrays) + 4
    aliases = {start + place: place for place in range(len(extra))}
    return pl.pallas_call(
        functools.partial(expert_kernel, masks, sources, pair_bit, first, earlier is not None),
        grid_spec=pltpu.PrefetchScalarGridSpec(
            num_scalar_prefetch=1,
            grid=(members, steps),
            in_specs=[any_spec] * len(arrays)
            + [block_spec, block_spec, table, table]
            + [any_spec] * len(extra),
            out_specs=[
                pl.BlockSpec(
                    (BLOCKS_PER_STEP, 1, slots, w), lambda g, i, s: (i, first + g, 0, 0)
                )
                for w in widths
            ]
            + [any_spec],
            scratch_shapes=[
                pltpu.VMEM((2, width, 2 * inner), BF16),
                pltpu.VMEM((2, inner, width), BF16),
                pltpu.VMEM((width, 2 * inner), BF16),
                pltpu.VMEM((inner, width), BF16),
                pltpu.VMEM((rows, width), BF16),
                pltpu.VMEM((rows, width), BF16),
                pltpu.VMEM((rows, inner), BF16),
                pltpu.VMEM((rows, 2 * inner), BF16),
                pltpu.SemaphoreType.DMA((2, copies)),
                pltpu.SemaphoreType.DMA((copies,)),
            ],
        ),
        out_shape=[jax.ShapeDtypeStruct((block_count, local, slots, w), BF16) for w in widths]
        + [jax.ShapeDtypeStruct((count // 2, 2, members, piece_rows, inner), BF16)],
        input_output_aliases=aliases,
        cost_estimate=lasting(31 * members),
        compiler_params=params(60, 2),
    )(me, *arrays, h_all, dy_all, ranks[:, None], gates[:, None], *extra)


def combine_kernel(src_ref, place_ref, out_ref):
    _, local, slots, width = src_ref.shape
    tokens = out_ref.shape[1]
    lane = lax.broadcasted_iota(jnp.int32, (tokens, local * slots), 1)
    hit = lane == place_ref[0, :, 0:1]
    for expert in range(1, local):
        hit = hit | (lane == place_ref[0, :, expert : expert + 1])
    source = src_ref[0].reshape(local * slots, width)
    out_ref[0] = dot(jnp.where(hit, 1.0, 0.0).astype(BF16), source).astype(BF16)


def combine(source, places, first, size):
    _, local, slots, width = source.shape
    tokens = places.shape[1]
    return pl.pallas_call(
        combine_kernel,
        grid=(size,),
        in_specs=[
            pl.BlockSpec((1, local, slots, width), lambda i: (first + i, 0, 0, 0)),
            pl.BlockSpec((1, tokens, places.shape[2]), lambda i: (first + i, 0, 0)),
        ],
        out_specs=pl.BlockSpec((1, tokens, width), lambda i: (i, 0, 0)),
        out_shape=jax.ShapeDtypeStruct((size, tokens, width), BF16),
        cost_estimate=lasting(4.4),
        compiler_params=params(60),
    )(source, places)


def pack_experts(gate, up, down):
    count, shallow, width = down.shape
    inner = gate.shape[2]
    turned = down.reshape(count, shallow, width // inner, inner).transpose(0, 2, 1, 3)
    return jnp.concatenate(
        [gate, up, turned.reshape(count, shallow * width // inner, inner)], axis=1
    )


def slot_codes(picks, valid, capacity):
    rows = picks.shape[0]
    ids = jnp.arange(EXPERTS, dtype=jnp.int32)
    named = jnp.any(picks[:, :, None] == ids[None, None, :], axis=1)
    counted = (named & valid[:, None]).astype(BF16)
    before = (
        lax.broadcasted_iota(jnp.int32, (rows, rows), 1)
        < lax.broadcasted_iota(jnp.int32, (rows, rows), 0)
    ).astype(BF16)
    ranks = dot(before, counted)
    kept = (counted > 0) & (ranks < capacity[None, :].astype(F32))
    return jnp.where(kept, ranks, jnp.where(named, -1.0, -2.0))


def shards(
    layer_input,
    cotangent,
    lengths,
    routes,
    capacity,
    w_query,
    key_weight,
    value_weight,
    w_output,
    w_router,
    gain_attn,
    gain_moe,
    w_gate,
    w_up,
    w_down,
):
    micro_count, tokens, width = layer_input.shape[1:]
    dp_count, owner_count = lax.axis_size("dp"), lax.axis_size("expert")
    dp_index, owner_index = lax.axis_index("dp"), lax.axis_index("expert")
    slots = tokens // 4
    owned = w_gate.shape[0]
    key_width = key_weight.shape[1]
    dp_bits = dp_count.bit_length() - 1
    owner_bits = owner_count.bit_length() - 1
    split = 2 if owned % 2 == 0 and dp_bits > 1 else 1
    local = owned // split
    pair_bit = 1 if dp_bits > 1 else 0
    dp_places = [("dp", pair_bit)] + [
        ("dp", bit) for bit in reversed(range(dp_bits)) if bit != pair_bit
    ]
    row_places = [("expert", bit) for bit in range(1, owner_bits)]
    key_places = row_places + [("expert", 0)]
    if split == 2:
        token_places = [
            row_places + [("dp", pair_bit), ("expert", 0)],
            [("dp", pair_bit)] + row_places + [("expert", 0)],
        ]
    else:
        token_places = [key_places, key_places]
    half = (dp_index >> pair_bit) & 1 if split == 2 else 0
    first_expert = owner_index * owned + half * local

    rows_owned = w_query.shape[0]

    def padded(parts):
        taken = sum(part.shape[1] for part in parts)
        return parts + [jnp.zeros((rows_owned, -taken % LANES), BF16)]

    packed = padded([w_output, w_router, gain_moe[:, None]])
    packed += padded([w_query, key_weight, value_weight, gain_attn[:, None]])
    dense = lax.all_gather(jnp.concatenate(packed, axis=1), AXES, axis=0, tiled=True)

    def packed_half(which):
        return pack_experts(
            *[
                lax.dynamic_slice_in_dim(weight, which * local, local, 0)
                for weight in (w_gate, w_up, w_down)
            ]
        )

    mine_packed = packed_half(half)
    other_packed = packed_half(1 - half) if split == 2 else mine_packed
    weight_masks = [mask["dp"] for mask in masks_of(dp_places)]
    start_row = owner_index * tokens
    places = start_row + jnp.arange(tokens, dtype=jnp.int32)
    freqs = rope_base ** (-jnp.arange(0, HEAD_DIMENSION, 2, dtype=F32) / HEAD_DIMENSION)
    angles = places.astype(F32)[:, None] * freqs[None, :]
    cos_half, sin_half = jnp.cos(angles), jnp.sin(angles)
    cos = jnp.tile(cos_half, (1, LANES // HALF_HEAD))
    sin = jnp.tile(jnp.concatenate([-sin_half, sin_half], axis=1), (1, LANES // HEAD_DIMENSION))
    cos_t, sin_t = cos_half.T, sin_half.T
    key_starts = jnp.stack(
        [(owner_index ^ mask["expert"]) * tokens for mask in masks_of(key_places)]
    )
    codes, attend_places, dys, dy_rows = [], [], [], []
    for index in range(micro_count):
        length = lengths[0, index]
        valid = places < length
        code = slot_codes(routes[0, index], valid, capacity)
        code = jnp.concatenate([code, jnp.full((tokens, LANES - EXPERTS), -2.0, F32)], axis=1)
        codes.append(code)
        attend_places.append(
            jnp.concatenate([jnp.stack([start_row, length]), key_starts]).astype(jnp.int32)
        )
        dy = jnp.where(valid[:, None], cotangent[0, index], 0)
        dys.append(dy)
        dy_rows.append(jnp.concatenate([dy, code.astype(BF16)], axis=1))

    cut = (local + 1) // 2
    rows_here = jnp.stack(dy_rows)[None]
    first_piece = swap(other_packed, dp_places[0])
    last_piece = swap(mine_packed, dp_places[-1])
    dy_received = swap(rows_here, token_places[0][0])
    own_rows, dense, rows_here, first_piece, last_piece, dy_received = after(
        mine_packed, dense, rows_here, first_piece, last_piece, dy_received
    )
    between = swap(own_rows, dp_places[1])
    rows_here = jnp.concatenate([rows_here, dy_received], axis=0)
    dy_received = swap(rows_here, token_places[0][1])
    if len(token_places[0]) > 3:
        rows_here = jnp.concatenate([rows_here, dy_received], axis=0)
        dy_received = swap(rows_here, token_places[0][2])
    forward = swap(first_piece, dp_places[-1])

    gain_one = dense[:, dense.shape[1] - LANES].astype(F32)[None]
    gain_two = dense[:, width + EXPERTS].astype(F32)[None]
    x = layer_input[0]
    normed, queries, keys_values = project(x, gain_one, dense, cos, sin)
    key_rows, attended, log_totals, middles, normed_two, gates = [], [], [], [], [], []
    row_halves = []
    for index in range(micro_count):
        halves = gather_rows(keys_values[index], key_places)
        key_rows.append(jnp.concatenate(halves, axis=0).reshape(-1, 2 * key_width))

    rows, lse = attend(attend_places[0], queries[0], key_rows[0])
    attended.append(rows)
    log_totals.append(lse)
    rows, lse = attend(attend_places[1], queries[1], key_rows[1])
    attended.append(rows)
    log_totals.append(lse)
    stage_rows = []
    for index in range(micro_count):
        middle, normed_rows, gate = middle_rows(
            x[index], attended[index], dense, gain_two, codes[index]
        )
        middles.append(middle)
        normed_two.append(normed_rows)
        gates.append(gate)
        stage_rows.append([swap(normed_rows, place) for place in token_places[index][:-1]])
    flat = [row for rows in stage_rows for row in rows]
    between, forward, first_piece, dy_received, *flat = after(
        between, forward, first_piece, dy_received, *flat
    )
    rows_here = jnp.concatenate([rows_here, dy_received], axis=0)
    stage_rows = [flat[: len(flat) // 2], flat[len(flat) // 2 :]]
    firsts = [first_piece[:cut], first_piece[cut:]]
    onward = [swap(firsts[0], dp_places[1])]
    along = swap(between, dp_places[-1])
    rows_there = swap(rows_here, token_places[0][-1])

    dy_blocks = []
    per_micro = 2 * rows_here.shape[0]
    block_count = micro_count * per_micro
    for index in range(micro_count):
        order = [token_places[0].index(place) for place in token_places[index]]
        for piece in range(per_micro):
            source = sum((piece >> stage & 1) << order[stage] for stage in range(len(order)))
            side = rows_here if source < per_micro // 2 else rows_there
            dy_blocks.append(side[source % (per_micro // 2), index])
    dy_all = jnp.stack(dy_blocks)
    code_all = dy_all[:, :, width : width + EXPERTS].astype(F32).transpose(2, 0, 1)
    code_all = jnp.roll(code_all.reshape(EXPERTS, block_count * tokens), -first_expert, axis=0)
    rank_table = code_all[:8].astype(jnp.int32)

    for index in range(micro_count):
        pieces = [normed_two[index], *stage_rows[index]]
        pieces.append(swap(pieces[1], token_places[index][1]))
        pieces = jnp.stack(pieces)
        if index == 1:
            pieces, along, onward[0], firsts[1], dy_all, rank_table = after(
                pieces, along, onward[0], firsts[1], dy_all, rank_table
            )
            onward.append(swap(firsts[1], dp_places[1]))
            across = [swap(part, dp_places[-1]) for part in onward]
        row_halves += [pieces, swap(pieces, token_places[index][-1])]
    row_all = jnp.concatenate(row_halves, axis=0)

    def expert_pieces(expert):
        return [
            (parts[0], expert)
            if len(parts) == 1
            else (parts[expert >= cut], expert - cut * (expert >= cut))
            for parts in weight_parts
        ]

    router_t = jnp.roll(dense[:, width : width + EXPERTS].T, -first_expert, axis=0)
    logits = dot_cols(router_t, row_all.reshape(block_count * tokens, width))
    chosen = code_all > -1.5
    peak = jnp.max(jnp.where(chosen, logits, masked_score), axis=0, keepdims=True)
    raised = jnp.where(chosen, jnp.exp(jnp.where(chosen, logits, peak) - peak), 0.0)
    gate_table = (raised / jnp.sum(raised, axis=0, keepdims=True))[:8]
    me = jnp.stack([dp_index, first_expert]).astype(jnp.int32)
    held = None
    groups = [
        [index for index in range(dp_count) if index >> pair_bit & 1 == side] for side in range(2)
    ]
    summed = []
    me, *across = after(me, *across)
    weight_parts = [[mine_packed], [first_piece], [between], onward, [last_piece], [forward], [along], across]
    if len(dp_places) > 3:
        more = [[mine_packed], [first_piece], [between], onward]
        for place in dp_places[2:-1]:
            more = more + [[swap(part, place) for part in parts] for parts in more]
        weight_parts = more + [[swap(part, dp_places[-1]) for part in parts] for parts in more]

    for first, end in ((0, cut), (cut, local)):
        *held, grads = run_experts(
            first, me, [expert_pieces(expert) for expert in range(first, end)], weight_masks,
            pair_bit, row_all, dy_all, rank_table, gate_table, slots, local, held,
        )
        summed.append(
            lax.psum_scatter(
                grads, "dp", scatter_dimension=0, axis_index_groups=groups, tiled=True
            )[0]
        )
    eg_all, db_all = held

    slot_place = rank_table[:local]
    slot_place = jnp.where(
        slot_place >= 0, slot_place + slots * jnp.arange(local, dtype=jnp.int32)[:, None], -1
    )
    slot_place = jnp.concatenate(
        [slot_place, jnp.full((8 - local, block_count * tokens), -1, jnp.int32)], axis=0
    )
    slot_place = slot_place.reshape(8, block_count, tokens).transpose(1, 2, 0)

    def first_trade(source, places):
        found = []
        for index in range(micro_count):
            first, size = index * per_micro, per_micro // 2
            high = combine(source, places, first + size, size)
            received = swap(high, token_places[index][-1])
            low = combine(source, places, first, size)
            half_size = size // 2
            found.append(
                [
                    add_rounded(low[:half_size], received[:half_size]),
                    add_rounded(low[half_size:], received[half_size:]),
                ]
            )
        return found

    sums = first_trade(db_all, slot_place)
    received = [
        swap(sums[index][1], token_places[index][-2]) for index in range(micro_count)
    ]
    mix_place, *lows = after(slot_place, *[pair[0] for pair in sums])
    mixed = first_trade(eg_all, mix_place)
    flat, shape = jax.tree.flatten((received, mixed))
    received, mixed = jax.tree.unflatten(shape, lax.optimization_barrier(tuple(flat)))
    row_grads = []
    for index in range(micro_count):
        total = add_rounded(lows[index], received[index])
        row_grads.append(sum_home(total[:1], total[1:], token_places[index][:1])[0])

    router_grads, middle_grads, branch_grads, head_grads, gain_two_grads = [], [], [], [], []
    for index in range(micro_count):
        dz, dy1, branch, head_grad, gain_grad = middle_back(
            row_grads[index], middles[index], dys[index], gates[index], gain_two, dense
        )
        router_grads.append(dz)
        middle_grads.append(dy1)
        branch_grads.append(branch)
        head_grads.append(head_grad)
        gain_two_grads.append(gain_grad)

    def tall(parts):
        return jnp.concatenate(parts, axis=0)

    query_grads, pair_grads = [], []
    for index in range(micro_count):
        if index == micro_count - 1:
            attend_places[index], query_grads[0] = after(attend_places[index], query_grads[0])
        dq, pairs = attend_back(
            attend_places[index], queries[index], key_rows[index], head_grads[index],
            attended[index], log_totals[index], cos_t, sin_t,
        )
        pairs = pairs.reshape(owner_count, tokens, pairs.shape[1])
        middle_point = owner_count // 2
        pair_grads.append(sum_home(pairs[:middle_point], pairs[middle_point:], key_places)[0])
        query_grads.append(dq)
    branch_grads[0], query_grads[-1] = after(branch_grads[0], query_grads[-1])
    early = weight_grads(
        [tall(attended), tall(normed_two)],
        [tall(branch_grads), tall(router_grads)],
        sum(gain_two_grads),
        width + LANES,
    )
    along_z = [("dp", bit) for bit in reversed(range(1, dp_bits))]
    along_x = [("dp", 0)] if dp_bits else []
    home_two = Homeward(early, [("expert", 0)] + along_x + row_places + along_z)

    normed_all = normed.reshape(micro_count * tokens, width)

    pair_grads[0], summed[0], early = after(pair_grads[0], summed[0], early)
    other = [swap(summed[0][1], dp_places[0])]
    key_grads, input_grads, gain_one_grads = [], [], []
    for index in range(micro_count):
        dx, dkv, gain_grad = project_back(
            query_grads[index], pair_grads[index], x[index], middle_grads[index], gain_one,
            dense, cos, sin,
        )
        input_grads.append(dx)
        key_grads.append(dkv)
        gain_one_grads.append(gain_grad)
    gain_one_grad = home_two.pin(sum(gain_one_grads))
    late = weight_grads(
        [normed_all, normed_all],
        [tall(query_grads), tall(key_grads)],
        gain_one_grad,
        width + 2 * key_width + LANES,
    )
    home_one = Homeward(late, [("expert", 0)] + row_places + along_x + along_z)
    other.append(swap(summed[1][1], dp_places[0]))
    home_one.join()
    home_one.join()
    highs = after(home_one.held, *[pair[1] for pair in mixed])[1:]
    mix_received = [
        swap(highs[index], token_places[index][-2]) for index in range(micro_count)
    ]
    home_one.received, home_two.received, other[0], *mix_received = after(
        home_one.received, home_two.received, other[0], *mix_received
    )
    home_one.join()
    home_two.join()
    home_one.received, home_two.received, other[1] = after(
        home_one.received, home_two.received, other[1]
    )
    home_one.join()
    home_two.join()
    mixtures = []
    for index in range(micro_count):
        total = add_rounded(mixed[index][0], mix_received[index])
        mixtures.append(sum_home(total[:1], total[1:], token_places[index][:1])[0])
    layer_output = jnp.stack(
        [
            (middles[index] + mixtures[index].astype(F32)).astype(BF16)
            for index in range(micro_count)
        ]
    )[None]

    mine = jnp.concatenate([part[0] for part in summed], axis=0).astype(F32)
    other = jnp.concatenate(other, axis=0).astype(F32)
    if split == 2:
        lower = half == 0
        mine = jnp.concatenate(
            [jnp.where(lower, mine, other), jnp.where(lower, other, mine)], axis=0
        )
    else:
        mine = mine + other
    deep = w_gate.shape[1]
    inner = w_gate.shape[2]
    grad_gate = mine[:, :deep]
    grad_up = mine[:, deep : 2 * deep]
    grad_down = (
        mine[:, 2 * deep :]
        .reshape(owned, width // inner, w_down.shape[1], inner)
        .transpose(0, 2, 1, 3)
        .reshape(w_down.shape)
    )
    late_grads = home_one.rows()
    output_grads = home_two.rows()
    return (
        layer_output,
        jnp.stack(input_grads)[None],
        late_grads[:, :width],
        late_grads[:, width : width + key_width],
        late_grads[:, width + key_width : width + 2 * key_width],
        output_grads[:, :width],
        output_grads[:, width : width + EXPERTS],
        late_grads[:, width + 2 * key_width + EXPERTS],
        output_grads[:, width + EXPERTS],
        grad_gate,
        grad_up,
        grad_down,
    )


def solution(mesh):
    return jax.shard_map(
        shards,
        mesh=mesh,
        in_specs=(
            P("dp", None, "expert", None),
            P("dp", None, "expert", None),
            P("dp", None),
            P("dp", None, "expert", None),
            P(),
            P(("dp", "expert"), None),
            P(("dp", "expert"), None),
            P(("dp", "expert"), None),
            P(("dp", "expert"), None),
            P(("dp", "expert"), None),
            P(("dp", "expert")),
            P(("dp", "expert")),
            P("expert", "dp", None),
            P("expert", "dp", None),
            P("expert", "dp", None),
        ),
        out_specs=(
            P("dp", None, "expert", None),
            P("dp", None, "expert", None),
            P(("dp", "expert"), None),
            P(("dp", "expert"), None),
            P(("dp", "expert"), None),
            P(("dp", "expert"), None),
            P(("dp", "expert"), None),
            P(("dp", "expert")),
            P(("dp", "expert")),
            P("expert", "dp", None),
            P("expert", "dp", None),
            P("expert", "dp", None),
        ),
        check_vma=False,
    )
```

```python
import functools

import jax
import jax.numpy as jnp
from jax import lax
from jax.experimental import pallas as pl
from jax.experimental.pallas import tpu as pltpu
from jax.sharding import PartitionSpec as P

QUERY_HEAD_COUNT = 24
KEY_VALUE_HEADS = 8
HEAD_DIMENSION = 64
EXPERTS = 40
TOPK = 8

epsilon = 1e-06
rope_base = 10000.0
masked_score = -1e30

F32 = jnp.float32
BF16 = jnp.bfloat16
AXES = ("dp", "expert")
HALF_HEAD = HEAD_DIMENSION // 2
GROUP = QUERY_HEAD_COUNT // KEY_VALUE_HEADS
PAIRS = KEY_VALUE_HEADS // 2
PAIR_LANES = 2 * HEAD_DIMENSION
QUERY_LANES = GROUP * PAIR_LANES
LANES = 128
BLOCKS_PER_STEP = 4


def dot(left, right):
    return jnp.dot(left, right, preferred_element_type=F32)


def dot_rows(left, right):
    return lax.dot_general(left, right, (((0,), (0,)), ((), ())), preferred_element_type=F32)


def dot_cols(left, right):
    return lax.dot_general(left, right, (((1,), (1,)), ((), ())), preferred_element_type=F32)


def add_rounded(left, right):
    return (left.astype(F32) + right.astype(F32)).astype(left.dtype)


def params(limit_mib, steps=1):
    return pltpu.CompilerParams(
        dimension_semantics=("arbitrary",) * steps, vmem_limit_bytes=limit_mib << 20
    )


def lasting(micros):
    return pl.CostEstimate(flops=int(micros * 3e7), bytes_accessed=0, transcendentals=0)


def whole_spec():
    return pl.BlockSpec(memory_space=pltpu.VMEM)


def swap(array, place):
    axis, bit = place
    dp_count, owner_count = lax.axis_size("dp"), lax.axis_size("expert")
    flip = (1 << bit) * (owner_count if axis == "dp" else 1)
    return lax.ppermute(array, AXES, [(i, i ^ flip) for i in range(dp_count * owner_count)])


def gather_pieces(array, places):
    pieces = [array]
    for place in places:
        pieces = pieces + [swap(piece, place) for piece in pieces]
    return pieces


def after(value, *others):
    return lax.optimization_barrier((value, *others))


def gather_rows(array, places):
    pieces = jnp.stack(gather_pieces(array, places[:-1]))
    return pieces, swap(pieces, places[-1])


def sum_home(low, high, places):
    for place in reversed(places):
        total = high.shape[0]
        received = swap(high, place)
        if total == 1:
            return add_rounded(low, received)
        low, high = (
            add_rounded(low[: total // 2], received[: total // 2]),
            add_rounded(low[total // 2 :], received[total // 2 :]),
        )
    return low


def without_bit(index, bit):
    return ((index >> (bit + 1)) << bit) | (index & ((1 << bit) - 1))


class Homeward:
    def __init__(self, grads, places):
        bits = lax.axis_size("dp").bit_length() + lax.axis_size("expert").bit_length() - 2
        self.held = grads.reshape((2,) * bits + (grads.shape[0] >> bits, grads.shape[1]))
        self.ranks = list(reversed(range(bits)))
        self.places = list(places)
        self.start()

    def start(self):
        axis, bit = self.places[0]
        owner_bits = lax.axis_size("expert").bit_length() - 1
        depth = self.ranks.index(bit + (owner_bits if axis == "dp" else 0))
        self.ranks.pop(depth)
        upper = (lax.axis_index(axis) >> bit) & 1
        away = lax.dynamic_index_in_dim(self.held, 1 - upper, depth, False)
        self.held = lax.dynamic_index_in_dim(self.held, upper, depth, False)
        self.received = swap(away, self.places.pop(0))

    def join(self):
        self.held = add_rounded(self.held, self.received)
        if self.places:
            self.start()
        else:
            self.received = None

    def pin(self, value):
        value, self.received = after(value, self.received)
        self.join()
        return value

    def rows(self):
        while self.received is not None:
            self.join()
        return self.held.astype(F32)


def masks_of(places):
    found = []
    for piece in range(1 << len(places)):
        mask = {"dp": 0, "expert": 0}
        for stage, (axis, bit) in enumerate(places):
            if piece >> stage & 1:
                mask[axis] |= 1 << bit
        found.append(mask)
    return found


def half_swap(rows):
    lane = lax.broadcasted_iota(jnp.int32, rows.shape, 1)
    return jnp.where(
        lane % HEAD_DIMENSION < HALF_HEAD,
        pltpu.roll(rows, rows.shape[1] - HALF_HEAD, 1),
        pltpu.roll(rows, HALF_HEAD, 1),
    )


def project_kernel(x_ref, gain_ref, w_ref, cos_ref, sin_ref, h_ref, q_ref, kv_ref):
    x = x_ref[0].astype(F32)
    scale = lax.rsqrt(jnp.mean(x * x, axis=1, keepdims=True) + epsilon)
    h_ref[0] = (x * scale * gain_ref[...]).astype(BF16)
    cos, sin = cos_ref[...], sin_ref[...]
    width = q_ref.shape[2]
    key_width = kv_ref.shape[2] // 2

    def turn_into(out_ref, start, rows):
        for tile in range(0, rows.shape[1], LANES):
            part = rows[:, tile : tile + LANES]
            out_ref[0, :, start + tile : start + tile + LANES] = (
                part * cos + half_swap(part) * sin
            ).astype(BF16)

    first = width + LANES
    for start in range(0, width, key_width):
        turn_into(q_ref, start, dot(h_ref[0], w_ref[:, first + start : first + start + key_width]))
    first = first + width
    turn_into(kv_ref, 0, dot(h_ref[0], w_ref[:, first : first + key_width]))
    value = dot(h_ref[0], w_ref[:, first + key_width : first + 2 * key_width])
    kv_ref[0, :, key_width:] = value.astype(BF16)


def project(x, gain, dense, cos, sin):
    count, rows, width = x.shape
    key_width = KEY_VALUE_HEADS * HEAD_DIMENSION
    row_spec = pl.BlockSpec((1, rows, width), lambda i: (i, 0, 0))
    return pl.pallas_call(
        project_kernel,
        grid=(count,),
        in_specs=[
            row_spec,
            pl.BlockSpec((1, width), lambda i: (0, 0)),
            pl.BlockSpec(dense.shape, lambda i: (0, 0), pipeline_mode=pl.Buffered(1)),
            pl.BlockSpec((rows, LANES), lambda i: (0, 0)),
            pl.BlockSpec((rows, LANES), lambda i: (0, 0)),
        ],
        out_specs=[
            row_spec,
            row_spec,
            pl.BlockSpec((1, rows, 2 * key_width), lambda i: (i, 0, 0)),
        ],
        out_shape=[
            jax.ShapeDtypeStruct(x.shape, BF16),
            jax.ShapeDtypeStruct(x.shape, BF16),
            jax.ShapeDtypeStruct((count, rows, 2 * key_width), BF16),
        ],
        cost_estimate=lasting(8),
        compiler_params=params(48),
    )(x, gain, dense, cos, sin)


def middle_kernel(x_ref, o_ref, wo_ref, wr_ref, gain_ref, code_ref, y_ref, h_ref, g_ref):
    middle = x_ref[...].astype(F32) + dot(o_ref[...], wo_ref[...])
    y_ref[...] = middle
    scale = lax.rsqrt(jnp.mean(middle * middle, axis=1, keepdims=True) + epsilon)
    normed = (middle * scale * gain_ref[...]).astype(BF16)
    h_ref[...] = normed
    logits = dot(normed, wr_ref[...])
    chosen = code_ref[...] > -1.5
    peak = jnp.max(jnp.where(chosen, logits, masked_score), axis=1, keepdims=True)
    raised = jnp.where(chosen, jnp.exp(jnp.where(chosen, logits, peak) - peak), 0.0)
    g_ref[...] = raised / jnp.sum(raised, axis=1, keepdims=True)


def middle_rows(x, attended, dense, gain, code):
    rows, width = x.shape
    full = pl.BlockSpec((rows, width), lambda i: (0, 0))
    return pl.pallas_call(
        middle_kernel,
        grid=(1,),
        in_specs=[
            full,
            full,
            pl.BlockSpec((width, width), lambda i: (0, 0)),
            pl.BlockSpec((width, LANES), lambda i: (0, width // LANES)),
            pl.BlockSpec((1, width), lambda i: (0, 0)),
            pl.BlockSpec((rows, LANES), lambda i: (0, 0)),
        ],
        out_specs=[full, full, pl.BlockSpec((rows, LANES), lambda i: (0, 0))],
        out_shape=[
            jax.ShapeDtypeStruct((rows, width), F32),
            jax.ShapeDtypeStruct((rows, width), BF16),
            jax.ShapeDtypeStruct((rows, LANES), F32),
        ],
        cost_estimate=lasting(4.5),
        compiler_params=params(48),
    )(x, attended, dense, dense, gain, code)


def middle_back_kernel(
    acc_ref, y_ref, dy_ref, g_ref, dg_ref, gain_ref, wr_ref, wo_ref,
    dz_ref, dy1_ref, dr_ref, do_ref, dgain_ref,
):
    gates, gate_grads = g_ref[...], dg_ref[...].astype(F32)
    mean = jnp.sum(gates * gate_grads, axis=1, keepdims=True)
    dz = (gates * (gate_grads - mean)).astype(BF16)
    dz_ref[...] = dz
    dh = acc_ref[...].astype(F32) + dot_cols(dz, wr_ref[...])
    middle = y_ref[...]
    scale = lax.rsqrt(jnp.mean(middle * middle, axis=1, keepdims=True) + epsilon)
    dgain_ref[...] = jnp.sum(dh * middle * scale, axis=0, keepdims=True)
    scaled = dh * gain_ref[...]
    along = jnp.mean(scaled * middle, axis=1, keepdims=True)
    dy1 = dy_ref[...].astype(F32) + scale * scaled - middle * (scale * scale * scale * along)
    dy1_ref[...] = dy1
    rounded = dy1.astype(BF16)
    dr_ref[...] = rounded
    do_ref[...] = dot_cols(rounded, wo_ref[...]).astype(BF16)


def middle_back(acc, middle, dy, gates, gain, dense):
    rows, width = middle.shape
    full = pl.BlockSpec((rows, width), lambda i: (0, 0))
    lane = pl.BlockSpec((rows, LANES), lambda i: (0, 0))
    line = pl.BlockSpec((1, width), lambda i: (0, 0))
    return pl.pallas_call(
        middle_back_kernel,
        grid=(1,),
        in_specs=[
            full, full, full, lane,
            pl.BlockSpec((rows, LANES), lambda i: (0, width // LANES)),
            line,
            pl.BlockSpec((width, LANES), lambda i: (0, width // LANES)),
            pl.BlockSpec((width, width), lambda i: (0, 0)),
        ],
        out_specs=[lane, full, full, full, line],
        out_shape=[
            jax.ShapeDtypeStruct((rows, LANES), BF16),
            jax.ShapeDtypeStruct((rows, width), F32),
            jax.ShapeDtypeStruct((rows, width), BF16),
            jax.ShapeDtypeStruct((rows, width), BF16),
            jax.ShapeDtypeStruct((1, width), F32),
        ],
        cost_estimate=lasting(6.6),
        compiler_params=params(56),
    )(acc, middle, dy, gates, acc, gain, dense, dense)


def project_back_kernel(
    dq_ref, pairs_ref, x_ref, dy1_ref, gain_ref, w_ref, cos_ref, sin_ref,
    dx_ref, dkv_ref, dgain_ref,
):
    cos, sin = cos_ref[...], sin_ref[...]
    width = x_ref.shape[1]
    key_width = dkv_ref.shape[1] // 2
    for pair in range(PAIRS):
        lanes = slice(pair * LANES, (pair + 1) * LANES)
        start = 2 * pair * LANES
        part = pairs_ref[:, start : start + LANES].astype(F32)
        dkv_ref[:, lanes] = (part * cos - half_swap(part) * sin).astype(BF16)
        lanes = slice(key_width + pair * LANES, key_width + (pair + 1) * LANES)
        dkv_ref[:, lanes] = pairs_ref[:, start + LANES : start + 2 * LANES]
    first = width + LANES
    dh = dot_cols(dq_ref[...], w_ref[:, first : first + width])
    first = first + width
    dh = dh + dot_cols(dkv_ref[...], w_ref[:, first : first + 2 * key_width])
    x = x_ref[...].astype(F32)
    scale = lax.rsqrt(jnp.mean(x * x, axis=1, keepdims=True) + epsilon)
    dgain_ref[...] = jnp.sum(dh * x * scale, axis=0, keepdims=True)
    scaled = dh * gain_ref[...]
    along = jnp.mean(scaled * x, axis=1, keepdims=True)
    dx_ref[...] = dy1_ref[...] + scale * scaled - x * (scale * scale * scale * along)


def project_back(dq, pairs, x, dy1, gain, dense, cos, sin):
    rows, width = x.shape
    key_width = pairs.shape[1] // 2
    full = pl.BlockSpec((rows, width), lambda i: (0, 0))
    lane = pl.BlockSpec((rows, LANES), lambda i: (0, 0))
    line = pl.BlockSpec((1, width), lambda i: (0, 0))
    both = pl.BlockSpec((rows, 2 * key_width), lambda i: (0, 0))
    return pl.pallas_call(
        project_back_kernel,
        grid=(1,),
        in_specs=[
            full, both, full, full, line,
            pl.BlockSpec(dense.shape, lambda i: (0, 0), pipeline_mode=pl.Buffered(1)),
            lane, lane,
        ],
        out_specs=[full, both, line],
        out_shape=[
            jax.ShapeDtypeStruct((rows, width), F32),
            jax.ShapeDtypeStruct((rows, 2 * key_width), BF16),
            jax.ShapeDtypeStruct((1, width), F32),
        ],
        cost_estimate=lasting(8.2),
        compiler_params=params(56),
    )(dq, pairs, x, dy1, gain, dense, cos, sin)


def weight_grad_kernel(count, *refs):
    left_refs, right_refs, out_ref = refs[:count], refs[count : 2 * count], refs[-1]
    rows, columns = out_ref.shape
    if len(refs) > 2 * count + 1:
        gain = jnp.broadcast_to(refs[2 * count][...], (8, rows)).T
    lane = lax.broadcasted_iota(jnp.int32, (rows, LANES), 1)
    start = 0
    for left_ref, right_ref in zip(left_refs, right_refs):
        left = left_ref[...].T
        width = right_ref.shape[1]
        step = min(width, 4 * LANES)
        for tile in range(0, width, step):
            part = dot(left, right_ref[:, tile : tile + step])
            if start + tile + step == columns and len(refs) > 2 * count + 1:
                edge = part[:, step - LANES :]
                edge = jnp.where(lane == EXPERTS, gain[:, 0:1], edge)
                out_ref[:, columns - LANES :] = edge.astype(BF16)
                part = part[:, : step - LANES]
            if part.shape[1]:
                out_ref[:, start + tile : start + tile + part.shape[1]] = part.astype(BF16)
        start += width
    if start < columns:
        out_ref[:, start:] = jnp.where(lane == EXPERTS, gain[:, 0:1], 0.0).astype(BF16)


def weight_grads(lefts, rights, gain, columns):
    rows = lefts[0].shape[1]
    operands = [*lefts, *rights] + ([] if gain is None else [gain])
    return pl.pallas_call(
        functools.partial(weight_grad_kernel, len(lefts)),
        in_specs=[whole_spec() for _ in operands],
        out_specs=whole_spec(),
        out_shape=jax.ShapeDtypeStruct((rows, columns), BF16),
        cost_estimate=lasting(9),
        compiler_params=pltpu.CompilerParams(vmem_limit_bytes=56 << 20),
    )(*operands)


def fill_bias(places_ref, bias_ref, rows):
    query = places_ref[0] + lax.broadcasted_iota(jnp.int32, (rows, rows), 1)
    inside = lax.broadcasted_iota(jnp.int32, (rows, rows), 0)
    for block in range(bias_ref.shape[0] // rows):
        key = places_ref[2 + block] + inside
        allowed = (key <= query) & (key < places_ref[1])
        bias_ref[block * rows : (block + 1) * rows, :] = jnp.where(allowed, 0.0, masked_score)


def attend_kernel(places_ref, q_ref, k_ref, v_ref, o_ref, lse_ref, bias_ref):
    rows = q_ref.shape[0]

    @pl.when(pl.program_id(0) == 0)
    def _():
        fill_bias(places_ref, bias_ref, rows)

    outs = []
    for side in range(2):
        lanes = slice(side * HEAD_DIMENSION, (side + 1) * HEAD_DIMENSION)
        key = k_ref[:, lanes]
        value_t = v_ref[:, lanes].T
        for member in range(GROUP):
            head = side * GROUP + member
            query = q_ref[:, head * HEAD_DIMENSION : (head + 1) * HEAD_DIMENSION]
            scores = dot_cols(key, query * HEAD_DIMENSION**-0.5) + bias_ref[...]
            peak = jnp.max(scores, axis=0, keepdims=True)
            raised = jnp.exp(scores - peak)
            total = jnp.sum(raised, axis=0, keepdims=True)
            outs.append(dot(value_t, raised.astype(BF16)) / total)
            lse_ref[0, head : head + 1, :] = peak + jnp.log(total)
    o_ref[...] = jnp.concatenate(outs, axis=0).T.astype(BF16)


def attend(places, q, kv):
    rows, width = q.shape
    keys = kv.shape[0]
    return pl.pallas_call(
        attend_kernel,
        grid_spec=pltpu.PrefetchScalarGridSpec(
            num_scalar_prefetch=1,
            grid=(PAIRS,),
            in_specs=[
                pl.BlockSpec((rows, QUERY_LANES), lambda i, s: (0, i)),
                pl.BlockSpec((keys, PAIR_LANES), lambda i, s: (0, i)),
                pl.BlockSpec((keys, PAIR_LANES), lambda i, s: (0, PAIRS + i)),
            ],
            out_specs=[
                pl.BlockSpec((rows, QUERY_LANES), lambda i, s: (0, i)),
                pl.BlockSpec((1, 8, rows), lambda i, s: (i, 0, 0)),
            ],
            scratch_shapes=[pltpu.VMEM((keys, rows), F32)],
        ),
        out_shape=[
            jax.ShapeDtypeStruct((rows, width), BF16),
            jax.ShapeDtypeStruct((PAIRS, 8, rows), F32),
        ],
        cost_estimate=lasting(19),
        compiler_params=params(48),
    )(places, q, kv, kv)


def attend_back_kernel(
    places_ref, q_ref, k_ref, v_ref, do_ref, o_ref, lse_ref, cos_ref, sin_ref,
    dq_ref, dkv_ref, bias_ref,
):
    rows = q_ref.shape[0]

    @pl.when(pl.program_id(0) == 0)
    def _():
        fill_bias(places_ref, bias_ref, rows)

    score_scale = HEAD_DIMENSION**-0.5
    cos, sin = cos_ref[...], sin_ref[...]
    ones = jnp.ones((8, HEAD_DIMENSION), F32)
    query_grads = []
    for side in range(2):
        lanes = slice(side * HEAD_DIMENSION, (side + 1) * HEAD_DIMENSION)
        key, value = k_ref[:, lanes], v_ref[:, lanes]
        key_t = key.T
        key_grad = None
        value_grad = None
        for member in range(GROUP):
            head = side * GROUP + member
            columns = slice(head * HEAD_DIMENSION, (head + 1) * HEAD_DIMENSION)
            query = q_ref[:, columns] * score_scale
            grad = do_ref[:, columns]
            overlap = grad.astype(F32) * o_ref[:, columns].astype(F32)
            along = lax.dot_general(
                ones, overlap, (((1,), (1,)), ((), ())),
                precision=lax.Precision.HIGHEST, preferred_element_type=F32,
            )[0:1]
            scores = dot_cols(key, query) + bias_ref[...]
            probs = jnp.exp(scores - lse_ref[0, head : head + 1, :])
            score_grad = (probs * (dot_cols(value, grad) - along)).astype(BF16)
            value_part = dot(probs.astype(BF16), grad)
            key_part = dot(score_grad, query)
            value_grad = value_part if value_grad is None else value_grad + value_part
            key_grad = key_part if key_grad is None else key_grad + key_part
            turned = dot(key_t, score_grad) * score_scale
            upper, lower = turned[:HALF_HEAD], turned[HALF_HEAD:]
            query_grads += [upper * cos + lower * sin, lower * cos - upper * sin]
        dkv_ref[:, lanes] = key_grad.astype(BF16)
        shifted = slice(LANES + side * HEAD_DIMENSION, LANES + (side + 1) * HEAD_DIMENSION)
        dkv_ref[:, shifted] = value_grad.astype(BF16)
    dq_ref[...] = jnp.concatenate(query_grads, axis=0).T.astype(BF16)


def attend_back(places, q, kv, grad, attended, lse, cos_t, sin_t):
    rows, width = q.shape
    keys = kv.shape[0]
    key_width = kv.shape[1] // 2
    wide = pl.BlockSpec((rows, QUERY_LANES), lambda i, s: (0, i))
    tall = pl.BlockSpec((keys, PAIR_LANES), lambda i, s: (0, i))
    table = pl.BlockSpec((HALF_HEAD, rows), lambda i, s: (0, 0))
    return pl.pallas_call(
        attend_back_kernel,
        grid_spec=pltpu.PrefetchScalarGridSpec(
            num_scalar_prefetch=1,
            grid=(PAIRS,),
            in_specs=[
                wide,
                tall,
                pl.BlockSpec((keys, PAIR_LANES), lambda i, s: (0, PAIRS + i)),
                wide,
                wide,
                pl.BlockSpec((1, 8, rows), lambda i, s: (i, 0, 0)),
                table,
                table,
            ],
            out_specs=[wide, pl.BlockSpec((keys, 2 * PAIR_LANES), lambda i, s: (0, i))],
            scratch_shapes=[pltpu.VMEM((keys, rows), F32)],
        ),
        out_shape=[
            jax.ShapeDtypeStruct((rows, width), BF16),
            jax.ShapeDtypeStruct((keys, 2 * key_width), BF16),
        ],
        cost_estimate=lasting(23.5),
        compiler_params=params(56),
    )(places, q, kv, kv, grad, attended, lse, cos_t, sin_t)


def expert_kernel(masks, sources, pair_bit, first, aliased, me_ref, *refs):
    count = len(masks)
    arrays = 1 + max(array for per_expert in sources for array, _ in per_expert)
    pieces, refs = refs[:arrays], refs[arrays:]
    h_ref, dy_ref, rank_ref, gate_ref = refs[:4]
    refs = refs[4 + (2 if aliased else 0) :]
    eg_ref, db_ref = refs[:2]
    out_ref, refs = refs[2], refs[3:]
    w_in, w_down, g_in, g_down, rows_all, de_all, hidden_all, dau_all, in_sem, out_sem = refs
    member, step = pl.program_id(0), pl.program_id(1)
    expert = first + member
    side = lax.rem(member, 2)
    blocks, tokens, width = h_ref.shape
    slots = eg_ref.shape[2]
    chunk = blocks * slots
    inner = w_down.shape[1]
    deep = width // count
    shallow = inner // count
    wide = width // inner
    me = me_ref[0]

    def windows(piece_ref, shard, into, down):
        top = pl.ds(pl.multiple_of(shard * deep, 16), deep)
        low = pl.ds(pl.multiple_of(shard * shallow, 16), shallow)
        pairs = [
            (piece_ref.at[pl.ds(0, deep)], into.at[top, pl.ds(0, inner)]),
            (piece_ref.at[pl.ds(deep, deep)], into.at[top, pl.ds(inner, inner)]),
        ]
        for part in range(wide):
            pairs.append(
                (
                    piece_ref.at[pl.ds(2 * deep + part * shallow, shallow)],
                    down.at[low, pl.ds(part * inner, inner)],
                )
            )
        return pairs

    def loads(which):
        made = []
        into, down, sems = w_in.at[which % 2], w_down.at[which % 2], in_sem.at[which % 2]
        for (array, index), mask in zip(sources[which], masks):
            for source, target in windows(pieces[array].at[index], me ^ mask, into, down):
                made.append(pltpu.make_async_copy(source, target, sems.at[len(made)]))
        return made

    def stores(which):
        made = []
        for piece, mask in enumerate(masks):
            target = out_ref.at[without_bit(me ^ mask, pair_bit), piece & 1, which]
            for there, here in windows(target, me ^ mask, g_in, g_down):
                made.append(pltpu.make_async_copy(here, there, out_sem.at[len(made)]))
        return made

    for which in range(len(sources)):
        early = (member == 0) & (step == 0) if which == 0 else (member == which - 1) & (step == 1)

        @pl.when(early)
        def _(which=which):
            for copy in loads(which):
                copy.start()

    slot = lax.broadcasted_iota(jnp.int32, (slots, tokens), 0)
    grads = []
    weights = []
    for block in range(blocks):
        start = pl.multiple_of((step * blocks + block) * tokens, LANES)
        hit = slot == rank_ref[expert, :, pl.ds(start, tokens)]
        select = jnp.where(hit, 1.0, 0.0).astype(BF16)
        place = pl.ds(pl.multiple_of(step * chunk + block * slots, 16), slots)
        rows_all[place, :] = dot(select, h_ref[block]).astype(BF16)
        grads.append(dot(select, dy_ref[block]))
        gate = gate_ref[expert, :, pl.ds(start, tokens)]
        weights.append(jnp.sum(jnp.where(hit, gate, 0.0), axis=1, keepdims=True))

    for which in range(len(sources)):

        @pl.when((member == which) & (step == 0))
        def _(which=which):
            for copy in loads(which):
                copy.wait()

    here = pl.ds(pl.multiple_of(step * chunk, 16), chunk)
    grad_rows = jnp.concatenate(grads, axis=0)
    weight = jnp.concatenate(weights, axis=0)
    pre = dot(rows_all[here, :], w_in[side])
    gate_pre, up_pre = pre[:, :inner], pre[:, inner:]
    sigmoid = 1.0 / (1.0 + jnp.exp(-gate_pre))
    silu = gate_pre * sigmoid
    hidden = (silu * up_pre).astype(BF16)
    hidden_all[here, :] = hidden
    out = dot(hidden, w_down[side]).astype(BF16).astype(F32)
    row_grad = jnp.sum(grad_rows * out, axis=1, keepdims=True)
    out = (weight * out).astype(BF16)
    lane = lax.broadcasted_iota(jnp.int32, (slots, LANES), 1)
    for block in range(blocks):
        part = slice(block * slots, (block + 1) * slots)
        eg_ref[block, 0] = out[part]
        db_ref[block, 0, :, width:] = jnp.where(lane == me_ref[1] + expert, row_grad[part], 0.0).astype(
            BF16
        )
    de = (weight * grad_rows).astype(BF16)
    de_all[here, :] = de
    grad_hidden = dot_cols(de, w_down[side])
    grad_up = (grad_hidden * silu).astype(BF16)
    grad_gate = (
        grad_hidden * up_pre * sigmoid * (1.0 + gate_pre * (1.0 - sigmoid))
    ).astype(BF16)
    dau_all[here, :inner] = grad_gate
    dau_all[here, inner:] = grad_up
    back = dot_cols(dau_all[here, :], w_in[side]).astype(BF16)
    for block in range(blocks):
        db_ref[block, 0, :, :width] = back[block * slots : (block + 1) * slots]

    last = step == pl.num_programs(1) - 1
    for which in range(1, len(sources)):

        @pl.when(last & (member == which))
        def _(which=which):
            for copy in stores(which - 1):
                copy.wait()

    @pl.when(last)
    def _():
        for part in range(wide):
            lanes = slice(part * inner, (part + 1) * inner)
            g_in[lanes, :] = dot_rows(rows_all[:, lanes], dau_all[...]).astype(BF16)
        g_down[...] = dot_rows(hidden_all[...], de_all[...]).astype(BF16)

    for which in range(len(sources)):

        @pl.when(last & (member == which))
        def _(which=which):
            for copy in stores(which):
                copy.start()
            if which == len(sources) - 1:
                for copy in stores(which):
                    copy.wait()


def run_experts(first, me, pieces, masks, pair_bit, h_all, dy_all, ranks, gates, slots, local, earlier):
    block_count, tokens, width = h_all.shape
    members = len(pieces)
    arrays = []
    sources = []
    for per_expert in pieces:
        found = []
        for array, index in per_expert:
            known = [place for place, other in enumerate(arrays) if other is array]
            if not known:
                known = [len(arrays)]
                arrays.append(array)
            found.append((known[0], index))
        sources.append(found)
    piece_rows, inner = arrays[0].shape[1:]
    count = len(masks)
    steps = block_count // BLOCKS_PER_STEP
    rows = block_count * slots
    block_spec = pl.BlockSpec((BLOCKS_PER_STEP, tokens, width), lambda g, i, s: (i, 0, 0))
    any_spec = pl.BlockSpec(memory_space=pl.ANY)
    table = pl.BlockSpec((ranks.shape[0], 1, ranks.shape[1]), lambda g, i, s: (0, 0, 0))
    widths = (width, width + LANES)
    copies = count * (2 + width // inner)
    extra = [] if earlier is None else list(earlier)
    start = 1 + len(arrays) + 4
    aliases = {start + place: place for place in range(len(extra))}
    return pl.pallas_call(
        functools.partial(expert_kernel, masks, sources, pair_bit, first, earlier is not None),
        grid_spec=pltpu.PrefetchScalarGridSpec(
            num_scalar_prefetch=1,
            grid=(members, steps),
            in_specs=[any_spec] * len(arrays)
            + [block_spec, block_spec, table, table]
            + [any_spec] * len(extra),
            out_specs=[
                pl.BlockSpec(
                    (BLOCKS_PER_STEP, 1, slots, w), lambda g, i, s: (i, first + g, 0, 0)
                )
                for w in widths
            ]
            + [any_spec],
            scratch_shapes=[
                pltpu.VMEM((2, width, 2 * inner), BF16),
                pltpu.VMEM((2, inner, width), BF16),
                pltpu.VMEM((width, 2 * inner), BF16),
                pltpu.VMEM((inner, width), BF16),
                pltpu.VMEM((rows, width), BF16),
                pltpu.VMEM((rows, width), BF16),
                pltpu.VMEM((rows, inner), BF16),
                pltpu.VMEM((rows, 2 * inner), BF16),
                pltpu.SemaphoreType.DMA((2, copies)),
                pltpu.SemaphoreType.DMA((copies,)),
            ],
        ),
        out_shape=[jax.ShapeDtypeStruct((block_count, local, slots, w), BF16) for w in widths]
        + [jax.ShapeDtypeStruct((count // 2, 2, members, piece_rows, inner), BF16)],
        input_output_aliases=aliases,
        cost_estimate=lasting(31 * members),
        compiler_params=params(60, 2),
    )(me, *arrays, h_all, dy_all, ranks[:, None], gates[:, None], *extra)


def combine_kernel(src_ref, place_ref, out_ref):
    _, local, slots, width = src_ref.shape
    tokens = out_ref.shape[1]
    lane = lax.broadcasted_iota(jnp.int32, (tokens, local * slots), 1)
    hit = lane == place_ref[0, :, 0:1]
    for expert in range(1, local):
        hit = hit | (lane == place_ref[0, :, expert : expert + 1])
    source = src_ref[0].reshape(local * slots, width)
    out_ref[0] = dot(jnp.where(hit, 1.0, 0.0).astype(BF16), source).astype(BF16)


def combine(source, places, first, size):
    _, local, slots, width = source.shape
    tokens = places.shape[1]
    return pl.pallas_call(
        combine_kernel,
        grid=(size,),
        in_specs=[
            pl.BlockSpec((1, local, slots, width), lambda i: (first + i, 0, 0, 0)),
            pl.BlockSpec((1, tokens, places.shape[2]), lambda i: (first + i, 0, 0)),
        ],
        out_specs=pl.BlockSpec((1, tokens, width), lambda i: (i, 0, 0)),
        out_shape=jax.ShapeDtypeStruct((size, tokens, width), BF16),
        cost_estimate=lasting(4.4),
        compiler_params=params(60),
    )(source, places)


def pack_experts(gate, up, down):
    width = down.shape[2]
    inner = gate.shape[2]
    columns = [down[:, :, start : start + inner] for start in range(0, width, inner)]
    return jnp.concatenate([gate, up] + columns, axis=1)


def slot_codes(picks, valid, capacity):
    rows = picks.shape[0]
    ids = jnp.arange(EXPERTS, dtype=jnp.int32)
    named = jnp.any(picks[:, :, None] == ids[None, None, :], axis=1)
    counted = (named & valid[:, None]).astype(BF16)
    before = (
        lax.broadcasted_iota(jnp.int32, (rows, rows), 1)
        < lax.broadcasted_iota(jnp.int32, (rows, rows), 0)
    ).astype(BF16)
    ranks = dot(before, counted)
    kept = (counted > 0) & (ranks < capacity[None, :].astype(F32))
    return jnp.where(kept, ranks, jnp.where(named, -1.0, -2.0))


def shards(
    layer_input,
    cotangent,
    lengths,
    routes,
    capacity,
    w_query,
    key_weight,
    value_weight,
    w_output,
    w_router,
    gain_attn,
    gain_moe,
    w_gate,
    w_up,
    w_down,
):
    micro_count, tokens, width = layer_input.shape[1:]
    dp_count, owner_count = lax.axis_size("dp"), lax.axis_size("expert")
    dp_index, owner_index = lax.axis_index("dp"), lax.axis_index("expert")
    slots = tokens // 4
    owned = w_gate.shape[0]
    key_width = key_weight.shape[1]
    dp_bits = dp_count.bit_length() - 1
    owner_bits = owner_count.bit_length() - 1
    split = 2 if owned % 2 == 0 and dp_bits > 1 else 1
    local = owned // split
    pair_bit = 1 if dp_bits > 1 else 0
    dp_places = [("dp", pair_bit)] + [
        ("dp", bit) for bit in reversed(range(dp_bits)) if bit != pair_bit
    ]
    row_places = [("expert", bit) for bit in range(1, owner_bits)]
    key_places = row_places + [("expert", 0)]
    if split == 2:
        token_places = [
            row_places + [("dp", pair_bit), ("expert", 0)],
            [("dp", pair_bit)] + row_places + [("expert", 0)],
        ]
    else:
        token_places = [key_places, key_places]
    half = (dp_index >> pair_bit) & 1 if split == 2 else 0
    first_expert = owner_index * owned + half * local

    rows_owned = w_query.shape[0]

    def padded(parts):
        taken = sum(part.shape[1] for part in parts)
        return parts + [jnp.zeros((rows_owned, -taken % LANES), BF16)]

    packed = padded([w_output, w_router, gain_moe[:, None]])
    packed += padded([w_query, key_weight, value_weight, gain_attn[:, None]])
    dense = lax.all_gather(jnp.concatenate(packed, axis=1), AXES, axis=0, tiled=True)

    def packed_half(which):
        return pack_experts(
            *[
                lax.dynamic_slice_in_dim(weight, which * local, local, 0)
                for weight in (w_gate, w_up, w_down)
            ]
        )

    mine_packed = packed_half(half)
    other_packed = packed_half(1 - half) if split == 2 else mine_packed
    weight_masks = [mask["dp"] for mask in masks_of(dp_places)]
    start_row = owner_index * tokens
    places = start_row + jnp.arange(tokens, dtype=jnp.int32)
    freqs = rope_base ** (-jnp.arange(0, HEAD_DIMENSION, 2, dtype=F32) / HEAD_DIMENSION)
    angles = places.astype(F32)[:, None] * freqs[None, :]
    cos_half, sin_half = jnp.cos(angles), jnp.sin(angles)
    cos = jnp.tile(cos_half, (1, LANES // HALF_HEAD))
    sin = jnp.tile(jnp.concatenate([-sin_half, sin_half], axis=1), (1, LANES // HEAD_DIMENSION))
    cos_t, sin_t = cos_half.T, sin_half.T
    key_starts = jnp.stack(
        [(owner_index ^ mask["expert"]) * tokens for mask in masks_of(key_places)]
    )
    codes, attend_places, dys, dy_rows = [], [], [], []
    for index in range(micro_count):
        length = lengths[0, index]
        valid = places < length
        code = slot_codes(routes[0, index], valid, capacity)
        code = jnp.concatenate([code, jnp.full((tokens, LANES - EXPERTS), -2.0, F32)], axis=1)
        codes.append(code)
        attend_places.append(
            jnp.concatenate([jnp.stack([start_row, length]), key_starts]).astype(jnp.int32)
        )
        dy = jnp.where(valid[:, None], cotangent[0, index], 0)
        dys.append(dy)
        dy_rows.append(jnp.concatenate([dy, code.astype(BF16)], axis=1))

    cut = (local + 1) // 2
    rows_here = jnp.stack(dy_rows)[None]
    first_piece = swap(other_packed, dp_places[0])
    last_piece = swap(mine_packed, dp_places[-1])
    dy_received = swap(rows_here, token_places[0][0])
    own_rows, dense, rows_here, first_piece, last_piece, dy_received = after(
        mine_packed, dense, rows_here, first_piece, last_piece, dy_received
    )
    between = swap(own_rows, dp_places[1])
    rows_here = jnp.concatenate([rows_here, dy_received], axis=0)
    dy_received = swap(rows_here, token_places[0][1])
    if len(token_places[0]) > 3:
        rows_here = jnp.concatenate([rows_here, dy_received], axis=0)
        dy_received = swap(rows_here, token_places[0][2])
    forward = swap(first_piece, dp_places[-1])

    gain_one = dense[:, dense.shape[1] - LANES].astype(F32)[None]
    gain_two = dense[:, width + EXPERTS].astype(F32)[None]
    x = layer_input[0]
    normed, queries, keys_values = project(x, gain_one, dense, cos, sin)
    key_rows, attended, log_totals, middles, normed_two, gates = [], [], [], [], [], []
    row_halves = []
    for index in range(micro_count):
        halves = gather_rows(keys_values[index], key_places)
        key_rows.append(jnp.concatenate(halves, axis=0).reshape(-1, 2 * key_width))

    rows, lse = attend(attend_places[0], queries[0], key_rows[0])
    attended.append(rows)
    log_totals.append(lse)
    rows, lse = attend(attend_places[1], queries[1], key_rows[1])
    attended.append(rows)
    log_totals.append(lse)
    stage_rows = []
    for index in range(micro_count):
        middle, normed_rows, gate = middle_rows(
            x[index], attended[index], dense, gain_two, codes[index]
        )
        middles.append(middle)
        normed_two.append(normed_rows)
        gates.append(gate)
        stage_rows.append([swap(normed_rows, place) for place in token_places[index][:-1]])
    flat = [row for rows in stage_rows for row in rows]
    between, forward, first_piece, dy_received, *flat = after(
        between, forward, first_piece, dy_received, *flat
    )
    rows_here = jnp.concatenate([rows_here, dy_received], axis=0)
    stage_rows = [flat[: len(flat) // 2], flat[len(flat) // 2 :]]
    firsts = [first_piece[:cut], first_piece[cut:]]
    onward = [swap(firsts[0], dp_places[1])]
    along = swap(between, dp_places[-1])
    rows_there = swap(rows_here, token_places[0][-1])

    dy_blocks = []
    per_micro = 2 * rows_here.shape[0]
    block_count = micro_count * per_micro
    for index in range(micro_count):
        order = [token_places[0].index(place) for place in token_places[index]]
        for piece in range(per_micro):
            source = sum((piece >> stage & 1) << order[stage] for stage in range(len(order)))
            side = rows_here if source < per_micro // 2 else rows_there
            dy_blocks.append(side[source % (per_micro // 2), index])
    dy_all = jnp.stack(dy_blocks)
    code_all = dy_all[:, :, width : width + EXPERTS].astype(F32).transpose(2, 0, 1)
    code_all = jnp.roll(code_all.reshape(EXPERTS, block_count * tokens), -first_expert, axis=0)
    rank_table = code_all[:8].astype(jnp.int32)

    for index in range(micro_count):
        pieces = [normed_two[index], *stage_rows[index]]
        pieces.append(swap(pieces[1], token_places[index][1]))
        pieces = jnp.stack(pieces)
        if index == 1:
            pieces, along, onward[0], firsts[1], dy_all, rank_table = after(
                pieces, along, onward[0], firsts[1], dy_all, rank_table
            )
            onward.append(swap(firsts[1], dp_places[1]))
            across = [swap(part, dp_places[-1]) for part in onward]
        row_halves += [pieces, swap(pieces, token_places[index][-1])]
    row_all = jnp.concatenate(row_halves, axis=0)

    def expert_pieces(expert):
        return [
            (parts[0], expert)
            if len(parts) == 1
            else (parts[expert >= cut], expert - cut * (expert >= cut))
            for parts in weight_parts
        ]

    router_t = jnp.roll(dense[:, width : width + EXPERTS].T, -first_expert, axis=0)
    logits = dot_cols(router_t, row_all.reshape(block_count * tokens, width))
    chosen = code_all > -1.5
    peak = jnp.max(jnp.where(chosen, logits, masked_score), axis=0, keepdims=True)
    raised = jnp.where(chosen, jnp.exp(jnp.where(chosen, logits, peak) - peak), 0.0)
    gate_table = (raised / jnp.sum(raised, axis=0, keepdims=True))[:8]
    me = jnp.stack([dp_index, first_expert]).astype(jnp.int32)
    held = None
    groups = [
        [index for index in range(dp_count) if index >> pair_bit & 1 == side] for side in range(2)
    ]
    summed = []
    me, *across = after(me, *across)
    weight_parts = [[mine_packed], [first_piece], [between], onward, [last_piece], [forward], [along], across]
    if len(dp_places) > 3:
        more = [[mine_packed], [first_piece], [between], onward]
        for place in dp_places[2:-1]:
            more = more + [[swap(part, place) for part in parts] for parts in more]
        weight_parts = more + [[swap(part, dp_places[-1]) for part in parts] for parts in more]

    for first, end in ((0, cut), (cut, local)):
        *held, grads = run_experts(
            first, me, [expert_pieces(expert) for expert in range(first, end)], weight_masks,
            pair_bit, row_all, dy_all, rank_table, gate_table, slots, local, held,
        )
        summed.append(
            lax.psum_scatter(
                grads, "dp", scatter_dimension=0, axis_index_groups=groups, tiled=True
            )[0]
        )
    eg_all, db_all = held

    slot_place = rank_table[:local]
    slot_place = jnp.where(
        slot_place >= 0, slot_place + slots * jnp.arange(local, dtype=jnp.int32)[:, None], -1
    )
    slot_place = jnp.concatenate(
        [slot_place, jnp.full((8 - local, block_count * tokens), -1, jnp.int32)], axis=0
    )
    slot_place = slot_place.reshape(8, block_count, tokens).transpose(1, 2, 0)

    def first_trade(source, places):
        found = []
        for index in range(micro_count):
            first, size = index * per_micro, per_micro // 2
            high = combine(source, places, first + size, size)
            received = swap(high, token_places[index][-1])
            low = combine(source, places, first, size)
            half_size = size // 2
            found.append(
                [
                    add_rounded(low[:half_size], received[:half_size]),
                    add_rounded(low[half_size:], received[half_size:]),
                ]
            )
        return found

    sums = first_trade(db_all, slot_place)
    received = [
        swap(sums[index][1], token_places[index][-2]) for index in range(micro_count)
    ]
    mix_place, *lows = after(slot_place, *[pair[0] for pair in sums])
    mixed = first_trade(eg_all, mix_place)
    flat, shape = jax.tree.flatten((received, mixed))
    received, mixed = jax.tree.unflatten(shape, lax.optimization_barrier(tuple(flat)))
    row_grads = []
    for index in range(micro_count):
        total = add_rounded(lows[index], received[index])
        row_grads.append(sum_home(total[:1], total[1:], token_places[index][:1])[0])

    router_grads, middle_grads, branch_grads, head_grads, gain_two_grads = [], [], [], [], []
    for index in range(micro_count):
        dz, dy1, branch, head_grad, gain_grad = middle_back(
            row_grads[index], middles[index], dys[index], gates[index], gain_two, dense
        )
        router_grads.append(dz)
        middle_grads.append(dy1)
        branch_grads.append(branch)
        head_grads.append(head_grad)
        gain_two_grads.append(gain_grad)

    def tall(parts):
        return jnp.concatenate(parts, axis=0)

    query_grads, pair_grads = [], []
    for index in range(micro_count):
        if index == micro_count - 1:
            attend_places[index], query_grads[0] = after(attend_places[index], query_grads[0])
        dq, pairs = attend_back(
            attend_places[index], queries[index], key_rows[index], head_grads[index],
            attended[index], log_totals[index], cos_t, sin_t,
        )
        pairs = pairs.reshape(owner_count, tokens, pairs.shape[1])
        middle_point = owner_count // 2
        pair_grads.append(sum_home(pairs[:middle_point], pairs[middle_point:], key_places)[0])
        query_grads.append(dq)
    branch_grads[0], query_grads[-1] = after(branch_grads[0], query_grads[-1])
    early = weight_grads(
        [tall(attended), tall(normed_two)],
        [tall(branch_grads), tall(router_grads)],
        sum(gain_two_grads),
        width + LANES,
    )
    along_z = [("dp", bit) for bit in reversed(range(1, dp_bits))]
    along_x = [("dp", 0)] if dp_bits else []
    home_two = Homeward(early, [("expert", 0)] + along_x + row_places + along_z)

    normed_all = normed.reshape(micro_count * tokens, width)

    pair_grads[0], summed[0], early = after(pair_grads[0], summed[0], early)
    other = [swap(summed[0][1], dp_places[0])]
    key_grads, input_grads, gain_one_grads = [], [], []
    for index in range(micro_count):
        dx, dkv, gain_grad = project_back(
            query_grads[index], pair_grads[index], x[index], middle_grads[index], gain_one,
            dense, cos, sin,
        )
        input_grads.append(dx)
        key_grads.append(dkv)
        gain_one_grads.append(gain_grad)
    gain_one_grad = home_two.pin(sum(gain_one_grads))
    late = weight_grads(
        [normed_all, normed_all],
        [tall(query_grads), tall(key_grads)],
        gain_one_grad,
        width + 2 * key_width + LANES,
    )
    home_one = Homeward(late, [("expert", 0)] + row_places + along_x + along_z)
    other.append(swap(summed[1][1], dp_places[0]))
    home_one.join()
    home_one.join()
    highs = after(home_one.held, *[pair[1] for pair in mixed])[1:]
    mix_received = [
        swap(highs[index], token_places[index][-2]) for index in range(micro_count)
    ]
    home_one.received, home_two.received, other[0], *mix_received = after(
        home_one.received, home_two.received, other[0], *mix_received
    )
    home_one.join()
    home_two.join()
    home_one.received, home_two.received, other[1] = after(
        home_one.received, home_two.received, other[1]
    )
    home_one.join()
    home_two.join()
    mixtures = []
    for index in range(micro_count):
        total = add_rounded(mixed[index][0], mix_received[index])
        mixtures.append(sum_home(total[:1], total[1:], token_places[index][:1])[0])
    layer_output = jnp.stack(
        [
            (middles[index] + mixtures[index].astype(F32)).astype(BF16)
            for index in range(micro_count)
        ]
    )[None]

    mine = jnp.concatenate([part[0] for part in summed], axis=0).astype(F32)
    other = jnp.concatenate(other, axis=0).astype(F32)
    if split == 2:
        lower = half == 0
        mine = jnp.concatenate(
            [jnp.where(lower, mine, other), jnp.where(lower, other, mine)], axis=0
        )
    else:
        mine = mine + other
    deep = w_gate.shape[1]
    inner = w_gate.shape[2]
    grad_gate = mine[:, :deep]
    grad_up = mine[:, deep : 2 * deep]
    shallow = w_down.shape[1]
    grad_down = jnp.concatenate(
        [
            mine[:, start : start + shallow]
            for start in range(2 * deep, mine.shape[1], shallow)
        ],
        axis=2,
    )
    late_grads = home_one.rows()
    output_grads = home_two.rows()
    return (
        layer_output,
        jnp.stack(input_grads)[None],
        late_grads[:, :width],
        late_grads[:, width : width + key_width],
        late_grads[:, width + key_width : width + 2 * key_width],
        output_grads[:, :width],
        output_grads[:, width : width + EXPERTS],
        late_grads[:, width + 2 * key_width + EXPERTS],
        output_grads[:, width + EXPERTS],
        grad_gate,
        grad_up,
        grad_down,
    )


def solution(mesh):
    return jax.shard_map(
        shards,
        mesh=mesh,
        in_specs=(
            P("dp", None, "expert", None),
            P("dp", None, "expert", None),
            P("dp", None),
            P("dp", None, "expert", None),
            P(),
            P(("dp", "expert"), None),
            P(("dp", "expert"), None),
            P(("dp", "expert"), None),
            P(("dp", "expert"), None),
            P(("dp", "expert"), None),
            P(("dp", "expert")),
            P(("dp", "expert")),
            P("expert", "dp", None),
            P("expert", "dp", None),
            P("expert", "dp", None),
        ),
        out_specs=(
            P("dp", None, "expert", None),
            P("dp", None, "expert", None),
            P(("dp", "expert"), None),
            P(("dp", "expert"), None),
            P(("dp", "expert"), None),
            P(("dp", "expert"), None),
            P(("dp", "expert"), None),
            P(("dp", "expert")),
            P(("dp", "expert")),
            P("expert", "dp", None),
            P("expert", "dp", None),
            P("expert", "dp", None),
        ),
        check_vma=False,
    )
```
